256 devices in a mesh: tile: 16 (over z, core), blk: 16 (over y, x).
Axes of the slice: x: 4, y: 4, z: 8, core: 2. Of those that a mesh axis runs over, the one named last changes fastest.
Arguments:
- spectra: float32 [4096, 3, 2, 2048], P(('tile', 'blk')), may hold values from -200 to 200
- send_rows: int32 [256, 16, 2], P(('tile', 'blk')), may hold values from 0 to 15
- send_counts: int32 [256, 16], P(('tile', 'blk')), may hold values from 1 to 2, as said below
- pair_rows: int32 [2, 65536], P(None, ('tile', 'blk')), may hold values from 0 to 511, as said below
- pair_counts: int32 [256], P(('tile', 'blk')), may hold values from 32 to 256, as said below
Outputs:
- stacks: bfloat16 [129, 9, 65536], P(None, None, ('tile', 'blk'))
The draws below stay inside these ranges and needn't reach their ends.
Inputs may be any that keep to these rules, and one draw needn't show every extreme that they name: `send_counts`: each entry counts the live slots of one list; some entry equals 2 in every draw. `pair_rows`: every entry of pair p, owned by device d = p // 256, is d2 * 2 + s with s < send_counts[d2, d mod 16], a live row of the panel of its owner's column. `pair_counts`: some device has all 256 pairs live in every draw.
All inputs are finite; a program needn't handle non-finite values.
Results may differ from the reference program's by a relative error of at most 0.0067.
Values may be sent and summed in bfloat16 or wider, within the bound.
A program may use at most 128 MiB of HBM per device.

```python
import math
import jax
import jax.numpy as jnp
from jax import lax

BINS = 2048
LAGS = 129
STA_DEV = 16
SLOT = 2
PAIRS_DEV = 256
NSTA = 4096
NPAIRS = 65536
N_BLK = 16
DEVICES = 256


def draw_spectra(key, part):
    shape_full = (NSTA, 3, 2, BINS)
    first_key, second_key = jax.random.split(key, 2)
    base_part = jnp.clip(jax.random.normal(first_key, shape_full, jnp.float32), -8.0, 8.0)
    element_scale = jnp.exp(jax.random.uniform(second_key, shape_full, jnp.float32, 0.0, math.log(10.0)))
    return base_part * element_scale


def counts_table(key):
    inner_key = jax.random.fold_in(key, 7)
    table_vals = jax.random.randint(inner_key, (DEVICES * N_BLK,), 1, SLOT + 1, dtype=jnp.int32)
    full_at = jax.random.randint(jax.random.fold_in(inner_key, 1), (), 0, DEVICES * N_BLK, dtype=jnp.int32)
    table_vals = table_vals.at[full_at].set(SLOT)
    return table_vals.reshape(DEVICES, N_BLK)


def draw_send_counts(key, part):
    return counts_table(key)


def draw_pair_rows(key, part):
    table_vals = counts_table(key)
    inner_key = jax.random.fold_in(key, 11)
    source = jax.random.randint(jax.random.fold_in(inner_key, 1), (2, NPAIRS), 0, DEVICES, dtype=jnp.int32)
    column = jnp.arange(NPAIRS, dtype=jnp.int32) // PAIRS_DEV % N_BLK
    limit = table_vals[source, column[None, :]]
    slot_pick = jax.random.randint(jax.random.fold_in(inner_key, 2), (2, NPAIRS), 0, 1048576, dtype=jnp.int32) % limit
    return source * SLOT + slot_pick


def draw_pair_counts(key, part):
    inner_key = jax.random.fold_in(key, 13)
    base_vals = jax.random.randint(inner_key, (DEVICES,), PAIRS_DEV // 8, PAIRS_DEV // 2 + 1, dtype=jnp.int32)
    heavy = jax.random.randint(jax.random.fold_in(inner_key, 1), (DEVICES,), 0, 16, dtype=jnp.int32) == 0
    base_vals = jnp.where(heavy, PAIRS_DEV, base_vals)
    full_at = jax.random.randint(jax.random.fold_in(inner_key, 2), (), 0, DEVICES, dtype=jnp.int32)
    return base_vals.at[full_at].set(PAIRS_DEV)


def place_ends(values, rng, least, largest):
    longest = values.shape.index(max(values.shape))
    spots = []
    for shift in (0, 1):
        where = [jax.random.randint(jax.random.fold_in(rng, axis), (), 0, length) for axis, length in enumerate(values.shape)]
        where[longest] = (where[longest] + shift) % values.shape[longest]
        spots.append(tuple(where))
    return values.at[spots[0]].set(least).at[spots[1]].set(largest)


def setup_inputs(seed: int = 0) -> dict:
    key_of = jax.random.split(jax.random.key(seed), 6)
    spectra = draw_spectra(jax.random.fold_in(key_of[5], 71), 0)
    send_rows = place_ends(jax.random.randint(key_of[1], (DEVICES, N_BLK, SLOT), 0, STA_DEV), jax.random.fold_in(key_of[1], 1), 0, STA_DEV - 1).astype(jnp.int32)
    send_counts = draw_send_counts(jax.random.fold_in(key_of[5], 71), 0)
    pair_rows = draw_pair_rows(jax.random.fold_in(key_of[5], 71), 0)
    pair_counts = draw_pair_counts(jax.random.fold_in(key_of[5], 71), 0)
    return {"spectra": spectra, "send_rows": send_rows, "send_counts": send_counts, "pair_rows": pair_rows, "pair_counts": pair_counts}


def whiten(spectra):
    station_count = spectra.shape[0]
    bin_count = spectra.shape[-1]
    ramp_bins = bin_count // 32
    bin_index = jnp.arange(bin_count, dtype=jnp.int32)
    edge_dist = jnp.minimum(bin_index, bin_count - 1 - bin_index).astype(jnp.float32) + 0.5
    ramp_vals = 0.5 - 0.5 * jnp.cos(jnp.pi * edge_dist / ramp_bins)
    taper = jnp.where(edge_dist < ramp_bins, ramp_vals, jnp.ones_like(ramp_vals))
    blocked = spectra.reshape(station_count, 3, 2, bin_count // 64, 64)
    power = lax.optimization_barrier(jnp.mean(blocked * blocked, axis=(1, 2, 4)))
    inverse = 1.0 / jnp.sqrt(power + 1e-05)
    spread_scale = jnp.repeat(inverse, 64, axis=1)
    return (spectra * taper * spread_scale[:, None, None, :]).astype(jnp.bfloat16)

def lag_table(lag_count, bin_count):
    lag_index = jnp.arange(lag_count, dtype=jnp.int32) - lag_count // 2
    bin_index = jnp.arange(bin_count, dtype=jnp.int32)
    phase_steps = lag_index[:, None] * bin_index[None, :] % (2 * bin_count)
    angle = phase_steps.astype(jnp.float32) * (jnp.pi / bin_count)
    return jnp.concatenate([jnp.cos(angle), -jnp.sin(angle)], axis=1).astype(jnp.bfloat16)

def cross_spectrum(first_rows, second_rows):
    pair_total = first_rows.shape[0]
    bin_count = first_rows.shape[-1]
    left_vals = first_rows.astype(jnp.float32)
    right_vals = second_rows.astype(jnp.float32)
    left_re = left_vals[:, :, None, 0, :]
    left_im = left_vals[:, :, None, 1, :]
    right_re = right_vals[:, None, :, 0, :]
    right_im = right_vals[:, None, :, 1, :]
    real_part = left_re * right_re + left_im * right_im
    imag_part = left_im * right_re - left_re * right_im
    merged = jnp.concatenate([real_part, imag_part], axis=-1)
    return merged.reshape(pair_total, 9, 2 * bin_count).astype(jnp.bfloat16)

def reference(spectra, send_rows, send_counts, pair_rows, pair_counts):
    whitened = whiten(spectra)
    lag_rows = lag_table(LAGS, BINS)
    block_rows = math.gcd(PAIRS_DEV, 512)
    block_total = NPAIRS // block_rows
    scale_factor = 1.0 / math.sqrt(BINS)

    def one_block(block_id):
        offset = block_id * block_rows
        pair_ids = offset + jnp.arange(block_rows, dtype=jnp.int32)
        owner_dev = pair_ids // PAIRS_DEV
        column = owner_dev % N_BLK

        def fetch(panel_rows):
            source = panel_rows // SLOT
            slot_id = panel_rows % SLOT
            station = source * STA_DEV + send_rows[source, column, slot_id]
            alive_slot = slot_id < send_counts[source, column]
            fetched = jnp.take(whitened, station, axis=0)
            return jnp.where(alive_slot[:, None, None, None], fetched, jnp.zeros_like(fetched))
        first_rows = fetch(lax.dynamic_slice_in_dim(pair_rows[0], offset, block_rows))
        second_rows = fetch(lax.dynamic_slice_in_dim(pair_rows[1], offset, block_rows))
        cross_spec = cross_spectrum(first_rows, second_rows)
        lag_sums = jnp.einsum('lf,pcf->lcp', lag_rows.astype(jnp.float32), cross_spec.astype(jnp.float32)) * scale_factor
        alive_pairs = pair_ids % PAIRS_DEV < pair_counts[owner_dev]
        return jnp.where(alive_pairs[None, None, :], lag_sums, 0.0).astype(jnp.bfloat16)
    stacked = lax.map(one_block, jnp.arange(block_total, dtype=jnp.int32))
    return stacked.transpose(1, 2, 0, 3).reshape(LAGS, 9, NPAIRS)
```

```python
import functools
import math

import jax
import jax.numpy as jnp
from jax import lax
from jax.experimental import pallas as pl
from jax.experimental.pallas import tpu as pltpu
from jax.sharding import Mesh
from jax.sharding import PartitionSpec as P

LAGS = 129
LAG_ROWS = 144
PAIR_BLOCK = 128
BIN_CHUNK = 256
GATHER_CHUNK = 512


def whiten(spectra):
    station_count = spectra.shape[0]
    bin_count = spectra.shape[-1]
    ramp_bins = bin_count // 32
    bin_index = jnp.arange(bin_count, dtype=jnp.int32)
    edge_dist = jnp.minimum(bin_index, bin_count - 1 - bin_index).astype(jnp.float32) + 0.5
    ramp_vals = 0.5 - 0.5 * jnp.cos(jnp.pi * edge_dist / ramp_bins)
    taper = jnp.where(edge_dist < ramp_bins, ramp_vals, jnp.ones_like(ramp_vals))
    blocked = spectra.reshape(station_count, 3, 2, bin_count // 64, 64)
    power = jnp.mean(blocked * blocked, axis=(1, 2, 4))
    inverse = 1.0 / jnp.sqrt(power + 1e-05)
    spread_scale = jnp.repeat(inverse, 64, axis=1)
    return (spectra * taper * spread_scale[:, None, None, :]).astype(jnp.bfloat16)


def lag_part(bin_count, first_bin, part_bins):
    lag_index = jnp.arange(LAGS, dtype=jnp.int32) - LAGS // 2
    bin_index = first_bin + jnp.arange(part_bins, dtype=jnp.int32)
    phase_steps = lag_index[:, None] * bin_index[None, :] % (2 * bin_count)
    angle = phase_steps.astype(jnp.float32) * (jnp.pi / bin_count)
    pad = ((0, LAG_ROWS - LAGS), (0, 0))
    cos_rows = jnp.pad(jnp.cos(angle).astype(jnp.bfloat16), pad)
    sin_rows = jnp.pad((-jnp.sin(angle)).astype(jnp.bfloat16), pad)
    return cos_rows, sin_rows


def pair_kernel(counts_ref, first_ref, second_ref, panel_ref, cos_ref, sin_ref, out_ref,
                f_scr, s_scr, *, blocks_per_owner, part_bins):
    step = pl.program_id(0)
    owner = step // blocks_per_owner
    start = (step % blocks_per_owner) * PAIR_BLOCK
    live = start < counts_ref[owner]

    @pl.when(jnp.logical_not(live))
    def _():
        out_ref[...] = jnp.zeros_like(out_ref)

    @pl.when(live)
    def _():
        rows = panel_ref.shape[0]
        width = panel_ref.shape[1]
        iota = lax.broadcasted_iota(jnp.int32, (PAIR_BLOCK, rows), 1)
        pick_first = (first_ref[...] == iota).astype(jnp.bfloat16)
        pick_second = (second_ref[...] == iota).astype(jnp.bfloat16)

        def gather(c, carry):
            off = pl.multiple_of(c * GATHER_CHUNK, GATHER_CHUNK)
            block = panel_ref[:, pl.ds(off, GATHER_CHUNK)]
            f_scr[:, pl.ds(off, GATHER_CHUNK)] = jnp.dot(
                pick_first, block, preferred_element_type=jnp.float32)
            s_scr[:, pl.ds(off, GATHER_CHUNK)] = jnp.dot(
                pick_second, block, preferred_element_type=jnp.float32)
            return carry

        lax.fori_loop(0, width // GATHER_CHUNK, gather, 0)
        out_ref[...] = jnp.zeros_like(out_ref)
        nt = (((1,), (1,)), ((), ()))

        def chunk(kc, carry):
            off = pl.multiple_of(kc * BIN_CHUNK, BIN_CHUNK)
            cos_blk = cos_ref[:, pl.ds(off, BIN_CHUNK)]
            sin_blk = sin_ref[:, pl.ds(off, BIN_CHUNK)]
            for a in range(3):
                f_re = f_scr[:, pl.ds(2 * a * part_bins + off, BIN_CHUNK)]
                f_im = f_scr[:, pl.ds((2 * a + 1) * part_bins + off, BIN_CHUNK)]
                for b in range(3):
                    s_re = s_scr[:, pl.ds(2 * b * part_bins + off, BIN_CHUNK)]
                    s_im = s_scr[:, pl.ds((2 * b + 1) * part_bins + off, BIN_CHUNK)]
                    real_part = (f_re * s_re + f_im * s_im).astype(jnp.bfloat16)
                    imag_part = (f_im * s_re - f_re * s_im).astype(jnp.bfloat16)
                    acc = lax.dot_general(cos_blk, real_part, nt,
                                          preferred_element_type=jnp.float32)
                    acc = acc + lax.dot_general(sin_blk, imag_part, nt,
                                                preferred_element_type=jnp.float32)
                    out_ref[0, 3 * a + b] += acc
            return carry

        lax.fori_loop(0, part_bins // BIN_CHUNK, chunk, 0)


def pair_sums(counts, first_idx, second_idx, panel, cos_rows, sin_rows, owners):
    rows, width = panel.shape
    part_bins = width // 6
    pairs = first_idx.shape[0]
    per_owner = pairs // owners
    blocks_per_owner = per_owner // PAIR_BLOCK
    grid = (pairs // PAIR_BLOCK,)
    kernel = functools.partial(pair_kernel, blocks_per_owner=blocks_per_owner,
                               part_bins=part_bins)
    flops = 2 * pairs * rows * width * 2 + 2 * LAG_ROWS * 2 * part_bins * 9 * pairs
    cost = pl.CostEstimate(flops=flops, transcendentals=0,
                           bytes_accessed=rows * width * 2 + owners * 9 * LAG_ROWS * per_owner * 4)
    return pl.pallas_call(
        kernel,
        out_shape=jax.ShapeDtypeStruct((owners, 9, LAG_ROWS, per_owner), jnp.float32),
        grid_spec=pltpu.PrefetchScalarGridSpec(
            num_scalar_prefetch=1,
            grid=grid,
            in_specs=[
                pl.BlockSpec((PAIR_BLOCK, 1), lambda i, c: (i, 0)),
                pl.BlockSpec((PAIR_BLOCK, 1), lambda i, c: (i, 0)),
                pl.BlockSpec((rows, width), lambda i, c: (0, 0)),
                pl.BlockSpec((LAG_ROWS, part_bins), lambda i, c: (0, 0)),
                pl.BlockSpec((LAG_ROWS, part_bins), lambda i, c: (0, 0)),
            ],
            out_specs=pl.BlockSpec(
                (1, 9, LAG_ROWS, PAIR_BLOCK),
                lambda i, c: (i // blocks_per_owner, 0, 0, i % blocks_per_owner)),
            scratch_shapes=[
                pltpu.VMEM((PAIR_BLOCK, width), jnp.float32),
                pltpu.VMEM((PAIR_BLOCK, width), jnp.float32),
            ],
        ),
        compiler_params=pltpu.CompilerParams(
            dimension_semantics=("arbitrary",), vmem_limit_bytes=60 * 1024 * 1024),
        cost_estimate=cost,
    )(counts, first_idx, second_idx, panel, cos_rows, sin_rows)


def shards(spectra, send_rows, send_counts, pair_rows, pair_counts):
    whitened = whiten(spectra)
    station_count, comps, parts, bin_count = whitened.shape
    row_width = comps * parts * bin_count
    slot_count = send_rows.shape[2]
    cores = lax.axis_size("core")
    part_bins = bin_count // cores
    core = lax.axis_index("core")

    flat = whitened.reshape(station_count, row_width)
    lists = send_rows[0]
    col_count = lists.shape[0]
    picked = jnp.take(flat, lists.reshape(-1), axis=0).reshape(col_count, slot_count, row_width)
    alive = jnp.arange(slot_count, dtype=jnp.int32)[None, :] < send_counts[0][:, None]
    picked = jnp.where(alive[:, :, None], picked, jnp.zeros_like(picked))
    received = lax.all_to_all(picked, "blk", 0, 0, tiled=True)

    halves = received.reshape(col_count, slot_count, comps * parts, cores, part_bins)
    halves = jnp.transpose(halves, (3, 0, 1, 2, 4)).reshape(
        cores, col_count * slot_count, comps * parts * part_bins)
    mine = lax.all_to_all(halves, "core", 0, 0, tiled=True)
    mine = mine.reshape(cores * col_count * slot_count, comps * parts * part_bins)
    panel = lax.all_gather(mine, "z", axis=0, tiled=True)

    chip_pairs = lax.all_gather(pair_rows, "core", axis=1, tiled=True)
    chip_counts = lax.all_gather(pair_counts, "core", axis=0, tiled=True)
    cos_rows, sin_rows = lag_part(bin_count, core * part_bins, part_bins)
    partial = pair_sums(chip_counts, chip_pairs[0][:, None], chip_pairs[1][:, None],
                        panel, cos_rows, sin_rows, cores)
    partial = lax.all_to_all(partial, "core", 0, 0, tiled=True)
    total = jnp.sum(partial, axis=0)[:, :LAGS, :] * (1.0 / math.sqrt(bin_count))
    pair_total = pair_rows.shape[1]
    live = jnp.arange(pair_total, dtype=jnp.int32) < pair_counts[0]
    total = jnp.where(live[None, None, :], total, 0.0).astype(jnp.bfloat16)
    return jnp.transpose(total, (1, 0, 2))


def solution(mesh):
    tile_size = mesh.shape["tile"]
    blk_size = mesh.shape["blk"]
    split = Mesh(mesh.devices.reshape(tile_size // 2, 2, blk_size), ("z", "core", "blk"))
    dev = ("z", "core", "blk")
    return jax.shard_map(
        shards,
        mesh=split,
        in_specs=(
            P(dev, None, None, None),
            P(dev, None, None),
            P(dev, None),
            P(None, dev),
            P(dev),
        ),
        out_specs=P(None, None, dev),
        check_vma=False,
    )
```

```python
import functools
import math

import jax
import jax.numpy as jnp
from jax import lax
from jax.experimental import pallas as pl
from jax.experimental.pallas import tpu as pltpu
from jax.sharding import Mesh
from jax.sharding import PartitionSpec as P

LAGS = 129
LAG_ROWS = 144
PAIR_BLOCK = 128
BIN_CHUNK = 256
GATHER_CHUNK = 512
CHUNKS = 4


def whiten(spectra):
    station_count = spectra.shape[0]
    bin_count = spectra.shape[-1]
    ramp_bins = bin_count // 32
    bin_index = jnp.arange(bin_count, dtype=jnp.int32)
    edge_dist = jnp.minimum(bin_index, bin_count - 1 - bin_index).astype(jnp.float32) + 0.5
    ramp_vals = 0.5 - 0.5 * jnp.cos(jnp.pi * edge_dist / ramp_bins)
    taper = jnp.where(edge_dist < ramp_bins, ramp_vals, jnp.ones_like(ramp_vals))
    blocked = spectra.reshape(station_count, 3, 2, bin_count // 64, 64)
    power = jnp.mean(blocked * blocked, axis=(1, 2, 4))
    inverse = 1.0 / jnp.sqrt(power + 1e-05)
    spread_scale = jnp.repeat(inverse, 64, axis=1)
    return (spectra * taper * spread_scale[:, None, None, :]).astype(jnp.bfloat16)


def lag_part(bin_count, first_bin, part_bins):
    lag_index = jnp.arange(LAGS, dtype=jnp.int32) - LAGS // 2
    bin_index = first_bin + jnp.arange(part_bins, dtype=jnp.int32)
    phase_steps = lag_index[:, None] * bin_index[None, :] % (2 * bin_count)
    angle = phase_steps.astype(jnp.float32) * (jnp.pi / bin_count)
    pad = ((0, LAG_ROWS - LAGS), (0, 0))
    cos_rows = jnp.pad(jnp.cos(angle).astype(jnp.bfloat16), pad)
    sin_rows = jnp.pad((-jnp.sin(angle)).astype(jnp.bfloat16), pad)
    return cos_rows, sin_rows


def pair_kernel(counts_ref, first_ref, second_ref, panel_ref, cos_ref, sin_ref, *rest,
                blocks_per_owner, part_bins, accumulate):
    if accumulate:
        acc_ref, out_ref, f_scr, s_scr = rest
    else:
        out_ref, f_scr, s_scr = rest
    step = pl.program_id(0)
    owner = step // blocks_per_owner
    start = (step % blocks_per_owner) * PAIR_BLOCK
    live = start < counts_ref[owner]
    if accumulate:
        out_ref[...] = acc_ref[...]
    else:
        out_ref[...] = jnp.zeros_like(out_ref)

    @pl.when(live)
    def _():
        rows = panel_ref.shape[0]
        width = panel_ref.shape[1]
        iota = lax.broadcasted_iota(jnp.int32, (PAIR_BLOCK, rows), 1)
        pick_first = (first_ref[...] == iota).astype(jnp.bfloat16)
        pick_second = (second_ref[...] == iota).astype(jnp.bfloat16)
        gather_chunk = min(GATHER_CHUNK, width)

        def gather(c, carry):
            off = pl.multiple_of(c * gather_chunk, gather_chunk)
            block = panel_ref[:, pl.ds(off, gather_chunk)]
            f_scr[:, pl.ds(off, gather_chunk)] = jnp.dot(
                pick_first, block, preferred_element_type=jnp.float32)
            s_scr[:, pl.ds(off, gather_chunk)] = jnp.dot(
                pick_second, block, preferred_element_type=jnp.float32)
            return carry

        lax.fori_loop(0, width // gather_chunk, gather, 0)
        nt = (((1,), (1,)), ((), ()))
        bin_chunk = min(BIN_CHUNK, part_bins)

        def chunk(kc, carry):
            off = pl.multiple_of(kc * bin_chunk, bin_chunk)
            cos_blk = cos_ref[:, pl.ds(off, bin_chunk)]
            sin_blk = sin_ref[:, pl.ds(off, bin_chunk)]
            for a in range(3):
                f_re = f_scr[:, pl.ds(2 * a * part_bins + off, bin_chunk)]
                f_im = f_scr[:, pl.ds((2 * a + 1) * part_bins + off, bin_chunk)]
                for b in range(3):
                    s_re = s_scr[:, pl.ds(2 * b * part_bins + off, bin_chunk)]
                    s_im = s_scr[:, pl.ds((2 * b + 1) * part_bins + off, bin_chunk)]
                    real_part = (f_re * s_re + f_im * s_im).astype(jnp.bfloat16)
                    imag_part = (f_im * s_re - f_re * s_im).astype(jnp.bfloat16)
                    acc = lax.dot_general(cos_blk, real_part, nt,
                                          preferred_element_type=jnp.float32)
                    acc = acc + lax.dot_general(sin_blk, imag_part, nt,
                                                preferred_element_type=jnp.float32)
                    out_ref[0, 3 * a + b] += acc
            return carry

        lax.fori_loop(0, part_bins // bin_chunk, chunk, 0)


def pair_sums(counts, first_idx, second_idx, panel, cos_rows, sin_rows, owners, chunk_id, acc):
    rows, width = panel.shape
    part_bins = width // 6
    pairs = first_idx.shape[0]
    per_owner = pairs // owners
    blocks_per_owner = per_owner // PAIR_BLOCK
    grid = (pairs // PAIR_BLOCK,)
    accumulate = acc is not None
    kernel = functools.partial(pair_kernel, blocks_per_owner=blocks_per_owner,
                               part_bins=part_bins, accumulate=accumulate)
    flops = 2 * pairs * rows * width * 2 + 2 * LAG_ROWS * 2 * part_bins * 9 * pairs
    out_bytes = owners * 9 * LAG_ROWS * per_owner * 4
    cost = pl.CostEstimate(flops=flops, transcendentals=0,
                           bytes_accessed=rows * width * 2 + out_bytes * (2 if accumulate else 1))
    out_spec = pl.BlockSpec(
        (1, 9, LAG_ROWS, PAIR_BLOCK),
        lambda i, c: (i // blocks_per_owner, 0, 0, i % blocks_per_owner))
    in_specs = [
        pl.BlockSpec((PAIR_BLOCK, 1), lambda i, c: (i, 0)),
        pl.BlockSpec((PAIR_BLOCK, 1), lambda i, c: (i, 0)),
        pl.BlockSpec((rows, width), lambda i, c: (0, 0)),
        pl.BlockSpec((LAG_ROWS, part_bins), lambda i, c: (0, chunk_id)),
        pl.BlockSpec((LAG_ROWS, part_bins), lambda i, c: (0, chunk_id)),
    ]
    args = [counts, first_idx, second_idx, panel, cos_rows, sin_rows]
    aliases = {}
    if accumulate:
        in_specs.append(out_spec)
        args.append(acc)
        aliases = {len(args) - 1: 0}
    return pl.pallas_call(
        kernel,
        out_shape=jax.ShapeDtypeStruct((owners, 9, LAG_ROWS, per_owner), jnp.float32),
        grid_spec=pltpu.PrefetchScalarGridSpec(
            num_scalar_prefetch=1,
            grid=grid,
            in_specs=in_specs,
            out_specs=out_spec,
            scratch_shapes=[
                pltpu.VMEM((PAIR_BLOCK, width), jnp.float32),
                pltpu.VMEM((PAIR_BLOCK, width), jnp.float32),
            ],
        ),
        input_output_aliases=aliases,
        compiler_params=pltpu.CompilerParams(
            dimension_semantics=("arbitrary",), vmem_limit_bytes=60 * 1024 * 1024),
        cost_estimate=cost,
    )(*args)


def shards(spectra, send_rows, send_counts, pair_rows, pair_counts):
    whitened = whiten(spectra)
    station_count, comps, parts, bin_count = whitened.shape
    row_width = comps * parts * bin_count
    slot_count = send_rows.shape[2]
    cores = lax.axis_size("core")
    part_bins = bin_count // cores
    core = lax.axis_index("core")

    flat = whitened.reshape(station_count, row_width)
    lists = send_rows[0]
    col_count = lists.shape[0]
    picked = jnp.take(flat, lists.reshape(-1), axis=0).reshape(col_count, slot_count, row_width)
    alive = jnp.arange(slot_count, dtype=jnp.int32)[None, :] < send_counts[0][:, None]
    picked = jnp.where(alive[:, :, None], picked, jnp.zeros_like(picked))
    received = lax.all_to_all(picked, "blk", 0, 0, tiled=True)

    chip_pairs = lax.all_gather(pair_rows, "core", axis=1, tiled=True)
    chip_counts = lax.all_gather(pair_counts, "core", axis=0, tiled=True)
    cos_rows, sin_rows = lag_part(bin_count, core * part_bins, part_bins)
    chunk_bins = part_bins // CHUNKS
    pieces = received.reshape(col_count, slot_count, comps * parts, cores, CHUNKS, chunk_bins)
    partial = None
    for chunk_id in range(CHUNKS):
        piece = jnp.transpose(pieces[:, :, :, :, chunk_id, :], (3, 0, 1, 2, 4)).reshape(
            cores, col_count * slot_count, comps * parts * chunk_bins)
        mine = lax.all_to_all(piece, "core", 0, 0, tiled=True)
        mine = mine.reshape(cores * col_count * slot_count, comps * parts * chunk_bins)
        panel = lax.all_gather(mine, "z", axis=0, tiled=True)
        partial = pair_sums(chip_counts, chip_pairs[0][:, None], chip_pairs[1][:, None],
                            panel, cos_rows, sin_rows, cores, chunk_id, partial)
    partial = lax.all_to_all(partial, "core", 0, 0, tiled=True)
    total = jnp.sum(partial, axis=0)[:, :LAGS, :] * (1.0 / math.sqrt(bin_count))
    pair_total = pair_rows.shape[1]
    live = jnp.arange(pair_total, dtype=jnp.int32) < pair_counts[0]
    total = jnp.where(live[None, None, :], total, 0.0).astype(jnp.bfloat16)
    return jnp.transpose(total, (1, 0, 2))


def solution(mesh):
    tile_size = mesh.shape["tile"]
    blk_size = mesh.shape["blk"]
    split = Mesh(mesh.devices.reshape(tile_size // 2, 2, blk_size), ("z", "core", "blk"))
    dev = ("z", "core", "blk")
    return jax.shard_map(
        shards,
        mesh=split,
        in_specs=(
            P(dev, None, None, None),
            P(dev, None, None),
            P(dev, None),
            P(None, dev),
            P(dev),
        ),
        out_specs=P(None, None, dev),
        check_vma=False,
    )
```

```python
import functools
import math

import jax
import jax.numpy as jnp
from jax import lax
from jax.experimental import pallas as pl
from jax.experimental.pallas import tpu as pltpu
from jax.sharding import Mesh
from jax.sharding import PartitionSpec as P

LAGS = 129
LAG_ROWS = 144
PAIR_BLOCK = 128
BIN_CHUNK = 256
GATHER_CHUNK = 512


def whiten(spectra):
    station_count = spectra.shape[0]
    bin_count = spectra.shape[-1]
    ramp_bins = bin_count // 32
    bin_index = jnp.arange(bin_count, dtype=jnp.int32)
    edge_dist = jnp.minimum(bin_index, bin_count - 1 - bin_index).astype(jnp.float32) + 0.5
    ramp_vals = 0.5 - 0.5 * jnp.cos(jnp.pi * edge_dist / ramp_bins)
    taper = jnp.where(edge_dist < ramp_bins, ramp_vals, jnp.ones_like(ramp_vals))
    blocked = spectra.reshape(station_count, 3, 2, bin_count // 64, 64)
    power = jnp.mean(blocked * blocked, axis=(1, 2, 4))
    inverse = 1.0 / jnp.sqrt(power + 1e-05)
    spread_scale = jnp.repeat(inverse, 64, axis=1)
    return (spectra * taper * spread_scale[:, None, None, :]).astype(jnp.bfloat16)


def lag_part(bin_count, first_bin, part_bins):
    lag_index = jnp.arange(LAGS, dtype=jnp.int32) - LAGS // 2
    bin_index = first_bin + jnp.arange(part_bins, dtype=jnp.int32)
    phase_steps = lag_index[:, None] * bin_index[None, :] % (2 * bin_count)
    angle = phase_steps.astype(jnp.float32) * (jnp.pi / bin_count)
    pad = ((0, LAG_ROWS - LAGS), (0, 0))
    cos_rows = jnp.pad(jnp.cos(angle).astype(jnp.bfloat16), pad)
    sin_rows = jnp.pad((-jnp.sin(angle)).astype(jnp.bfloat16), pad)
    return cos_rows, sin_rows


def pair_kernel(counts_ref, first_ref, second_ref, panel_ref, cos_ref, sin_ref, *rest,
                blocks_per_owner, part_bins, accumulate):
    if accumulate:
        acc_ref, out_ref, f_scr, s_scr = rest
    else:
        out_ref, f_scr, s_scr = rest
    step = pl.program_id(0)
    owner = step // blocks_per_owner
    start = (step % blocks_per_owner) * PAIR_BLOCK
    live = start < counts_ref[owner]
    if accumulate:
        out_ref[...] = acc_ref[...]
    else:
        out_ref[...] = jnp.zeros_like(out_ref)

    @pl.when(live)
    def _():
        rows = panel_ref.shape[0]
        width = panel_ref.shape[1]
        iota = lax.broadcasted_iota(jnp.int32, (PAIR_BLOCK, rows), 1)
        pick_first = (first_ref[...] == iota).astype(jnp.bfloat16)
        pick_second = (second_ref[...] == iota).astype(jnp.bfloat16)
        gather_chunk = min(GATHER_CHUNK, width)

        def gather(c, carry):
            off = pl.multiple_of(c * gather_chunk, gather_chunk)
            block = panel_ref[:, pl.ds(off, gather_chunk)]
            f_scr[:, pl.ds(off, gather_chunk)] = jnp.dot(
                pick_first, block, preferred_element_type=jnp.float32)
            s_scr[:, pl.ds(off, gather_chunk)] = jnp.dot(
                pick_second, block, preferred_element_type=jnp.float32)
            return carry

        lax.fori_loop(0, width // gather_chunk, gather, 0)
        nt = (((1,), (1,)), ((), ()))
        bin_chunk = min(BIN_CHUNK, part_bins)

        def chunk(kc, carry):
            off = pl.multiple_of(kc * bin_chunk, bin_chunk)
            cos_blk = cos_ref[:, pl.ds(off, bin_chunk)]
            sin_blk = sin_ref[:, pl.ds(off, bin_chunk)]
            for a in range(3):
                f_re = f_scr[:, pl.ds(2 * a * part_bins + off, bin_chunk)]
                f_im = f_scr[:, pl.ds((2 * a + 1) * part_bins + off, bin_chunk)]
                for b in range(3):
                    s_re = s_scr[:, pl.ds(2 * b * part_bins + off, bin_chunk)]
                    s_im = s_scr[:, pl.ds((2 * b + 1) * part_bins + off, bin_chunk)]
                    real_part = (f_re * s_re + f_im * s_im).astype(jnp.bfloat16)
                    imag_part = (f_im * s_re - f_re * s_im).astype(jnp.bfloat16)
                    acc = lax.dot_general(cos_blk, real_part, nt,
                                          preferred_element_type=jnp.float32)
                    acc = acc + lax.dot_general(sin_blk, imag_part, nt,
                                                preferred_element_type=jnp.float32)
                    out_ref[0, 3 * a + b] += acc
            return carry

        lax.fori_loop(0, part_bins // bin_chunk, chunk, 0)


def pair_sums(counts, first_idx, second_idx, panel, cos_rows, sin_rows, owners, chunk_id, acc):
    rows, width = panel.shape
    part_bins = width // 6
    pairs = first_idx.shape[0]
    per_owner = pairs // owners
    blocks_per_owner = per_owner // PAIR_BLOCK
    grid = (pairs // PAIR_BLOCK,)
    accumulate = acc is not None
    kernel = functools.partial(pair_kernel, blocks_per_owner=blocks_per_owner,
                               part_bins=part_bins, accumulate=accumulate)
    flops = 2 * pairs * rows * width * 2 + 2 * LAG_ROWS * 2 * part_bins * 9 * pairs
    out_bytes = owners * 9 * LAG_ROWS * per_owner * 4
    cost = pl.CostEstimate(flops=flops, transcendentals=0,
                           bytes_accessed=rows * width * 2 + out_bytes * (2 if accumulate else 1))
    out_spec = pl.BlockSpec(
        (1, 9, LAG_ROWS, PAIR_BLOCK),
        lambda i, c: (i // blocks_per_owner, 0, 0, i % blocks_per_owner))
    in_specs = [
        pl.BlockSpec((PAIR_BLOCK, 1), lambda i, c: (i, 0)),
        pl.BlockSpec((PAIR_BLOCK, 1), lambda i, c: (i, 0)),
        pl.BlockSpec((rows, width), lambda i, c: (0, 0)),
        pl.BlockSpec((LAG_ROWS, part_bins), lambda i, c: (0, chunk_id)),
        pl.BlockSpec((LAG_ROWS, part_bins), lambda i, c: (0, chunk_id)),
    ]
    args = [counts, first_idx, second_idx, panel, cos_rows, sin_rows]
    aliases = {}
    if accumulate:
        in_specs.append(out_spec)
        args.append(acc)
        aliases = {len(args) - 1: 0}
    return pl.pallas_call(
        kernel,
        out_shape=jax.ShapeDtypeStruct((owners, 9, LAG_ROWS, per_owner), jnp.float32),
        grid_spec=pltpu.PrefetchScalarGridSpec(
            num_scalar_prefetch=1,
            grid=grid,
            in_specs=in_specs,
            out_specs=out_spec,
            scratch_shapes=[
                pltpu.VMEM((PAIR_BLOCK, width), jnp.float32),
                pltpu.VMEM((PAIR_BLOCK, width), jnp.float32),
            ],
        ),
        input_output_aliases=aliases,
        compiler_params=pltpu.CompilerParams(
            dimension_semantics=("arbitrary",), vmem_limit_bytes=60 * 1024 * 1024),
        cost_estimate=cost,
    )(*args)


def shards(spectra, send_rows, send_counts, pair_rows, pair_counts):
    whitened = whiten(spectra)
    station_count, comps, parts, bin_count = whitened.shape
    row_width = comps * parts * bin_count
    slot_count = send_rows.shape[2]
    cores = lax.axis_size("core")
    part_bins = bin_count // cores
    core = lax.axis_index("core")

    flat = whitened.reshape(station_count, row_width)
    lists = send_rows[0]
    col_count = lists.shape[0]
    picked = jnp.take(flat, lists.reshape(-1), axis=0).reshape(col_count, slot_count, row_width)
    alive = jnp.arange(slot_count, dtype=jnp.int32)[None, :] < send_counts[0][:, None]
    picked = jnp.where(alive[:, :, None], picked, jnp.zeros_like(picked))
    pieces = picked.reshape(col_count, slot_count, comps * parts, cores, part_bins)
    pieces = jnp.transpose(pieces, (3, 0, 1, 2, 4)).reshape(
        cores * col_count, slot_count, comps * parts * part_bins)
    mine = lax.all_to_all(pieces, ("core", "blk"), 0, 0, tiled=True)
    mine = mine.reshape(cores * col_count * slot_count, comps * parts * part_bins)
    panel = lax.all_gather(mine, "z", axis=0, tiled=True)

    chip_pairs = lax.all_gather(pair_rows, "core", axis=1, tiled=True)
    chip_counts = lax.all_gather(pair_counts, "core", axis=0, tiled=True)
    cos_rows, sin_rows = lag_part(bin_count, core * part_bins, part_bins)
    partial = pair_sums(chip_counts, chip_pairs[0][:, None], chip_pairs[1][:, None],
                        panel, cos_rows, sin_rows, cores, 0, None)
    partial = lax.all_to_all(partial, "core", 0, 0, tiled=True)
    total = jnp.sum(partial, axis=0)[:, :LAGS, :] * (1.0 / math.sqrt(bin_count))
    pair_total = pair_rows.shape[1]
    live = jnp.arange(pair_total, dtype=jnp.int32) < pair_counts[0]
    total = jnp.where(live[None, None, :], total, 0.0).astype(jnp.bfloat16)
    return jnp.transpose(total, (1, 0, 2))


def solution(mesh):
    tile_size = mesh.shape["tile"]
    blk_size = mesh.shape["blk"]
    split = Mesh(mesh.devices.reshape(tile_size // 2, 2, blk_size), ("z", "core", "blk"))
    dev = ("z", "core", "blk")
    return jax.shard_map(
        shards,
        mesh=split,
        in_specs=(
            P(dev, None, None, None),
            P(dev, None, None),
            P(dev, None),
            P(None, dev),
            P(dev),
        ),
        out_specs=P(None, None, dev),
        check_vma=False,
    )
```

```python
import functools
import math

import jax
import jax.numpy as jnp
from jax import lax
from jax.experimental import pallas as pl
from jax.experimental.pallas import tpu as pltpu
from jax.sharding import Mesh
from jax.sharding import PartitionSpec as P

LAGS = 129
LAG_ROWS = 144
PAIR_BLOCK = 128
BIN_CHUNK = 256
GATHER_CHUNK = 512


def whiten(spectra):
    station_count = spectra.shape[0]
    bin_count = spectra.shape[-1]
    ramp_bins = bin_count // 32
    bin_index = jnp.arange(bin_count, dtype=jnp.int32)
    edge_dist = jnp.minimum(bin_index, bin_count - 1 - bin_index).astype(jnp.float32) + 0.5
    ramp_vals = 0.5 - 0.5 * jnp.cos(jnp.pi * edge_dist / ramp_bins)
    taper = jnp.where(edge_dist < ramp_bins, ramp_vals, jnp.ones_like(ramp_vals))
    blocked = spectra.reshape(station_count, 3, 2, bin_count // 64, 64)
    power = jnp.mean(blocked * blocked, axis=(1, 2, 4))
    inverse = 1.0 / jnp.sqrt(power + 1e-05)
    spread_scale = jnp.repeat(inverse, 64, axis=1)
    return (spectra * taper * spread_scale[:, None, None, :]).astype(jnp.bfloat16)


def lag_part(bin_count, first_bin, part_bins):
    lag_index = jnp.arange(LAGS, dtype=jnp.int32) - LAGS // 2
    bin_index = first_bin + jnp.arange(part_bins, dtype=jnp.int32)
    phase_steps = lag_index[:, None] * bin_index[None, :] % (2 * bin_count)
    angle = phase_steps.astype(jnp.float32) * (jnp.pi / bin_count)
    pad = ((0, LAG_ROWS - LAGS), (0, 0))
    cos_rows = jnp.pad(jnp.cos(angle).astype(jnp.bfloat16), pad)
    sin_rows = jnp.pad((-jnp.sin(angle)).astype(jnp.bfloat16), pad)
    return cos_rows, sin_rows


def pair_kernel(counts_ref, first_ref, second_ref, panel_ref, cos_ref, sin_ref, *rest,
                blocks_per_owner, part_bins, accumulate):
    if accumulate:
        acc_ref, out_ref, f_scr, s_scr = rest
    else:
        out_ref, f_scr, s_scr = rest
    step = pl.program_id(0)
    owner = step // blocks_per_owner
    start = (step % blocks_per_owner) * PAIR_BLOCK
    live = start < counts_ref[owner]
    if accumulate:
        out_ref[...] = acc_ref[...]
    else:
        out_ref[...] = jnp.zeros_like(out_ref)

    @pl.when(live)
    def _():
        rows = panel_ref.shape[0]
        width = panel_ref.shape[1]
        iota = lax.broadcasted_iota(jnp.int32, (PAIR_BLOCK, rows), 1)
        pick_first = (first_ref[...] == iota).astype(jnp.bfloat16)
        pick_second = (second_ref[...] == iota).astype(jnp.bfloat16)
        gather_chunk = min(GATHER_CHUNK, width)

        def gather(c, carry):
            off = pl.multiple_of(c * gather_chunk, gather_chunk)
            block = panel_ref[:, pl.ds(off, gather_chunk)]
            f_scr[:, pl.ds(off, gather_chunk)] = jnp.dot(
                pick_first, block, preferred_element_type=jnp.float32)
            s_scr[:, pl.ds(off, gather_chunk)] = jnp.dot(
                pick_second, block, preferred_element_type=jnp.float32)
            return carry

        lax.fori_loop(0, width // gather_chunk, gather, 0)
        nt = (((1,), (1,)), ((), ()))
        bin_chunk = min(BIN_CHUNK, part_bins)

        def chunk(kc, carry):
            off = pl.multiple_of(kc * bin_chunk, bin_chunk)
            cos_blk = cos_ref[:, pl.ds(off, bin_chunk)]
            sin_blk = sin_ref[:, pl.ds(off, bin_chunk)]
            for a in range(3):
                f_re = f_scr[:, pl.ds(2 * a * part_bins + off, bin_chunk)]
                f_im = f_scr[:, pl.ds((2 * a + 1) * part_bins + off, bin_chunk)]
                for b in range(3):
                    s_re = s_scr[:, pl.ds(2 * b * part_bins + off, bin_chunk)]
                    s_im = s_scr[:, pl.ds((2 * b + 1) * part_bins + off, bin_chunk)]
                    real_part = (f_re * s_re + f_im * s_im).astype(jnp.bfloat16)
                    imag_part = (f_im * s_re - f_re * s_im).astype(jnp.bfloat16)
                    acc = lax.dot_general(cos_blk, real_part, nt,
                                          preferred_element_type=jnp.float32)
                    acc = acc + lax.dot_general(sin_blk, imag_part, nt,
                                                preferred_element_type=jnp.float32)
                    out_ref[0, 3 * a + b] += acc
            return carry

        lax.fori_loop(0, part_bins // bin_chunk, chunk, 0)


def pair_sums(counts, first_idx, second_idx, panel, cos_rows, sin_rows, owners, chunk_id, acc):
    rows, width = panel.shape
    part_bins = width // 6
    pairs = first_idx.shape[0]
    per_owner = pairs // owners
    blocks_per_owner = per_owner // PAIR_BLOCK
    grid = (pairs // PAIR_BLOCK,)
    accumulate = acc is not None
    kernel = functools.partial(pair_kernel, blocks_per_owner=blocks_per_owner,
                               part_bins=part_bins, accumulate=accumulate)
    flops = 2 * pairs * rows * width * 2 + 2 * LAG_ROWS * 2 * part_bins * 9 * pairs
    out_bytes = owners * 9 * LAG_ROWS * per_owner * 4
    cost = pl.CostEstimate(flops=flops, transcendentals=0,
                           bytes_accessed=rows * width * 2 + out_bytes * (2 if accumulate else 1))
    out_spec = pl.BlockSpec(
        (1, 9, LAG_ROWS, PAIR_BLOCK),
        lambda i, c: (i // blocks_per_owner, 0, 0, i % blocks_per_owner))
    in_specs = [
        pl.BlockSpec((PAIR_BLOCK, 1), lambda i, c: (i, 0)),
        pl.BlockSpec((PAIR_BLOCK, 1), lambda i, c: (i, 0)),
        pl.BlockSpec((rows, width), lambda i, c: (0, 0)),
        pl.BlockSpec((LAG_ROWS, part_bins), lambda i, c: (0, chunk_id)),
        pl.BlockSpec((LAG_ROWS, part_bins), lambda i, c: (0, chunk_id)),
    ]
    args = [counts, first_idx, second_idx, panel, cos_rows, sin_rows]
    aliases = {}
    if accumulate:
        in_specs.append(out_spec)
        args.append(acc)
        aliases = {len(args) - 1: 0}
    return pl.pallas_call(
        kernel,
        out_shape=jax.ShapeDtypeStruct((owners, 9, LAG_ROWS, per_owner), jnp.float32),
        grid_spec=pltpu.PrefetchScalarGridSpec(
            num_scalar_prefetch=1,
            grid=grid,
            in_specs=in_specs,
            out_specs=out_spec,
            scratch_shapes=[
                pltpu.VMEM((PAIR_BLOCK, width), jnp.float32),
                pltpu.VMEM((PAIR_BLOCK, width), jnp.float32),
            ],
        ),
        input_output_aliases=aliases,
        compiler_params=pltpu.CompilerParams(
            dimension_semantics=("arbitrary",), vmem_limit_bytes=60 * 1024 * 1024),
        cost_estimate=cost,
    )(*args)


MESH_ID = pl.DeviceIdType.MESH


def spread_kernel(pieces_ref, panel_ref, send_plane, recv_plane, local_sem, send_right,
                  send_left, recv_ring, *, ring_size, plane_size, blk_size, slots):
    me_z = lax.axis_index("z")
    me_c = lax.axis_index("core")
    me_b = lax.axis_index("blk")
    me_q = me_c * blk_size + me_b
    right = (me_z + 1) % ring_size
    left = (me_z + ring_size - 1) % ring_size

    def plane_dev(q):
        return (me_z, q // blk_size, q % blk_size)

    barrier = pltpu.get_barrier_semaphore()

    def greet(i, carry):
        q = (me_q + i) % plane_size
        pl.semaphore_signal(barrier, 1, device_id=plane_dev(q), device_id_type=MESH_ID)
        return carry

    lax.fori_loop(1, plane_size, greet, 0)
    pl.semaphore_signal(barrier, 1, device_id=(right, me_c, me_b), device_id_type=MESH_ID)
    pl.semaphore_signal(barrier, 1, device_id=(left, me_c, me_b), device_id_type=MESH_ID)
    pl.semaphore_wait(barrier, plane_size + 1)

    block_rows = plane_size * slots
    base = me_z * block_rows

    def rows_of(q):
        return panel_ref.at[pl.ds(base + q * slots, slots)]

    local = pltpu.make_async_copy(pieces_ref.at[me_q], rows_of(me_q), local_sem)
    local.start()

    def plane_copy(q, src_q, dst_q):
        return pltpu.make_async_remote_copy(
            pieces_ref.at[q], rows_of(dst_q), send_plane.at[q], recv_plane.at[src_q],
            device_id=plane_dev(q), device_id_type=MESH_ID)

    def send(i, carry):
        q = (me_q + i) % plane_size
        plane_copy(q, me_q, me_q).start()
        return carry

    lax.fori_loop(1, plane_size, send, 0)

    def arrive(i, carry):
        q = (me_q + plane_size - i) % plane_size
        plane_copy(q, q, q).wait_recv()
        return carry

    lax.fori_loop(1, plane_size, arrive, 0)
    local.wait()

    def sent(i, carry):
        q = (me_q + i) % plane_size
        plane_copy(q, me_q, me_q).wait_send()
        return carry

    lax.fori_loop(1, plane_size, sent, 0)

    def block_of(k):
        return panel_ref.at[pl.ds(k * block_rows, block_rows)]

    def ring_copy(k, sem, dev):
        return pltpu.make_async_remote_copy(
            block_of(k), block_of(k), sem, recv_ring.at[k],
            device_id=(dev, me_c, me_b), device_id_type=MESH_ID)

    n_right = ring_size // 2
    n_left = ring_size - 1 - n_right
    right_sends = []
    left_sends = []
    for s in range(max(n_right, n_left)):
        if s < n_right:
            k = (me_z + ring_size - s) % ring_size
            if s > 0:
                ring_copy(k, send_right.at[s], left).wait_recv()
            c = ring_copy(k, send_right.at[s], right)
            c.start()
            right_sends.append(c)
        if s < n_left:
            k = (me_z + s) % ring_size
            if s > 0:
                ring_copy(k, send_left.at[s], right).wait_recv()
            c = ring_copy(k, send_left.at[s], left)
            c.start()
            left_sends.append(c)
    ring_copy((me_z + ring_size - n_right) % ring_size, send_right.at[0], left).wait_recv()
    if n_left > 0:
        ring_copy((me_z + n_left) % ring_size, send_left.at[0], right).wait_recv()
    for c in right_sends + left_sends:
        c.wait_send()


def spread(pieces, ring_size, plane_size, blk_size):
    _, slots, width = pieces.shape
    rows = ring_size * plane_size * slots
    kernel = functools.partial(spread_kernel, ring_size=ring_size, plane_size=plane_size,
                               blk_size=blk_size, slots=slots)
    n_right = ring_size // 2
    n_left = max(ring_size - 1 - n_right, 1)
    return pl.pallas_call(
        kernel,
        out_shape=jax.ShapeDtypeStruct((rows, width), pieces.dtype),
        in_specs=[pl.BlockSpec(memory_space=pl.ANY)],
        out_specs=pl.BlockSpec(memory_space=pl.ANY),
        scratch_shapes=[
            pltpu.SemaphoreType.DMA((plane_size,)),
            pltpu.SemaphoreType.DMA((plane_size,)),
            pltpu.SemaphoreType.DMA(()),
            pltpu.SemaphoreType.DMA((n_right,)),
            pltpu.SemaphoreType.DMA((n_left,)),
            pltpu.SemaphoreType.DMA((ring_size,)),
        ],
        compiler_params=pltpu.CompilerParams(collective_id=0, has_side_effects=True),
    )(pieces)


def shards(spectra, send_rows, send_counts, pair_rows, pair_counts):
    whitened = whiten(spectra)
    station_count, comps, parts, bin_count = whitened.shape
    row_width = comps * parts * bin_count
    slot_count = send_rows.shape[2]
    cores = lax.axis_size("core")
    part_bins = bin_count // cores
    core = lax.axis_index("core")

    flat = whitened.reshape(station_count, row_width)
    lists = send_rows[0]
    col_count = lists.shape[0]
    picked = jnp.take(flat, lists.reshape(-1), axis=0).reshape(col_count, slot_count, row_width)
    alive = jnp.arange(slot_count, dtype=jnp.int32)[None, :] < send_counts[0][:, None]
    picked = jnp.where(alive[:, :, None], picked, jnp.zeros_like(picked))
    pieces = picked.reshape(col_count, slot_count, comps * parts, cores, part_bins)
    pieces = jnp.transpose(pieces, (3, 0, 1, 2, 4)).reshape(
        cores * col_count, slot_count, comps * parts * part_bins)
    panel = spread(pieces, lax.axis_size("z"), cores * col_count, col_count)

    chip_pairs = lax.all_gather(pair_rows, "core", axis=1, tiled=True)
    chip_counts = lax.all_gather(pair_counts, "core", axis=0, tiled=True)
    cos_rows, sin_rows = lag_part(bin_count, core * part_bins, part_bins)
    partial = pair_sums(chip_counts, chip_pairs[0][:, None], chip_pairs[1][:, None],
                        panel, cos_rows, sin_rows, cores, 0, None)
    partial = lax.all_to_all(partial, "core", 0, 0, tiled=True)
    total = jnp.sum(partial, axis=0)[:, :LAGS, :] * (1.0 / math.sqrt(bin_count))
    pair_total = pair_rows.shape[1]
    live = jnp.arange(pair_total, dtype=jnp.int32) < pair_counts[0]
    total = jnp.where(live[None, None, :], total, 0.0).astype(jnp.bfloat16)
    return jnp.transpose(total, (1, 0, 2))


def solution(mesh):
    tile_size = mesh.shape["tile"]
    blk_size = mesh.shape["blk"]
    split = Mesh(mesh.devices.reshape(tile_size // 2, 2, blk_size), ("z", "core", "blk"))
    dev = ("z", "core", "blk")
    return jax.shard_map(
        shards,
        mesh=split,
        in_specs=(
            P(dev, None, None, None),
            P(dev, None, None),
            P(dev, None),
            P(None, dev),
            P(dev),
        ),
        out_specs=P(None, None, dev),
        check_vma=False,
    )
```

```python
import functools
import math

import jax
import ml_dtypes
import numpy as np
import jax.numpy as jnp
from jax import lax
from jax.experimental import pallas as pl
from jax.experimental.pallas import tpu as pltpu
from jax.sharding import Mesh
from jax.sharding import PartitionSpec as P

LAGS = 129
LAG_ROWS = 144
PAIR_BLOCK = 128
BIN_CHUNK = 256
GATHER_CHUNK = 512


def whiten(spectra):
    station_count = spectra.shape[0]
    bin_count = spectra.shape[-1]
    ramp_bins = bin_count // 32
    bin_index = jnp.arange(bin_count, dtype=jnp.int32)
    edge_dist = jnp.minimum(bin_index, bin_count - 1 - bin_index).astype(jnp.float32) + 0.5
    ramp_vals = 0.5 - 0.5 * jnp.cos(jnp.pi * edge_dist / ramp_bins)
    taper = jnp.where(edge_dist < ramp_bins, ramp_vals, jnp.ones_like(ramp_vals))
    blocked = spectra.reshape(station_count, 3, 2, bin_count // 64, 64)
    power = jnp.mean(blocked * blocked, axis=(1, 2, 4))
    inverse = 1.0 / jnp.sqrt(power + 1e-05)
    spread_scale = jnp.repeat(inverse, 64, axis=1)
    return (spectra * taper * spread_scale[:, None, None, :]).astype(jnp.bfloat16)


def lag_tables(bin_count):
    lag_index = np.arange(LAGS, dtype=np.int32) - LAGS // 2
    bin_index = np.arange(bin_count, dtype=np.int32)
    phase_steps = lag_index[:, None] * bin_index[None, :] % (2 * bin_count)
    angle = phase_steps.astype(np.float32) * np.float32(np.pi / bin_count)
    pad = ((0, LAG_ROWS - LAGS), (0, 0))
    cos_rows = np.pad(np.cos(angle).astype(np.float32).astype(ml_dtypes.bfloat16), pad)
    sin_rows = np.pad((-np.sin(angle)).astype(np.float32).astype(ml_dtypes.bfloat16), pad)
    return jnp.asarray(cos_rows), jnp.asarray(sin_rows)


def pair_kernel(counts_ref, first_ref, second_ref, panel_ref, cos_ref, sin_ref, *rest,
                blocks_per_owner, part_bins, accumulate):
    if accumulate:
        acc_ref, out_ref, f_scr, s_scr = rest
    else:
        out_ref, f_scr, s_scr = rest
    step = pl.program_id(0)
    owner = step // blocks_per_owner
    start = (step % blocks_per_owner) * PAIR_BLOCK
    live = start < counts_ref[owner]
    if accumulate:
        out_ref[...] = acc_ref[...]
    else:
        out_ref[...] = jnp.zeros_like(out_ref)

    @pl.when(live)
    def _():
        rows = panel_ref.shape[0]
        width = panel_ref.shape[1]
        iota = lax.broadcasted_iota(jnp.int32, (PAIR_BLOCK, rows), 1)
        pick_first = (first_ref[...] == iota).astype(jnp.bfloat16)
        pick_second = (second_ref[...] == iota).astype(jnp.bfloat16)
        gather_chunk = min(GATHER_CHUNK, width)

        def gather(c, carry):
            off = pl.multiple_of(c * gather_chunk, gather_chunk)
            block = panel_ref[:, pl.ds(off, gather_chunk)]
            f_scr[:, pl.ds(off, gather_chunk)] = jnp.dot(
                pick_first, block, preferred_element_type=jnp.float32)
            s_scr[:, pl.ds(off, gather_chunk)] = jnp.dot(
                pick_second, block, preferred_element_type=jnp.float32)
            return carry

        lax.fori_loop(0, width // gather_chunk, gather, 0)
        nt = (((1,), (1,)), ((), ()))
        bin_chunk = min(BIN_CHUNK, part_bins)

        def chunk(kc, carry):
            off = pl.multiple_of(kc * bin_chunk, bin_chunk)
            cos_blk = cos_ref[:, pl.ds(off, bin_chunk)]
            sin_blk = sin_ref[:, pl.ds(off, bin_chunk)]
            for a in range(3):
                f_re = f_scr[:, pl.ds(2 * a * part_bins + off, bin_chunk)]
                f_im = f_scr[:, pl.ds((2 * a + 1) * part_bins + off, bin_chunk)]
                for b in range(3):
                    s_re = s_scr[:, pl.ds(2 * b * part_bins + off, bin_chunk)]
                    s_im = s_scr[:, pl.ds((2 * b + 1) * part_bins + off, bin_chunk)]
                    real_part = (f_re * s_re + f_im * s_im).astype(jnp.bfloat16)
                    imag_part = (f_im * s_re - f_re * s_im).astype(jnp.bfloat16)
                    acc = lax.dot_general(cos_blk, real_part, nt,
                                          preferred_element_type=jnp.float32)
                    acc = acc + lax.dot_general(sin_blk, imag_part, nt,
                                                preferred_element_type=jnp.float32)
                    out_ref[0, 3 * a + b] += acc
            return carry

        lax.fori_loop(0, part_bins // bin_chunk, chunk, 0)


def pair_sums(counts, first_idx, second_idx, panel, cos_rows, sin_rows, owners, chunk_id, acc):
    rows, width = panel.shape
    part_bins = width // 6
    pairs = first_idx.shape[0]
    per_owner = pairs // owners
    blocks_per_owner = per_owner // PAIR_BLOCK
    grid = (pairs // PAIR_BLOCK,)
    accumulate = acc is not None
    kernel = functools.partial(pair_kernel, blocks_per_owner=blocks_per_owner,
                               part_bins=part_bins, accumulate=accumulate)
    flops = 2 * pairs * rows * width * 2 + 2 * LAG_ROWS * 2 * part_bins * 9 * pairs
    out_bytes = owners * 9 * LAG_ROWS * per_owner * 4
    cost = pl.CostEstimate(flops=flops, transcendentals=0,
                           bytes_accessed=rows * width * 2 + out_bytes * (2 if accumulate else 1))
    out_spec = pl.BlockSpec(
        (1, 9, LAG_ROWS, PAIR_BLOCK),
        lambda i, c: (i // blocks_per_owner, 0, 0, i % blocks_per_owner))
    in_specs = [
        pl.BlockSpec((PAIR_BLOCK, 1), lambda i, c: (i, 0)),
        pl.BlockSpec((PAIR_BLOCK, 1), lambda i, c: (i, 0)),
        pl.BlockSpec((rows, width), lambda i, c: (0, 0)),
        pl.BlockSpec((LAG_ROWS, part_bins), lambda i, c: (0, c[owners])),
        pl.BlockSpec((LAG_ROWS, part_bins), lambda i, c: (0, c[owners])),
    ]
    args = [counts, first_idx, second_idx, panel, cos_rows, sin_rows]
    aliases = {}
    if accumulate:
        in_specs.append(out_spec)
        args.append(acc)
        aliases = {len(args) - 1: 0}
    return pl.pallas_call(
        kernel,
        out_shape=jax.ShapeDtypeStruct((owners, 9, LAG_ROWS, per_owner), jnp.float32),
        grid_spec=pltpu.PrefetchScalarGridSpec(
            num_scalar_prefetch=1,
            grid=grid,
            in_specs=in_specs,
            out_specs=out_spec,
            scratch_shapes=[
                pltpu.VMEM((PAIR_BLOCK, width), jnp.float32),
                pltpu.VMEM((PAIR_BLOCK, width), jnp.float32),
            ],
        ),
        input_output_aliases=aliases,
        compiler_params=pltpu.CompilerParams(
            dimension_semantics=("arbitrary",), vmem_limit_bytes=60 * 1024 * 1024),
        cost_estimate=cost,
    )(*args)


MESH_ID = pl.DeviceIdType.MESH


def spread_kernel(pieces_ref, panel_ref, send_plane, recv_plane, local_sem, send_right,
                  send_left, recv_ring, *, ring_size, plane_size, blk_size, slots):
    me_z = lax.axis_index("z")
    me_c = lax.axis_index("core")
    me_b = lax.axis_index("blk")
    me_q = me_c * blk_size + me_b
    right = (me_z + 1) % ring_size
    left = (me_z + ring_size - 1) % ring_size

    def plane_dev(q):
        return (me_z, q // blk_size, q % blk_size)

    barrier = pltpu.get_barrier_semaphore()

    def greet(i, carry):
        q = (me_q + i) % plane_size
        pl.semaphore_signal(barrier, 1, device_id=plane_dev(q), device_id_type=MESH_ID)
        return carry

    lax.fori_loop(1, plane_size, greet, 0)
    pl.semaphore_signal(barrier, 1, device_id=(right, me_c, me_b), device_id_type=MESH_ID)
    pl.semaphore_signal(barrier, 1, device_id=(left, me_c, me_b), device_id_type=MESH_ID)
    pl.semaphore_wait(barrier, plane_size + 1)

    block_rows = plane_size * slots
    base = me_z * block_rows

    def rows_of(q):
        return panel_ref.at[pl.ds(base + q * slots, slots)]

    local = pltpu.make_async_copy(pieces_ref.at[me_q], rows_of(me_q), local_sem)
    local.start()

    def plane_copy(q, src_q, dst_q):
        return pltpu.make_async_remote_copy(
            pieces_ref.at[q], rows_of(dst_q), send_plane.at[q], recv_plane.at[src_q],
            device_id=plane_dev(q), device_id_type=MESH_ID)

    def send(i, carry):
        q = (me_q + i) % plane_size
        plane_copy(q, me_q, me_q).start()
        return carry

    lax.fori_loop(1, plane_size, send, 0)

    def arrive(i, carry):
        q = (me_q + plane_size - i) % plane_size
        plane_copy(q, q, q).wait_recv()
        return carry

    lax.fori_loop(1, plane_size, arrive, 0)
    local.wait()

    def sent(i, carry):
        q = (me_q + i) % plane_size
        plane_copy(q, me_q, me_q).wait_send()
        return carry

    lax.fori_loop(1, plane_size, sent, 0)

    def block_of(k):
        return panel_ref.at[pl.ds(k * block_rows, block_rows)]

    def ring_copy(k, sem, dev):
        return pltpu.make_async_remote_copy(
            block_of(k), block_of(k), sem, recv_ring.at[k],
            device_id=(dev, me_c, me_b), device_id_type=MESH_ID)

    half = ring_size // 2
    half_rows = block_rows // 2

    def part_of(k, first):
        start = k * block_rows + (0 if first else half_rows)
        return panel_ref.at[pl.ds(start, half_rows)]

    def part_copy(k, first, sem, dev):
        slot = k if first else ring_size
        return pltpu.make_async_remote_copy(
            part_of(k, first), part_of(k, first), sem, recv_ring.at[slot],
            device_id=(dev, me_c, me_b), device_id_type=MESH_ID)

    sends = []
    for s in range(half):
        k = (me_z + ring_size - s) % ring_size
        if s > 0:
            ring_copy(k, send_right.at[s], left).wait_recv()
        c = ring_copy(k, send_right.at[s], right) if s < half - 1 else part_copy(
            k, True, send_right.at[s], right)
        c.start()
        sends.append(c)
        k = (me_z + s) % ring_size
        if s > 0:
            ring_copy(k, send_left.at[s], right).wait_recv()
        c = ring_copy(k, send_left.at[s], left) if s < half - 1 else part_copy(
            k, False, send_left.at[s], left)
        c.start()
        sends.append(c)
    far = (me_z + half) % ring_size
    part_copy(far, True, send_right.at[0], left).wait_recv()
    part_copy(far, False, send_left.at[0], right).wait_recv()
    for c in sends:
        c.wait_send()


def spread(pieces, ring_size, plane_size, blk_size):
    _, slots, width = pieces.shape
    rows = ring_size * plane_size * slots
    kernel = functools.partial(spread_kernel, ring_size=ring_size, plane_size=plane_size,
                               blk_size=blk_size, slots=slots)
    half = ring_size // 2
    return pl.pallas_call(
        kernel,
        out_shape=jax.ShapeDtypeStruct((rows, width), pieces.dtype),
        in_specs=[pl.BlockSpec(memory_space=pl.ANY)],
        out_specs=pl.BlockSpec(memory_space=pl.ANY),
        scratch_shapes=[
            pltpu.SemaphoreType.DMA((plane_size,)),
            pltpu.SemaphoreType.DMA((plane_size,)),
            pltpu.SemaphoreType.DMA(()),
            pltpu.SemaphoreType.DMA((half,)),
            pltpu.SemaphoreType.DMA((half,)),
            pltpu.SemaphoreType.DMA((ring_size + 1,)),
        ],
        compiler_params=pltpu.CompilerParams(collective_id=0, has_side_effects=True),
    )(pieces)


def shards(spectra, send_rows, send_counts, pair_rows, pair_counts):
    whitened = whiten(spectra)
    station_count, comps, parts, bin_count = whitened.shape
    row_width = comps * parts * bin_count
    slot_count = send_rows.shape[2]
    cores = lax.axis_size("core")
    part_bins = bin_count // cores
    core = lax.axis_index("core")

    flat = whitened.reshape(station_count, row_width)
    lists = send_rows[0]
    col_count = lists.shape[0]
    picked = jnp.take(flat, lists.reshape(-1), axis=0).reshape(col_count, slot_count, row_width)
    alive = jnp.arange(slot_count, dtype=jnp.int32)[None, :] < send_counts[0][:, None]
    picked = jnp.where(alive[:, :, None], picked, jnp.zeros_like(picked))
    pieces = picked.reshape(col_count, slot_count, comps * parts, cores, part_bins)
    pieces = jnp.transpose(pieces, (3, 0, 1, 2, 4)).reshape(
        cores * col_count, slot_count, comps * parts * part_bins)
    panel = spread(pieces, lax.axis_size("z"), cores * col_count, col_count)

    chip_pairs = lax.all_gather(pair_rows, "core", axis=1, tiled=True)
    chip_counts = lax.all_gather(pair_counts, "core", axis=0, tiled=True)
    cos_rows, sin_rows = lag_tables(bin_count)
    chip_counts = jnp.concatenate([chip_counts, core.astype(jnp.int32)[None]])
    partial = pair_sums(chip_counts, chip_pairs[0][:, None], chip_pairs[1][:, None],
                        panel, cos_rows, sin_rows, cores, 0, None)
    partial = lax.all_to_all(partial, "core", 0, 0, tiled=True)
    total = jnp.sum(partial, axis=0)[:, :LAGS, :] * (1.0 / math.sqrt(bin_count))
    pair_total = pair_rows.shape[1]
    live = jnp.arange(pair_total, dtype=jnp.int32) < pair_counts[0]
    total = jnp.where(live[None, None, :], total, 0.0).astype(jnp.bfloat16)
    return jnp.transpose(total, (1, 0, 2))


def solution(mesh):
    tile_size = mesh.shape["tile"]
    blk_size = mesh.shape["blk"]
    split = Mesh(mesh.devices.reshape(tile_size // 2, 2, blk_size), ("z", "core", "blk"))
    dev = ("z", "core", "blk")
    return jax.shard_map(
        shards,
        mesh=split,
        in_specs=(
            P(dev, None, None, None),
            P(dev, None, None),
            P(dev, None),
            P(None, dev),
            P(dev),
        ),
        out_specs=P(None, None, dev),
        check_vma=False,
    )
```

```python
import functools
import math

import jax
import ml_dtypes
import numpy as np
import jax.numpy as jnp
from jax import lax
from jax.experimental import pallas as pl
from jax.experimental.pallas import tpu as pltpu
from jax.sharding import Mesh
from jax.sharding import PartitionSpec as P

LAGS = 129
LAG_ROWS = 144
PAIR_BLOCK = 128
BIN_CHUNK = 256
GATHER_CHUNK = 512


def whiten(spectra):
    station_count = spectra.shape[0]
    bin_count = spectra.shape[-1]
    ramp_bins = bin_count // 32
    bin_index = jnp.arange(bin_count, dtype=jnp.int32)
    edge_dist = jnp.minimum(bin_index, bin_count - 1 - bin_index).astype(jnp.float32) + 0.5
    ramp_vals = 0.5 - 0.5 * jnp.cos(jnp.pi * edge_dist / ramp_bins)
    taper = jnp.where(edge_dist < ramp_bins, ramp_vals, jnp.ones_like(ramp_vals))
    blocked = spectra.reshape(station_count, 3, 2, bin_count // 64, 64)
    power = jnp.mean(blocked * blocked, axis=(1, 2, 4))
    inverse = 1.0 / jnp.sqrt(power + 1e-05)
    spread_scale = jnp.repeat(inverse, 64, axis=1)
    return (spectra * taper * spread_scale[:, None, None, :]).astype(jnp.bfloat16)


def lag_tables(bin_count):
    lag_index = np.arange(LAGS, dtype=np.int32) - LAGS // 2
    bin_index = np.arange(bin_count, dtype=np.int32)
    phase_steps = lag_index[:, None] * bin_index[None, :] % (2 * bin_count)
    angle = phase_steps.astype(np.float32) * np.float32(np.pi / bin_count)
    pad = ((0, LAG_ROWS - LAGS), (0, 0))
    cos_rows = np.pad(np.cos(angle).astype(np.float32).astype(ml_dtypes.bfloat16), pad)
    sin_rows = np.pad((-np.sin(angle)).astype(np.float32).astype(ml_dtypes.bfloat16), pad)
    return jnp.asarray(cos_rows), jnp.asarray(sin_rows)


def pair_kernel(counts_ref, first_ref, second_ref, panel_ref, cos_ref, sin_ref, *rest,
                blocks_per_owner, part_bins, accumulate):
    if accumulate:
        acc_ref, out_ref, f_scr, s_scr = rest
    else:
        out_ref, f_scr, s_scr = rest
    step = pl.program_id(0)
    owner = step // blocks_per_owner
    start = (step % blocks_per_owner) * PAIR_BLOCK
    live = start < counts_ref[owner]
    if accumulate:
        out_ref[...] = acc_ref[...]
    else:
        out_ref[...] = jnp.zeros_like(out_ref)

    @pl.when(live)
    def _():
        rows = panel_ref.shape[0]
        width = panel_ref.shape[1]
        iota = lax.broadcasted_iota(jnp.int32, (PAIR_BLOCK, rows), 1)
        pick_first = (first_ref[...] == iota).astype(jnp.bfloat16)
        pick_second = (second_ref[...] == iota).astype(jnp.bfloat16)
        gather_chunk = min(GATHER_CHUNK, width)

        def gather(c, carry):
            off = pl.multiple_of(c * gather_chunk, gather_chunk)
            block = panel_ref[:, pl.ds(off, gather_chunk)]
            f_scr[:, pl.ds(off, gather_chunk)] = jnp.dot(
                pick_first, block, preferred_element_type=jnp.float32)
            s_scr[:, pl.ds(off, gather_chunk)] = jnp.dot(
                pick_second, block, preferred_element_type=jnp.float32)
            return carry

        lax.fori_loop(0, width // gather_chunk, gather, 0)
        nt = (((1,), (1,)), ((), ()))
        bin_chunk = min(BIN_CHUNK, part_bins)

        def chunk(kc, carry):
            off = pl.multiple_of(kc * bin_chunk, bin_chunk)
            cos_blk = cos_ref[:, pl.ds(off, bin_chunk)]
            sin_blk = sin_ref[:, pl.ds(off, bin_chunk)]
            for a in range(3):
                f_re = f_scr[:, pl.ds(2 * a * part_bins + off, bin_chunk)]
                f_im = f_scr[:, pl.ds((2 * a + 1) * part_bins + off, bin_chunk)]
                for b in range(3):
                    s_re = s_scr[:, pl.ds(2 * b * part_bins + off, bin_chunk)]
                    s_im = s_scr[:, pl.ds((2 * b + 1) * part_bins + off, bin_chunk)]
                    real_part = (f_re * s_re + f_im * s_im).astype(jnp.bfloat16)
                    imag_part = (f_im * s_re - f_re * s_im).astype(jnp.bfloat16)
                    acc = lax.dot_general(cos_blk, real_part, nt,
                                          preferred_element_type=jnp.float32)
                    acc = acc + lax.dot_general(sin_blk, imag_part, nt,
                                                preferred_element_type=jnp.float32)
                    out_ref[0, 3 * a + b] += acc
            return carry

        lax.fori_loop(0, part_bins // bin_chunk, chunk, 0)


def pair_sums(counts, first_idx, second_idx, panel, cos_rows, sin_rows, owners, chunk_id, acc):
    rows, width = panel.shape
    part_bins = width // 6
    pairs = first_idx.shape[0]
    per_owner = pairs // owners
    blocks_per_owner = per_owner // PAIR_BLOCK
    grid = (pairs // PAIR_BLOCK,)
    accumulate = acc is not None
    kernel = functools.partial(pair_kernel, blocks_per_owner=blocks_per_owner,
                               part_bins=part_bins, accumulate=accumulate)
    flops = 2 * pairs * rows * width * 2 + 2 * LAG_ROWS * 2 * part_bins * 9 * pairs
    out_bytes = owners * 9 * LAG_ROWS * per_owner * 4
    cost = pl.CostEstimate(flops=flops, transcendentals=0,
                           bytes_accessed=rows * width * 2 + out_bytes * (2 if accumulate else 1))
    out_spec = pl.BlockSpec(
        (1, 9, LAG_ROWS, PAIR_BLOCK),
        lambda i, c: (i // blocks_per_owner, 0, 0, i % blocks_per_owner))
    in_specs = [
        pl.BlockSpec((PAIR_BLOCK, 1), lambda i, c: (i, 0)),
        pl.BlockSpec((PAIR_BLOCK, 1), lambda i, c: (i, 0)),
        pl.BlockSpec((rows, width), lambda i, c: (0, 0)),
        pl.BlockSpec((LAG_ROWS, part_bins), lambda i, c: (0, c[owners])),
        pl.BlockSpec((LAG_ROWS, part_bins), lambda i, c: (0, c[owners])),
    ]
    args = [counts, first_idx, second_idx, panel, cos_rows, sin_rows]
    aliases = {}
    if accumulate:
        in_specs.append(out_spec)
        args.append(acc)
        aliases = {len(args) - 1: 0}
    return pl.pallas_call(
        kernel,
        out_shape=jax.ShapeDtypeStruct((owners, 9, LAG_ROWS, per_owner), jnp.float32),
        grid_spec=pltpu.PrefetchScalarGridSpec(
            num_scalar_prefetch=1,
            grid=grid,
            in_specs=in_specs,
            out_specs=out_spec,
            scratch_shapes=[
                pltpu.VMEM((PAIR_BLOCK, width), jnp.float32),
                pltpu.VMEM((PAIR_BLOCK, width), jnp.float32),
            ],
        ),
        input_output_aliases=aliases,
        compiler_params=pltpu.CompilerParams(
            dimension_semantics=("arbitrary",), vmem_limit_bytes=60 * 1024 * 1024),
        cost_estimate=cost,
    )(*args)


MESH_ID = pl.DeviceIdType.MESH


def spread_kernel(pieces_ref, meta_ref, panel_ref, chip_meta_ref, send_plane, recv_plane,
                  local_sem, send_right, send_left, recv_ring, meta_sems, *, ring_size,
                  plane_size, blk_size, slots):
    me_z = lax.axis_index("z")
    me_c = lax.axis_index("core")
    me_b = lax.axis_index("blk")
    me_q = me_c * blk_size + me_b
    right = (me_z + 1) % ring_size
    left = (me_z + ring_size - 1) % ring_size

    def plane_dev(q):
        return (me_z, q // blk_size, q % blk_size)

    barrier = pltpu.get_barrier_semaphore()

    def greet(i, carry):
        q = (me_q + i) % plane_size
        pl.semaphore_signal(barrier, 1, device_id=plane_dev(q), device_id_type=MESH_ID)
        return carry

    lax.fori_loop(1, plane_size, greet, 0)
    pl.semaphore_signal(barrier, 1, device_id=(right, me_c, me_b), device_id_type=MESH_ID)
    pl.semaphore_signal(barrier, 1, device_id=(left, me_c, me_b), device_id_type=MESH_ID)
    pl.semaphore_wait(barrier, plane_size + 1)

    partner = (me_z, 1 - me_c, me_b)
    meta_local = pltpu.make_async_copy(meta_ref, chip_meta_ref.at[me_c], meta_sems.at[0])
    meta_local.start()
    meta_copy = pltpu.make_async_remote_copy(
        meta_ref, chip_meta_ref.at[me_c], meta_sems.at[1], meta_sems.at[2],
        device_id=partner, device_id_type=MESH_ID)
    meta_copy.start()

    block_rows = plane_size * slots
    base = me_z * block_rows

    def rows_of(q):
        return panel_ref.at[pl.ds(base + q * slots, slots)]

    local = pltpu.make_async_copy(pieces_ref.at[me_q], rows_of(me_q), local_sem)
    local.start()

    def plane_copy(q, src_q, dst_q):
        return pltpu.make_async_remote_copy(
            pieces_ref.at[q], rows_of(dst_q), send_plane.at[q], recv_plane.at[src_q],
            device_id=plane_dev(q), device_id_type=MESH_ID)

    def send(i, carry):
        q = (me_q + i) % plane_size
        plane_copy(q, me_q, me_q).start()
        return carry

    lax.fori_loop(1, plane_size, send, 0)

    def arrive(i, carry):
        q = (me_q + plane_size - i) % plane_size
        plane_copy(q, q, q).wait_recv()
        return carry

    lax.fori_loop(1, plane_size, arrive, 0)
    local.wait()

    def sent(i, carry):
        q = (me_q + i) % plane_size
        plane_copy(q, me_q, me_q).wait_send()
        return carry

    lax.fori_loop(1, plane_size, sent, 0)

    def block_of(k):
        return panel_ref.at[pl.ds(k * block_rows, block_rows)]

    def ring_copy(k, sem, dev):
        return pltpu.make_async_remote_copy(
            block_of(k), block_of(k), sem, recv_ring.at[k],
            device_id=(dev, me_c, me_b), device_id_type=MESH_ID)

    half = ring_size // 2
    half_rows = block_rows // 2

    def part_of(k, first):
        start = k * block_rows + (0 if first else half_rows)
        return panel_ref.at[pl.ds(start, half_rows)]

    def part_copy(k, first, sem, dev):
        slot = k if first else ring_size
        return pltpu.make_async_remote_copy(
            part_of(k, first), part_of(k, first), sem, recv_ring.at[slot],
            device_id=(dev, me_c, me_b), device_id_type=MESH_ID)

    sends = []
    for s in range(half):
        k = (me_z + ring_size - s) % ring_size
        if s > 0:
            ring_copy(k, send_right.at[s], left).wait_recv()
        c = ring_copy(k, send_right.at[s], right) if s < half - 1 else part_copy(
            k, True, send_right.at[s], right)
        c.start()
        sends.append(c)
        k = (me_z + s) % ring_size
        if s > 0:
            ring_copy(k, send_left.at[s], right).wait_recv()
        c = ring_copy(k, send_left.at[s], left) if s < half - 1 else part_copy(
            k, False, send_left.at[s], left)
        c.start()
        sends.append(c)
    far = (me_z + half) % ring_size
    part_copy(far, True, send_right.at[0], left).wait_recv()
    part_copy(far, False, send_left.at[0], right).wait_recv()
    for c in sends:
        c.wait_send()
    meta_local.wait()
    pltpu.make_async_remote_copy(
        meta_ref, chip_meta_ref.at[1 - me_c], meta_sems.at[1], meta_sems.at[2],
        device_id=partner, device_id_type=MESH_ID).wait_recv()
    meta_copy.wait_send()


def spread(pieces, meta, ring_size, plane_size, blk_size):
    _, slots, width = pieces.shape
    rows = ring_size * plane_size * slots
    kernel = functools.partial(spread_kernel, ring_size=ring_size, plane_size=plane_size,
                               blk_size=blk_size, slots=slots)
    half = ring_size // 2
    return pl.pallas_call(
        kernel,
        out_shape=(jax.ShapeDtypeStruct((rows, width), pieces.dtype),
                   jax.ShapeDtypeStruct((2,) + meta.shape, meta.dtype)),
        in_specs=[pl.BlockSpec(memory_space=pl.ANY), pl.BlockSpec(memory_space=pl.ANY)],
        out_specs=(pl.BlockSpec(memory_space=pl.ANY), pl.BlockSpec(memory_space=pl.ANY)),
        scratch_shapes=[
            pltpu.SemaphoreType.DMA((plane_size,)),
            pltpu.SemaphoreType.DMA((plane_size,)),
            pltpu.SemaphoreType.DMA(()),
            pltpu.SemaphoreType.DMA((half,)),
            pltpu.SemaphoreType.DMA((half,)),
            pltpu.SemaphoreType.DMA((ring_size + 1,)),
            pltpu.SemaphoreType.DMA((3,)),
        ],
        compiler_params=pltpu.CompilerParams(collective_id=0, has_side_effects=True),
    )(pieces, meta)


def shards(spectra, send_rows, send_counts, pair_rows, pair_counts):
    whitened = whiten(spectra)
    station_count, comps, parts, bin_count = whitened.shape
    row_width = comps * parts * bin_count
    slot_count = send_rows.shape[2]
    cores = lax.axis_size("core")
    part_bins = bin_count // cores
    core = lax.axis_index("core")

    flat = whitened.reshape(station_count, row_width)
    lists = send_rows[0]
    col_count = lists.shape[0]
    picked = jnp.take(flat, lists.reshape(-1), axis=0).reshape(col_count, slot_count, row_width)
    alive = jnp.arange(slot_count, dtype=jnp.int32)[None, :] < send_counts[0][:, None]
    picked = jnp.where(alive[:, :, None], picked, jnp.zeros_like(picked))
    pieces = picked.reshape(col_count, slot_count, comps * parts, cores, part_bins)
    pieces = jnp.transpose(pieces, (3, 0, 1, 2, 4)).reshape(
        cores * col_count, slot_count, comps * parts * part_bins)
    pair_total = pair_rows.shape[1]
    meta = jnp.concatenate(
        [pair_rows, jnp.broadcast_to(pair_counts[:, None], (1, pair_total))], axis=0)
    panel, chip_meta = spread(pieces, meta, lax.axis_size("z"), cores * col_count, col_count)
    cos_rows, sin_rows = lag_tables(bin_count)
    chip_counts = jnp.concatenate([chip_meta[:, 2, 0], core.astype(jnp.int32)[None]])
    chip_first = chip_meta[:, 0, :].reshape(cores * pair_total, 1)
    chip_second = chip_meta[:, 1, :].reshape(cores * pair_total, 1)
    partial = pair_sums(chip_counts, chip_first, chip_second,
                        panel, cos_rows, sin_rows, cores, 0, None)
    partial = lax.all_to_all(partial, "core", 0, 0, tiled=True)
    total = jnp.sum(partial, axis=0)[:, :LAGS, :] * (1.0 / math.sqrt(bin_count))
    live = jnp.arange(pair_total, dtype=jnp.int32) < pair_counts[0]
    total = jnp.where(live[None, None, :], total, 0.0).astype(jnp.bfloat16)
    return jnp.transpose(total, (1, 0, 2))


def solution(mesh):
    tile_size = mesh.shape["tile"]
    blk_size = mesh.shape["blk"]
    split = Mesh(mesh.devices.reshape(tile_size // 2, 2, blk_size), ("z", "core", "blk"))
    dev = ("z", "core", "blk")
    return jax.shard_map(
        shards,
        mesh=split,
        in_specs=(
            P(dev, None, None, None),
            P(dev, None, None),
            P(dev, None),
            P(None, dev),
            P(dev),
        ),
        out_specs=P(None, None, dev),
        check_vma=False,
    )
```

```python
import functools
import math

import jax
import ml_dtypes
import numpy as np
import jax.numpy as jnp
from jax import lax
from jax.experimental import pallas as pl
from jax.experimental.pallas import tpu as pltpu
from jax.sharding import Mesh
from jax.sharding import PartitionSpec as P

LAGS = 129
LAG_ROWS = 144
PAIR_BLOCK = 128
BIN_CHUNK = 256
GATHER_CHUNK = 512


def whiten(spectra):
    station_count = spectra.shape[0]
    bin_count = spectra.shape[-1]
    ramp_bins = bin_count // 32
    bin_index = jnp.arange(bin_count, dtype=jnp.int32)
    edge_dist = jnp.minimum(bin_index, bin_count - 1 - bin_index).astype(jnp.float32) + 0.5
    ramp_vals = 0.5 - 0.5 * jnp.cos(jnp.pi * edge_dist / ramp_bins)
    taper = jnp.where(edge_dist < ramp_bins, ramp_vals, jnp.ones_like(ramp_vals))
    blocked = spectra.reshape(station_count, 3, 2, bin_count // 64, 64)
    power = jnp.mean(blocked * blocked, axis=(1, 2, 4))
    inverse = 1.0 / jnp.sqrt(power + 1e-05)
    spread_scale = jnp.repeat(inverse, 64, axis=1)
    return (spectra * taper * spread_scale[:, None, None, :]).astype(jnp.bfloat16)


def lag_tables(bin_count):
    lag_index = np.arange(LAGS, dtype=np.int32) - LAGS // 2
    bin_index = np.arange(bin_count, dtype=np.int32)
    phase_steps = lag_index[:, None] * bin_index[None, :] % (2 * bin_count)
    angle = phase_steps.astype(np.float32) * np.float32(np.pi / bin_count)
    pad = ((0, LAG_ROWS - LAGS), (0, 0))
    cos_rows = np.pad(np.cos(angle).astype(np.float32).astype(ml_dtypes.bfloat16), pad)
    sin_rows = np.pad((-np.sin(angle)).astype(np.float32).astype(ml_dtypes.bfloat16), pad)
    return jnp.asarray(cos_rows), jnp.asarray(sin_rows)


def pair_kernel(counts_ref, first_ref, second_ref, panel_ref, cos_ref, sin_ref, *rest,
                blocks_per_owner, part_bins, accumulate):
    if accumulate:
        acc_ref, out_ref, f_scr, s_scr = rest
    else:
        out_ref, f_scr, s_scr = rest
    step = pl.program_id(0)
    owner = step // blocks_per_owner
    start = (step % blocks_per_owner) * PAIR_BLOCK
    live = start < counts_ref[owner]
    if accumulate:
        out_ref[...] = acc_ref[...]
    else:
        out_ref[...] = jnp.zeros_like(out_ref)

    @pl.when(live)
    def _():
        rows = panel_ref.shape[0]
        width = panel_ref.shape[1]
        iota = lax.broadcasted_iota(jnp.int32, (PAIR_BLOCK, rows), 1)
        pick_first = (first_ref[...] == iota).astype(jnp.bfloat16)
        pick_second = (second_ref[...] == iota).astype(jnp.bfloat16)
        gather_chunk = min(GATHER_CHUNK, width)

        def gather(c, carry):
            off = pl.multiple_of(c * gather_chunk, gather_chunk)
            block = panel_ref[:, pl.ds(off, gather_chunk)]
            f_scr[:, pl.ds(off, gather_chunk)] = jnp.dot(
                pick_first, block, preferred_element_type=jnp.float32)
            s_scr[:, pl.ds(off, gather_chunk)] = jnp.dot(
                pick_second, block, preferred_element_type=jnp.float32)
            return carry

        lax.fori_loop(0, width // gather_chunk, gather, 0)
        nt = (((1,), (1,)), ((), ()))
        bin_chunk = min(BIN_CHUNK, part_bins)

        def chunk(kc, carry):
            off = pl.multiple_of(kc * bin_chunk, bin_chunk)
            cos_blk = cos_ref[:, pl.ds(off, bin_chunk)]
            sin_blk = sin_ref[:, pl.ds(off, bin_chunk)]
            for a in range(3):
                f_re = f_scr[:, pl.ds(2 * a * part_bins + off, bin_chunk)]
                f_im = f_scr[:, pl.ds((2 * a + 1) * part_bins + off, bin_chunk)]
                for b in range(3):
                    s_re = s_scr[:, pl.ds(2 * b * part_bins + off, bin_chunk)]
                    s_im = s_scr[:, pl.ds((2 * b + 1) * part_bins + off, bin_chunk)]
                    real_part = (f_re * s_re + f_im * s_im).astype(jnp.bfloat16)
                    imag_part = (f_im * s_re - f_re * s_im).astype(jnp.bfloat16)
                    acc = lax.dot_general(cos_blk, real_part, nt,
                                          preferred_element_type=jnp.float32)
                    acc = acc + lax.dot_general(sin_blk, imag_part, nt,
                                                preferred_element_type=jnp.float32)
                    out_ref[0, 3 * a + b] += acc
            return carry

        lax.fori_loop(0, part_bins // bin_chunk, chunk, 0)


def pair_sums(counts, first_idx, second_idx, panel, cos_rows, sin_rows, owners, chunk_id, acc):
    rows, width = panel.shape
    part_bins = width // 6
    pairs = first_idx.shape[0]
    per_owner = pairs // owners
    blocks_per_owner = per_owner // PAIR_BLOCK
    grid = (pairs // PAIR_BLOCK,)
    accumulate = acc is not None
    kernel = functools.partial(pair_kernel, blocks_per_owner=blocks_per_owner,
                               part_bins=part_bins, accumulate=accumulate)
    flops = 2 * pairs * rows * width * 2 + 2 * LAG_ROWS * 2 * part_bins * 9 * pairs
    out_bytes = owners * 9 * LAG_ROWS * per_owner * 4
    cost = pl.CostEstimate(flops=flops, transcendentals=0,
                           bytes_accessed=rows * width * 2 + out_bytes * (2 if accumulate else 1))
    out_spec = pl.BlockSpec(
        (1, 9, LAG_ROWS, PAIR_BLOCK),
        lambda i, c: (i // blocks_per_owner, 0, 0, i % blocks_per_owner))
    in_specs = [
        pl.BlockSpec((PAIR_BLOCK, 1), lambda i, c: (i, 0)),
        pl.BlockSpec((PAIR_BLOCK, 1), lambda i, c: (i, 0)),
        pl.BlockSpec((rows, width), lambda i, c: (0, 0)),
        pl.BlockSpec((LAG_ROWS, part_bins), lambda i, c: (0, c[owners])),
        pl.BlockSpec((LAG_ROWS, part_bins), lambda i, c: (0, c[owners])),
    ]
    args = [counts, first_idx, second_idx, panel, cos_rows, sin_rows]
    aliases = {}
    if accumulate:
        in_specs.append(out_spec)
        args.append(acc)
        aliases = {len(args) - 1: 0}
    return pl.pallas_call(
        kernel,
        out_shape=jax.ShapeDtypeStruct((owners, 9, LAG_ROWS, per_owner), jnp.float32),
        grid_spec=pltpu.PrefetchScalarGridSpec(
            num_scalar_prefetch=1,
            grid=grid,
            in_specs=in_specs,
            out_specs=out_spec,
            scratch_shapes=[
                pltpu.VMEM((PAIR_BLOCK, width), jnp.float32),
                pltpu.VMEM((PAIR_BLOCK, width), jnp.float32),
            ],
        ),
        input_output_aliases=aliases,
        compiler_params=pltpu.CompilerParams(
            dimension_semantics=("arbitrary",), vmem_limit_bytes=60 * 1024 * 1024),
        cost_estimate=cost,
    )(*args)


MESH_ID = pl.DeviceIdType.MESH


def spread_kernel(pieces_ref, meta_ref, panel_ref, chip_meta_ref, send_plane, recv_plane,
                  local_sem, send_right, send_left, recv_ring, meta_sems, *, ring_size,
                  plane_size, blk_size, slots):
    me_z = lax.axis_index("z")
    me_c = lax.axis_index("core")
    me_b = lax.axis_index("blk")
    me_q = me_c * blk_size + me_b
    right = (me_z + 1) % ring_size
    left = (me_z + ring_size - 1) % ring_size

    def plane_dev(q):
        return (me_z, q // blk_size, q % blk_size)

    barrier = pltpu.get_barrier_semaphore()

    def greet(i, carry):
        q = (me_q + i) % plane_size
        pl.semaphore_signal(barrier, 1, device_id=plane_dev(q), device_id_type=MESH_ID)
        return carry

    lax.fori_loop(1, plane_size, greet, 0)
    pl.semaphore_signal(barrier, 1, device_id=(right, me_c, me_b), device_id_type=MESH_ID)
    pl.semaphore_signal(barrier, 1, device_id=(left, me_c, me_b), device_id_type=MESH_ID)
    pl.semaphore_wait(barrier, plane_size + 1)

    partner = (me_z, 1 - me_c, me_b)
    meta_local = pltpu.make_async_copy(meta_ref, chip_meta_ref.at[me_c], meta_sems.at[0])
    meta_local.start()
    meta_copy = pltpu.make_async_remote_copy(
        meta_ref, chip_meta_ref.at[me_c], meta_sems.at[1], meta_sems.at[2],
        device_id=partner, device_id_type=MESH_ID)
    meta_copy.start()

    block_rows = plane_size * slots
    base = me_z * block_rows

    def rows_of(q):
        return panel_ref.at[pl.ds(base + q * slots, slots)]

    local = pltpu.make_async_copy(pieces_ref.at[me_q], rows_of(me_q), local_sem)
    local.start()

    def plane_copy(q, src_q, dst_q):
        return pltpu.make_async_remote_copy(
            pieces_ref.at[q], rows_of(dst_q), send_plane.at[q], recv_plane.at[src_q],
            device_id=plane_dev(q), device_id_type=MESH_ID)

    def send(i, carry):
        q = (me_q + i) % plane_size
        plane_copy(q, me_q, me_q).start()
        return carry

    lax.fori_loop(1, plane_size, send, 0)

    def arrive(i, carry):
        q = (me_q + plane_size - i) % plane_size
        plane_copy(q, q, q).wait_recv()
        return carry

    lax.fori_loop(1, plane_size, arrive, 0)
    local.wait()

    def sent(i, carry):
        q = (me_q + i) % plane_size
        plane_copy(q, me_q, me_q).wait_send()
        return carry

    lax.fori_loop(1, plane_size, sent, 0)

    def block_of(k):
        return panel_ref.at[pl.ds(k * block_rows, block_rows)]

    def ring_copy(k, sem, dev):
        return pltpu.make_async_remote_copy(
            block_of(k), block_of(k), sem, recv_ring.at[k],
            device_id=(dev, me_c, me_b), device_id_type=MESH_ID)

    half = ring_size // 2
    half_rows = block_rows // 2

    def part_of(k, first):
        start = k * block_rows + (0 if first else half_rows)
        return panel_ref.at[pl.ds(start, half_rows)]

    def part_copy(k, first, sem, dev):
        slot = k if first else ring_size
        return pltpu.make_async_remote_copy(
            part_of(k, first), part_of(k, first), sem, recv_ring.at[slot],
            device_id=(dev, me_c, me_b), device_id_type=MESH_ID)

    sends = []
    for s in range(half):
        k = (me_z + ring_size - s) % ring_size
        if s > 0:
            ring_copy(k, send_right.at[s], left).wait_recv()
        c = ring_copy(k, send_right.at[s], right) if s < half - 1 else part_copy(
            k, True, send_right.at[s], right)
        c.start()
        sends.append(c)
        k = (me_z + s) % ring_size
        if s > 0:
            ring_copy(k, send_left.at[s], right).wait_recv()
        c = ring_copy(k, send_left.at[s], left) if s < half - 1 else part_copy(
            k, False, send_left.at[s], left)
        c.start()
        sends.append(c)
    far = (me_z + half) % ring_size
    part_copy(far, True, send_right.at[0], left).wait_recv()
    part_copy(far, False, send_left.at[0], right).wait_recv()
    for c in sends:
        c.wait_send()
    meta_local.wait()
    pltpu.make_async_remote_copy(
        meta_ref, chip_meta_ref.at[1 - me_c], meta_sems.at[1], meta_sems.at[2],
        device_id=partner, device_id_type=MESH_ID).wait_recv()
    meta_copy.wait_send()


def spread(pieces, meta, ring_size, plane_size, blk_size):
    _, slots, width = pieces.shape
    rows = ring_size * plane_size * slots
    kernel = functools.partial(spread_kernel, ring_size=ring_size, plane_size=plane_size,
                               blk_size=blk_size, slots=slots)
    half = ring_size // 2
    return pl.pallas_call(
        kernel,
        out_shape=(jax.ShapeDtypeStruct((rows, width), pieces.dtype),
                   jax.ShapeDtypeStruct((2,) + meta.shape, meta.dtype)),
        in_specs=[pl.BlockSpec(memory_space=pl.ANY), pl.BlockSpec(memory_space=pl.ANY)],
        out_specs=(pl.BlockSpec(memory_space=pl.ANY), pl.BlockSpec(memory_space=pl.ANY)),
        scratch_shapes=[
            pltpu.SemaphoreType.DMA((plane_size,)),
            pltpu.SemaphoreType.DMA((plane_size,)),
            pltpu.SemaphoreType.DMA(()),
            pltpu.SemaphoreType.DMA((half,)),
            pltpu.SemaphoreType.DMA((half,)),
            pltpu.SemaphoreType.DMA((ring_size + 1,)),
            pltpu.SemaphoreType.DMA((3,)),
        ],
        compiler_params=pltpu.CompilerParams(collective_id=0, has_side_effects=True),
    )(pieces, meta)


def exchange_kernel(part_ref, out_ref, recv_buf, sems, *, scale):
    me_z = lax.axis_index("z")
    me_c = lax.axis_index("core")
    me_b = lax.axis_index("blk")
    partner = (me_z, 1 - me_c, me_b)
    barrier = pltpu.get_barrier_semaphore()
    pl.semaphore_signal(barrier, 1, device_id=partner, device_id_type=MESH_ID)
    pl.semaphore_wait(barrier, 1)
    copy = pltpu.make_async_remote_copy(
        part_ref.at[1 - me_c], recv_buf, sems.at[0], sems.at[1],
        device_id=partner, device_id_type=MESH_ID)
    copy.start()
    copy.wait()
    out_ref[...] = (part_ref[me_c] + recv_buf[...]) * scale


def exchange(partial, scale):
    shape = partial.shape[1:]
    return pl.pallas_call(
        functools.partial(exchange_kernel, scale=scale),
        out_shape=jax.ShapeDtypeStruct(shape, partial.dtype),
        in_specs=[pl.BlockSpec(memory_space=pltpu.VMEM)],
        out_specs=pl.BlockSpec(memory_space=pltpu.VMEM),
        scratch_shapes=[
            pltpu.VMEM(shape, partial.dtype),
            pltpu.SemaphoreType.DMA((2,)),
        ],
        compiler_params=pltpu.CompilerParams(collective_id=1, has_side_effects=True),
    )(partial)


def shards(spectra, send_rows, send_counts, pair_rows, pair_counts):
    whitened = whiten(spectra)
    station_count, comps, parts, bin_count = whitened.shape
    row_width = comps * parts * bin_count
    slot_count = send_rows.shape[2]
    cores = lax.axis_size("core")
    part_bins = bin_count // cores
    core = lax.axis_index("core")

    flat = whitened.reshape(station_count, row_width)
    lists = send_rows[0]
    col_count = lists.shape[0]
    picked = jnp.take(flat, lists.reshape(-1), axis=0).reshape(col_count, slot_count, row_width)
    alive = jnp.arange(slot_count, dtype=jnp.int32)[None, :] < send_counts[0][:, None]
    picked = jnp.where(alive[:, :, None], picked, jnp.zeros_like(picked))
    pieces = picked.reshape(col_count, slot_count, comps * parts, cores, part_bins)
    pieces = jnp.transpose(pieces, (3, 0, 1, 2, 4)).reshape(
        cores * col_count, slot_count, comps * parts * part_bins)
    pair_total = pair_rows.shape[1]
    meta = jnp.concatenate(
        [pair_rows, jnp.broadcast_to(pair_counts[:, None], (1, pair_total))], axis=0)
    panel, chip_meta = spread(pieces, meta, lax.axis_size("z"), cores * col_count, col_count)
    cos_rows, sin_rows = lag_tables(bin_count)
    chip_counts = jnp.concatenate([chip_meta[:, 2, 0], core.astype(jnp.int32)[None]])
    chip_first = chip_meta[:, 0, :].reshape(cores * pair_total, 1)
    chip_second = chip_meta[:, 1, :].reshape(cores * pair_total, 1)
    partial = pair_sums(chip_counts, chip_first, chip_second,
                        panel, cos_rows, sin_rows, cores, 0, None)
    total = exchange(partial, 1.0 / math.sqrt(bin_count))[:, :LAGS, :]
    live = jnp.arange(pair_total, dtype=jnp.int32) < pair_counts[0]
    total = jnp.where(live[None, None, :], total, 0.0).astype(jnp.bfloat16)
    return jnp.transpose(total, (1, 0, 2))


def solution(mesh):
    tile_size = mesh.shape["tile"]
    blk_size = mesh.shape["blk"]
    split = Mesh(mesh.devices.reshape(tile_size // 2, 2, blk_size), ("z", "core", "blk"))
    dev = ("z", "core", "blk")
    return jax.shard_map(
        shards,
        mesh=split,
        in_specs=(
            P(dev, None, None, None),
            P(dev, None, None),
            P(dev, None),
            P(None, dev),
            P(dev),
        ),
        out_specs=P(None, None, dev),
        check_vma=False,
    )
```

```python
import functools
import math

import jax
import ml_dtypes
import numpy as np
import jax.numpy as jnp
from jax import lax
from jax.experimental import pallas as pl
from jax.experimental.pallas import tpu as pltpu
from jax.sharding import Mesh
from jax.sharding import PartitionSpec as P

LAGS = 129
LAG_ROWS = 144
PAIR_BLOCK = 128
BIN_CHUNK = 256
GATHER_CHUNK = 512
SUBS = 2


def whiten(spectra):
    station_count = spectra.shape[0]
    bin_count = spectra.shape[-1]
    ramp_bins = bin_count // 32
    bin_index = jnp.arange(bin_count, dtype=jnp.int32)
    edge_dist = jnp.minimum(bin_index, bin_count - 1 - bin_index).astype(jnp.float32) + 0.5
    ramp_vals = 0.5 - 0.5 * jnp.cos(jnp.pi * edge_dist / ramp_bins)
    taper = jnp.where(edge_dist < ramp_bins, ramp_vals, jnp.ones_like(ramp_vals))
    blocked = spectra.reshape(station_count, 3, 2, bin_count // 64, 64)
    power = jnp.mean(blocked * blocked, axis=(1, 2, 4))
    inverse = 1.0 / jnp.sqrt(power + 1e-05)
    spread_scale = jnp.repeat(inverse, 64, axis=1)
    return (spectra * taper * spread_scale[:, None, None, :]).astype(jnp.bfloat16)


def lag_tables(bin_count):
    lag_index = np.arange(LAGS, dtype=np.int32) - LAGS // 2
    bin_index = np.arange(bin_count, dtype=np.int32)
    phase_steps = lag_index[:, None] * bin_index[None, :] % (2 * bin_count)
    angle = phase_steps.astype(np.float32) * np.float32(np.pi / bin_count)
    pad = ((0, LAG_ROWS - LAGS), (0, 0))
    cos_rows = np.pad(np.cos(angle).astype(np.float32).astype(ml_dtypes.bfloat16), pad)
    sin_rows = np.pad((-np.sin(angle)).astype(np.float32).astype(ml_dtypes.bfloat16), pad)
    return jnp.asarray(cos_rows), jnp.asarray(sin_rows)


def pair_kernel(counts_ref, first_ref, second_ref, panel_ref, cos_ref, sin_ref, *rest,
                blocks_per_owner, part_bins, accumulate):
    if accumulate:
        acc_ref, out_ref, f_scr, s_scr = rest
    else:
        out_ref, f_scr, s_scr = rest
    step = pl.program_id(0)
    owner = step // blocks_per_owner
    start = (step % blocks_per_owner) * PAIR_BLOCK
    live = start < counts_ref[owner]
    if accumulate:
        out_ref[...] = acc_ref[...]
    else:
        out_ref[...] = jnp.zeros_like(out_ref)

    @pl.when(live)
    def _():
        rows = panel_ref.shape[0]
        width = panel_ref.shape[1]
        iota = lax.broadcasted_iota(jnp.int32, (PAIR_BLOCK, rows), 1)
        pick_first = (first_ref[...] == iota).astype(jnp.bfloat16)
        pick_second = (second_ref[...] == iota).astype(jnp.bfloat16)
        gather_chunk = min(GATHER_CHUNK, width)

        def gather(c, carry):
            off = pl.multiple_of(c * gather_chunk, gather_chunk)
            block = panel_ref[:, pl.ds(off, gather_chunk)]
            f_scr[:, pl.ds(off, gather_chunk)] = jnp.dot(
                pick_first, block, preferred_element_type=jnp.float32)
            s_scr[:, pl.ds(off, gather_chunk)] = jnp.dot(
                pick_second, block, preferred_element_type=jnp.float32)
            return carry

        lax.fori_loop(0, width // gather_chunk, gather, 0)
        nt = (((1,), (1,)), ((), ()))
        sub_bins = part_bins // SUBS
        bin_chunk = min(BIN_CHUNK, sub_bins)
        for sub in range(SUBS):
            col0 = sub * 6 * sub_bins

            def chunk(kc, carry):
                off = pl.multiple_of(kc * bin_chunk, bin_chunk)
                cos_blk = cos_ref[:, pl.ds(sub * sub_bins + off, bin_chunk)]
                sin_blk = sin_ref[:, pl.ds(sub * sub_bins + off, bin_chunk)]
                for a in range(3):
                    f_re = f_scr[:, pl.ds(col0 + 2 * a * sub_bins + off, bin_chunk)]
                    f_im = f_scr[:, pl.ds(col0 + (2 * a + 1) * sub_bins + off, bin_chunk)]
                    for b in range(3):
                        s_re = s_scr[:, pl.ds(col0 + 2 * b * sub_bins + off, bin_chunk)]
                        s_im = s_scr[:, pl.ds(col0 + (2 * b + 1) * sub_bins + off, bin_chunk)]
                        real_part = (f_re * s_re + f_im * s_im).astype(jnp.bfloat16)
                        imag_part = (f_im * s_re - f_re * s_im).astype(jnp.bfloat16)
                        acc = lax.dot_general(cos_blk, real_part, nt,
                                              preferred_element_type=jnp.float32)
                        acc = acc + lax.dot_general(sin_blk, imag_part, nt,
                                                    preferred_element_type=jnp.float32)
                        out_ref[0, 3 * a + b] += acc
                return carry

            lax.fori_loop(0, sub_bins // bin_chunk, chunk, 0)


def pair_sums(counts, first_idx, second_idx, panel, cos_rows, sin_rows, owners, chunk_id, acc):
    rows, width = panel.shape
    part_bins = width // 6
    pairs = first_idx.shape[0]
    per_owner = pairs // owners
    blocks_per_owner = per_owner // PAIR_BLOCK
    grid = (pairs // PAIR_BLOCK,)
    accumulate = acc is not None
    kernel = functools.partial(pair_kernel, blocks_per_owner=blocks_per_owner,
                               part_bins=part_bins, accumulate=accumulate)
    flops = 2 * pairs * rows * width * 2 + 2 * LAG_ROWS * 2 * part_bins * 9 * pairs
    out_bytes = owners * 9 * LAG_ROWS * per_owner * 4
    cost = pl.CostEstimate(flops=flops, transcendentals=0,
                           bytes_accessed=rows * width * 2 + out_bytes * (2 if accumulate else 1))
    out_spec = pl.BlockSpec(
        (1, 9, LAG_ROWS, PAIR_BLOCK),
        lambda i, c: (i // blocks_per_owner, 0, 0, i % blocks_per_owner))
    in_specs = [
        pl.BlockSpec((PAIR_BLOCK, 1), lambda i, c: (i, 0)),
        pl.BlockSpec((PAIR_BLOCK, 1), lambda i, c: (i, 0)),
        pl.BlockSpec((rows, width), lambda i, c: (0, 0)),
        pl.BlockSpec((LAG_ROWS, part_bins), lambda i, c: (0, c[owners])),
        pl.BlockSpec((LAG_ROWS, part_bins), lambda i, c: (0, c[owners])),
    ]
    args = [counts, first_idx, second_idx, panel, cos_rows, sin_rows]
    aliases = {}
    if accumulate:
        in_specs.append(out_spec)
        args.append(acc)
        aliases = {len(args) - 1: 0}
    return pl.pallas_call(
        kernel,
        out_shape=jax.ShapeDtypeStruct((owners, 9, LAG_ROWS, per_owner), jnp.float32),
        grid_spec=pltpu.PrefetchScalarGridSpec(
            num_scalar_prefetch=1,
            grid=grid,
            in_specs=in_specs,
            out_specs=out_spec,
            scratch_shapes=[
                pltpu.VMEM((PAIR_BLOCK, width), jnp.float32),
                pltpu.VMEM((PAIR_BLOCK, width), jnp.float32),
            ],
        ),
        input_output_aliases=aliases,
        compiler_params=pltpu.CompilerParams(
            dimension_semantics=("arbitrary",), vmem_limit_bytes=60 * 1024 * 1024),
        cost_estimate=cost,
    )(*args)


MESH_ID = pl.DeviceIdType.MESH


def spread_kernel(pieces_ref, meta_ref, panel_ref, chip_meta_ref, send_plane, recv_plane,
                  local_sem, send_right, send_left, recv_ring, meta_sems, *, ring_size,
                  plane_size, blk_size, slots, subs):
    me_z = lax.axis_index("z")
    me_c = lax.axis_index("core")
    me_b = lax.axis_index("blk")
    me_q = me_c * blk_size + me_b
    right = (me_z + 1) % ring_size
    left = (me_z + ring_size - 1) % ring_size

    def plane_dev(q):
        return (me_z, q // blk_size, q % blk_size)

    barrier = pltpu.get_barrier_semaphore()

    def greet(i, carry):
        q = (me_q + i) % plane_size
        pl.semaphore_signal(barrier, 1, device_id=plane_dev(q), device_id_type=MESH_ID)
        return carry

    lax.fori_loop(1, plane_size, greet, 0)
    pl.semaphore_signal(barrier, 1, device_id=(right, me_c, me_b), device_id_type=MESH_ID)
    pl.semaphore_signal(barrier, 1, device_id=(left, me_c, me_b), device_id_type=MESH_ID)
    pl.semaphore_wait(barrier, plane_size + 1)

    partner = (me_z, 1 - me_c, me_b)
    meta_local = pltpu.make_async_copy(meta_ref, chip_meta_ref.at[me_c], meta_sems.at[0])
    meta_local.start()
    meta_copy = pltpu.make_async_remote_copy(
        meta_ref, chip_meta_ref.at[me_c], meta_sems.at[1], meta_sems.at[2],
        device_id=partner, device_id_type=MESH_ID)
    meta_copy.start()

    sub_width = panel_ref.shape[1] // subs
    block_rows = plane_size * slots
    half_rows = block_rows // 2
    base = me_z * block_rows
    half = ring_size // 2

    def cols(sub):
        return pl.ds(sub * sub_width, sub_width)

    def rows_of(q, sub):
        return panel_ref.at[pl.ds(base + q * slots, slots), cols(sub)]

    def local_copy(sub):
        return pltpu.make_async_copy(
            pieces_ref.at[me_q, :, cols(sub)], rows_of(me_q, sub), local_sem.at[sub])

    def plane_copy(q, src_q, sub):
        return pltpu.make_async_remote_copy(
            pieces_ref.at[q, :, cols(sub)], rows_of(src_q, sub), send_plane.at[sub, q],
            recv_plane.at[sub, src_q], device_id=plane_dev(q), device_id_type=MESH_ID)

    def scatter(sub):
        local_copy(sub).start()

        def send(i, carry):
            q = (me_q + i) % plane_size
            plane_copy(q, me_q, sub).start()
            return carry

        lax.fori_loop(1, plane_size, send, 0)

    def gathered(sub):
        def arrive(i, carry):
            q = (me_q + plane_size - i) % plane_size
            plane_copy(q, q, sub).wait_recv()
            return carry

        lax.fori_loop(1, plane_size, arrive, 0)
        local_copy(sub).wait()

    def block_of(k, sub):
        return panel_ref.at[pl.ds(k * block_rows, block_rows), cols(sub)]

    def part_of(k, first, sub):
        start = k * block_rows + (0 if first else half_rows)
        return panel_ref.at[pl.ds(start, half_rows), cols(sub)]

    def ring_copy(k, sem, dev, sub):
        return pltpu.make_async_remote_copy(
            block_of(k, sub), block_of(k, sub), sem, recv_ring.at[sub, k],
            device_id=(dev, me_c, me_b), device_id_type=MESH_ID)

    def part_copy(k, first, sem, dev, sub):
        slot = k if first else ring_size
        return pltpu.make_async_remote_copy(
            part_of(k, first, sub), part_of(k, first, sub), sem, recv_ring.at[sub, slot],
            device_id=(dev, me_c, me_b), device_id_type=MESH_ID)

    sends = []

    def ring_step(s, sub):
        k = (me_z + ring_size - s) % ring_size
        if s > 0:
            ring_copy(k, send_right.at[sub, s], left, sub).wait_recv()
        c = ring_copy(k, send_right.at[sub, s], right, sub) if s < half - 1 else part_copy(
            k, True, send_right.at[sub, s], right, sub)
        c.start()
        sends.append(c)
        k = (me_z + s) % ring_size
        if s > 0:
            ring_copy(k, send_left.at[sub, s], right, sub).wait_recv()
        c = ring_copy(k, send_left.at[sub, s], left, sub) if s < half - 1 else part_copy(
            k, False, send_left.at[sub, s], left, sub)
        c.start()
        sends.append(c)

    for sub in range(subs):
        scatter(sub)
        gathered(sub)
        ring_step(0, sub)
    for s in range(1, half):
        for sub in range(subs):
            ring_step(s, sub)
    far = (me_z + half) % ring_size
    for sub in range(subs):
        part_copy(far, True, send_right.at[sub, 0], left, sub).wait_recv()
        part_copy(far, False, send_left.at[sub, 0], right, sub).wait_recv()
    for sub in range(subs):
        def sent(i, carry):
            q = (me_q + i) % plane_size
            plane_copy(q, me_q, sub).wait_send()
            return carry

        lax.fori_loop(1, plane_size, sent, 0)
    for c in sends:
        c.wait_send()
    meta_local.wait()
    pltpu.make_async_remote_copy(
        meta_ref, chip_meta_ref.at[1 - me_c], meta_sems.at[1], meta_sems.at[2],
        device_id=partner, device_id_type=MESH_ID).wait_recv()
    meta_copy.wait_send()


def spread(pieces, meta, ring_size, plane_size, blk_size):
    _, slots, width = pieces.shape
    rows = ring_size * plane_size * slots
    kernel = functools.partial(spread_kernel, ring_size=ring_size, plane_size=plane_size,
                               blk_size=blk_size, slots=slots, subs=SUBS)
    half = ring_size // 2
    return pl.pallas_call(
        kernel,
        out_shape=(jax.ShapeDtypeStruct((rows, width), pieces.dtype),
                   jax.ShapeDtypeStruct((2,) + meta.shape, meta.dtype)),
        in_specs=[pl.BlockSpec(memory_space=pl.ANY), pl.BlockSpec(memory_space=pl.ANY)],
        out_specs=(pl.BlockSpec(memory_space=pl.ANY), pl.BlockSpec(memory_space=pl.ANY)),
        scratch_shapes=[
            pltpu.SemaphoreType.DMA((SUBS, plane_size)),
            pltpu.SemaphoreType.DMA((SUBS, plane_size)),
            pltpu.SemaphoreType.DMA((SUBS,)),
            pltpu.SemaphoreType.DMA((SUBS, half)),
            pltpu.SemaphoreType.DMA((SUBS, half)),
            pltpu.SemaphoreType.DMA((SUBS, ring_size + 1)),
            pltpu.SemaphoreType.DMA((3,)),
        ],
        compiler_params=pltpu.CompilerParams(collective_id=0, has_side_effects=True),
    )(pieces, meta)


def exchange_kernel(part_ref, out_ref, recv_buf, sems, *, scale):
    me_z = lax.axis_index("z")
    me_c = lax.axis_index("core")
    me_b = lax.axis_index("blk")
    partner = (me_z, 1 - me_c, me_b)
    barrier = pltpu.get_barrier_semaphore()
    pl.semaphore_signal(barrier, 1, device_id=partner, device_id_type=MESH_ID)
    pl.semaphore_wait(barrier, 1)
    copy = pltpu.make_async_remote_copy(
        part_ref.at[1 - me_c], recv_buf, sems.at[0], sems.at[1],
        device_id=partner, device_id_type=MESH_ID)
    copy.start()
    copy.wait()
    out_ref[...] = (part_ref[me_c] + recv_buf[...]) * scale


def exchange(partial, scale):
    shape = partial.shape[1:]
    return pl.pallas_call(
        functools.partial(exchange_kernel, scale=scale),
        out_shape=jax.ShapeDtypeStruct(shape, partial.dtype),
        in_specs=[pl.BlockSpec(memory_space=pltpu.VMEM)],
        out_specs=pl.BlockSpec(memory_space=pltpu.VMEM),
        scratch_shapes=[
            pltpu.VMEM(shape, partial.dtype),
            pltpu.SemaphoreType.DMA((2,)),
        ],
        compiler_params=pltpu.CompilerParams(collective_id=1, has_side_effects=True),
    )(partial)


def shards(spectra, send_rows, send_counts, pair_rows, pair_counts):
    whitened = whiten(spectra)
    station_count, comps, parts, bin_count = whitened.shape
    row_width = comps * parts * bin_count
    slot_count = send_rows.shape[2]
    cores = lax.axis_size("core")
    part_bins = bin_count // cores
    core = lax.axis_index("core")

    flat = whitened.reshape(station_count, row_width)
    lists = send_rows[0]
    col_count = lists.shape[0]
    picked = jnp.take(flat, lists.reshape(-1), axis=0).reshape(col_count, slot_count, row_width)
    alive = jnp.arange(slot_count, dtype=jnp.int32)[None, :] < send_counts[0][:, None]
    picked = jnp.where(alive[:, :, None], picked, jnp.zeros_like(picked))
    pieces = picked.reshape(col_count, slot_count, comps * parts, cores, SUBS,
                            part_bins // SUBS)
    pieces = jnp.transpose(pieces, (3, 0, 1, 4, 2, 5)).reshape(
        cores * col_count, slot_count, comps * parts * part_bins)
    pair_total = pair_rows.shape[1]
    meta = jnp.concatenate(
        [pair_rows, jnp.broadcast_to(pair_counts[:, None], (1, pair_total))], axis=0)
    panel, chip_meta = spread(pieces, meta, lax.axis_size("z"), cores * col_count, col_count)
    cos_rows, sin_rows = lag_tables(bin_count)
    chip_counts = jnp.concatenate([chip_meta[:, 2, 0], core.astype(jnp.int32)[None]])
    chip_first = chip_meta[:, 0, :].reshape(cores * pair_total, 1)
    chip_second = chip_meta[:, 1, :].reshape(cores * pair_total, 1)
    partial = pair_sums(chip_counts, chip_first, chip_second,
                        panel, cos_rows, sin_rows, cores, 0, None)
    total = exchange(partial, 1.0 / math.sqrt(bin_count))[:, :LAGS, :]
    live = jnp.arange(pair_total, dtype=jnp.int32) < pair_counts[0]
    total = jnp.where(live[None, None, :], total, 0.0).astype(jnp.bfloat16)
    return jnp.transpose(total, (1, 0, 2))


def solution(mesh):
    tile_size = mesh.shape["tile"]
    blk_size = mesh.shape["blk"]
    split = Mesh(mesh.devices.reshape(tile_size // 2, 2, blk_size), ("z", "core", "blk"))
    dev = ("z", "core", "blk")
    return jax.shard_map(
        shards,
        mesh=split,
        in_specs=(
            P(dev, None, None, None),
            P(dev, None, None),
            P(dev, None),
            P(None, dev),
            P(dev),
        ),
        out_specs=P(None, None, dev),
        check_vma=False,
    )
```

```python
import functools
import math

import jax
import ml_dtypes
import numpy as np
import jax.numpy as jnp
from jax import lax
from jax.experimental import pallas as pl
from jax.experimental.pallas import tpu as pltpu
from jax.sharding import Mesh
from jax.sharding import PartitionSpec as P

LAGS = 129
LAG_ROWS = 144
PAIR_BLOCK = 128
BIN_CHUNK = 256
GATHER_CHUNK = 512
SUBS = 4


def whiten(spectra):
    station_count = spectra.shape[0]
    bin_count = spectra.shape[-1]
    ramp_bins = bin_count // 32
    bin_index = jnp.arange(bin_count, dtype=jnp.int32)
    edge_dist = jnp.minimum(bin_index, bin_count - 1 - bin_index).astype(jnp.float32) + 0.5
    ramp_vals = 0.5 - 0.5 * jnp.cos(jnp.pi * edge_dist / ramp_bins)
    taper = jnp.where(edge_dist < ramp_bins, ramp_vals, jnp.ones_like(ramp_vals))
    blocked = spectra.reshape(station_count, 3, 2, bin_count // 64, 64)
    power = jnp.mean(blocked * blocked, axis=(1, 2, 4))
    inverse = 1.0 / jnp.sqrt(power + 1e-05)
    spread_scale = jnp.repeat(inverse, 64, axis=1)
    return (spectra * taper * spread_scale[:, None, None, :]).astype(jnp.bfloat16)


def lag_tables(bin_count):
    lag_index = np.arange(LAGS, dtype=np.int32) - LAGS // 2
    bin_index = np.arange(bin_count, dtype=np.int32)
    phase_steps = lag_index[:, None] * bin_index[None, :] % (2 * bin_count)
    angle = phase_steps.astype(np.float32) * np.float32(np.pi / bin_count)
    pad = ((0, LAG_ROWS - LAGS), (0, 0))
    cos_rows = np.pad(np.cos(angle).astype(np.float32).astype(ml_dtypes.bfloat16), pad)
    sin_rows = np.pad((-np.sin(angle)).astype(np.float32).astype(ml_dtypes.bfloat16), pad)
    return jnp.asarray(cos_rows), jnp.asarray(sin_rows)


def pair_kernel(counts_ref, first_ref, second_ref, panel_ref, cos_ref, sin_ref, *rest,
                blocks_per_owner, part_bins, accumulate):
    if accumulate:
        acc_ref, out_ref, f_scr, s_scr = rest
    else:
        out_ref, f_scr, s_scr = rest
    step = pl.program_id(0)
    owner = step // blocks_per_owner
    start = (step % blocks_per_owner) * PAIR_BLOCK
    live = start < counts_ref[owner]
    if accumulate:
        out_ref[...] = acc_ref[...]
    else:
        out_ref[...] = jnp.zeros_like(out_ref)

    @pl.when(live)
    def _():
        rows = panel_ref.shape[0]
        width = panel_ref.shape[1]
        iota = lax.broadcasted_iota(jnp.int32, (PAIR_BLOCK, rows), 1)
        pick_first = (first_ref[...] == iota).astype(jnp.bfloat16)
        pick_second = (second_ref[...] == iota).astype(jnp.bfloat16)
        gather_chunk = min(GATHER_CHUNK, width)

        def gather(c, carry):
            off = pl.multiple_of(c * gather_chunk, gather_chunk)
            block = panel_ref[:, pl.ds(off, gather_chunk)]
            f_scr[:, pl.ds(off, gather_chunk)] = jnp.dot(
                pick_first, block, preferred_element_type=jnp.float32)
            s_scr[:, pl.ds(off, gather_chunk)] = jnp.dot(
                pick_second, block, preferred_element_type=jnp.float32)
            return carry

        lax.fori_loop(0, width // gather_chunk, gather, 0)
        nt = (((1,), (1,)), ((), ()))
        sub_bins = part_bins // SUBS
        bin_chunk = min(BIN_CHUNK, sub_bins)
        for sub in range(SUBS):
            col0 = sub * 6 * sub_bins

            def chunk(kc, carry):
                off = pl.multiple_of(kc * bin_chunk, bin_chunk)
                cos_blk = cos_ref[:, pl.ds(sub * sub_bins + off, bin_chunk)]
                sin_blk = sin_ref[:, pl.ds(sub * sub_bins + off, bin_chunk)]
                for a in range(3):
                    f_re = f_scr[:, pl.ds(col0 + 2 * a * sub_bins + off, bin_chunk)]
                    f_im = f_scr[:, pl.ds(col0 + (2 * a + 1) * sub_bins + off, bin_chunk)]
                    for b in range(3):
                        s_re = s_scr[:, pl.ds(col0 + 2 * b * sub_bins + off, bin_chunk)]
                        s_im = s_scr[:, pl.ds(col0 + (2 * b + 1) * sub_bins + off, bin_chunk)]
                        real_part = (f_re * s_re + f_im * s_im).astype(jnp.bfloat16)
                        imag_part = (f_im * s_re - f_re * s_im).astype(jnp.bfloat16)
                        acc = lax.dot_general(cos_blk, real_part, nt,
                                              preferred_element_type=jnp.float32)
                        acc = acc + lax.dot_general(sin_blk, imag_part, nt,
                                                    preferred_element_type=jnp.float32)
                        out_ref[0, 3 * a + b] += acc
                return carry

            lax.fori_loop(0, sub_bins // bin_chunk, chunk, 0)


def pair_sums(counts, first_idx, second_idx, panel, cos_rows, sin_rows, owners, chunk_id, acc):
    rows, width = panel.shape
    part_bins = width // 6
    pairs = first_idx.shape[0]
    per_owner = pairs // owners
    blocks_per_owner = per_owner // PAIR_BLOCK
    grid = (pairs // PAIR_BLOCK,)
    accumulate = acc is not None
    kernel = functools.partial(pair_kernel, blocks_per_owner=blocks_per_owner,
                               part_bins=part_bins, accumulate=accumulate)
    flops = 2 * pairs * rows * width * 2 + 2 * LAG_ROWS * 2 * part_bins * 9 * pairs
    out_bytes = owners * 9 * LAG_ROWS * per_owner * 4
    cost = pl.CostEstimate(flops=flops, transcendentals=0,
                           bytes_accessed=rows * width * 2 + out_bytes * (2 if accumulate else 1))
    out_spec = pl.BlockSpec(
        (1, 9, LAG_ROWS, PAIR_BLOCK),
        lambda i, c: (i // blocks_per_owner, 0, 0, i % blocks_per_owner))
    in_specs = [
        pl.BlockSpec((PAIR_BLOCK, 1), lambda i, c: (i, 0)),
        pl.BlockSpec((PAIR_BLOCK, 1), lambda i, c: (i, 0)),
        pl.BlockSpec((rows, width), lambda i, c: (0, 0)),
        pl.BlockSpec((LAG_ROWS, part_bins), lambda i, c: (0, c[owners])),
        pl.BlockSpec((LAG_ROWS, part_bins), lambda i, c: (0, c[owners])),
    ]
    args = [counts, first_idx, second_idx, panel, cos_rows, sin_rows]
    aliases = {}
    if accumulate:
        in_specs.append(out_spec)
        args.append(acc)
        aliases = {len(args) - 1: 0}
    return pl.pallas_call(
        kernel,
        out_shape=jax.ShapeDtypeStruct((owners, 9, LAG_ROWS, per_owner), jnp.float32),
        grid_spec=pltpu.PrefetchScalarGridSpec(
            num_scalar_prefetch=1,
            grid=grid,
            in_specs=in_specs,
            out_specs=out_spec,
            scratch_shapes=[
                pltpu.VMEM((PAIR_BLOCK, width), jnp.float32),
                pltpu.VMEM((PAIR_BLOCK, width), jnp.float32),
            ],
        ),
        input_output_aliases=aliases,
        compiler_params=pltpu.CompilerParams(
            dimension_semantics=("arbitrary",), vmem_limit_bytes=60 * 1024 * 1024),
        cost_estimate=cost,
    )(*args)


MESH_ID = pl.DeviceIdType.MESH


def spread_kernel(pieces_ref, meta_ref, panel_ref, chip_meta_ref, send_plane, recv_plane,
                  local_sem, send_right, send_left, recv_ring, meta_sems, *, ring_size,
                  plane_size, blk_size, slots, subs):
    me_z = lax.axis_index("z")
    me_c = lax.axis_index("core")
    me_b = lax.axis_index("blk")
    me_q = me_c * blk_size + me_b
    right = (me_z + 1) % ring_size
    left = (me_z + ring_size - 1) % ring_size

    def plane_dev(q):
        return (me_z, q // blk_size, q % blk_size)

    barrier = pltpu.get_barrier_semaphore()

    def greet(i, carry):
        q = (me_q + i) % plane_size
        pl.semaphore_signal(barrier, 1, device_id=plane_dev(q), device_id_type=MESH_ID)
        return carry

    lax.fori_loop(1, plane_size, greet, 0)
    pl.semaphore_signal(barrier, 1, device_id=(right, me_c, me_b), device_id_type=MESH_ID)
    pl.semaphore_signal(barrier, 1, device_id=(left, me_c, me_b), device_id_type=MESH_ID)
    pl.semaphore_wait(barrier, plane_size + 1)

    partner = (me_z, 1 - me_c, me_b)
    meta_local = pltpu.make_async_copy(meta_ref, chip_meta_ref.at[me_c], meta_sems.at[0])
    meta_local.start()
    meta_copy = pltpu.make_async_remote_copy(
        meta_ref, chip_meta_ref.at[me_c], meta_sems.at[1], meta_sems.at[2],
        device_id=partner, device_id_type=MESH_ID)
    meta_copy.start()

    sub_width = panel_ref.shape[1] // subs
    block_rows = plane_size * slots
    half_rows = block_rows // 2
    base = me_z * block_rows
    half = ring_size // 2

    def cols(sub):
        return pl.ds(sub * sub_width, sub_width)

    def rows_of(q, sub):
        return panel_ref.at[pl.ds(base + q * slots, slots), cols(sub)]

    def local_copy(sub):
        return pltpu.make_async_copy(
            pieces_ref.at[me_q, :, cols(sub)], rows_of(me_q, sub), local_sem.at[sub])

    def plane_copy(q, src_q, sub):
        return pltpu.make_async_remote_copy(
            pieces_ref.at[q, :, cols(sub)], rows_of(src_q, sub), send_plane.at[sub, q],
            recv_plane.at[sub, src_q], device_id=plane_dev(q), device_id_type=MESH_ID)

    def scatter(sub):
        local_copy(sub).start()

        def send(i, carry):
            q = (me_q + i) % plane_size
            plane_copy(q, me_q, sub).start()
            return carry

        lax.fori_loop(1, plane_size, send, 0)

    def gathered(sub):
        def arrive(i, carry):
            q = (me_q + plane_size - i) % plane_size
            plane_copy(q, q, sub).wait_recv()
            return carry

        lax.fori_loop(1, plane_size, arrive, 0)
        local_copy(sub).wait()

    def block_of(k, sub):
        return panel_ref.at[pl.ds(k * block_rows, block_rows), cols(sub)]

    def part_of(k, first, sub):
        start = k * block_rows + (0 if first else half_rows)
        return panel_ref.at[pl.ds(start, half_rows), cols(sub)]

    def ring_copy(k, sem, dev, sub):
        return pltpu.make_async_remote_copy(
            block_of(k, sub), block_of(k, sub), sem, recv_ring.at[sub, k],
            device_id=(dev, me_c, me_b), device_id_type=MESH_ID)

    def part_copy(k, first, sem, dev, sub):
        slot = k if first else ring_size
        return pltpu.make_async_remote_copy(
            part_of(k, first, sub), part_of(k, first, sub), sem, recv_ring.at[sub, slot],
            device_id=(dev, me_c, me_b), device_id_type=MESH_ID)

    sends = []

    def ring_step(s, sub):
        k = (me_z + ring_size - s) % ring_size
        if s > 0:
            ring_copy(k, send_right.at[sub, s], left, sub).wait_recv()
        c = ring_copy(k, send_right.at[sub, s], right, sub) if s < half - 1 else part_copy(
            k, True, send_right.at[sub, s], right, sub)
        c.start()
        sends.append(c)
        k = (me_z + s) % ring_size
        if s > 0:
            ring_copy(k, send_left.at[sub, s], right, sub).wait_recv()
        c = ring_copy(k, send_left.at[sub, s], left, sub) if s < half - 1 else part_copy(
            k, False, send_left.at[sub, s], left, sub)
        c.start()
        sends.append(c)

    for sub in range(subs):
        scatter(sub)
        gathered(sub)
        ring_step(0, sub)
    for s in range(1, half):
        for sub in range(subs):
            ring_step(s, sub)
    far = (me_z + half) % ring_size
    for sub in range(subs):
        part_copy(far, True, send_right.at[sub, 0], left, sub).wait_recv()
        part_copy(far, False, send_left.at[sub, 0], right, sub).wait_recv()
    for sub in range(subs):
        def sent(i, carry):
            q = (me_q + i) % plane_size
            plane_copy(q, me_q, sub).wait_send()
            return carry

        lax.fori_loop(1, plane_size, sent, 0)
    for c in sends:
        c.wait_send()
    meta_local.wait()
    pltpu.make_async_remote_copy(
        meta_ref, chip_meta_ref.at[1 - me_c], meta_sems.at[1], meta_sems.at[2],
        device_id=partner, device_id_type=MESH_ID).wait_recv()
    meta_copy.wait_send()


def spread(pieces, meta, ring_size, plane_size, blk_size):
    _, slots, width = pieces.shape
    rows = ring_size * plane_size * slots
    kernel = functools.partial(spread_kernel, ring_size=ring_size, plane_size=plane_size,
                               blk_size=blk_size, slots=slots, subs=SUBS)
    half = ring_size // 2
    return pl.pallas_call(
        kernel,
        out_shape=(jax.ShapeDtypeStruct((rows, width), pieces.dtype),
                   jax.ShapeDtypeStruct((2,) + meta.shape, meta.dtype)),
        in_specs=[pl.BlockSpec(memory_space=pl.ANY), pl.BlockSpec(memory_space=pl.ANY)],
        out_specs=(pl.BlockSpec(memory_space=pl.ANY), pl.BlockSpec(memory_space=pl.ANY)),
        scratch_shapes=[
            pltpu.SemaphoreType.DMA((SUBS, plane_size)),
            pltpu.SemaphoreType.DMA((SUBS, plane_size)),
            pltpu.SemaphoreType.DMA((SUBS,)),
            pltpu.SemaphoreType.DMA((SUBS, half)),
            pltpu.SemaphoreType.DMA((SUBS, half)),
            pltpu.SemaphoreType.DMA((SUBS, ring_size + 1)),
            pltpu.SemaphoreType.DMA((3,)),
        ],
        compiler_params=pltpu.CompilerParams(collective_id=0, has_side_effects=True),
    )(pieces, meta)


def exchange_kernel(part_ref, out_ref, recv_buf, sems, *, scale):
    me_z = lax.axis_index("z")
    me_c = lax.axis_index("core")
    me_b = lax.axis_index("blk")
    partner = (me_z, 1 - me_c, me_b)
    barrier = pltpu.get_barrier_semaphore()
    pl.semaphore_signal(barrier, 1, device_id=partner, device_id_type=MESH_ID)
    pl.semaphore_wait(barrier, 1)
    copy = pltpu.make_async_remote_copy(
        part_ref.at[1 - me_c], recv_buf, sems.at[0], sems.at[1],
        device_id=partner, device_id_type=MESH_ID)
    copy.start()
    copy.wait()
    out_ref[...] = (part_ref[me_c] + recv_buf[...]) * scale


def exchange(partial, scale):
    shape = partial.shape[1:]
    return pl.pallas_call(
        functools.partial(exchange_kernel, scale=scale),
        out_shape=jax.ShapeDtypeStruct(shape, partial.dtype),
        in_specs=[pl.BlockSpec(memory_space=pltpu.VMEM)],
        out_specs=pl.BlockSpec(memory_space=pltpu.VMEM),
        scratch_shapes=[
            pltpu.VMEM(shape, partial.dtype),
            pltpu.SemaphoreType.DMA((2,)),
        ],
        compiler_params=pltpu.CompilerParams(collective_id=1, has_side_effects=True),
    )(partial)


def shards(spectra, send_rows, send_counts, pair_rows, pair_counts):
    whitened = whiten(spectra)
    station_count, comps, parts, bin_count = whitened.shape
    row_width = comps * parts * bin_count
    slot_count = send_rows.shape[2]
    cores = lax.axis_size("core")
    part_bins = bin_count // cores
    core = lax.axis_index("core")

    flat = whitened.reshape(station_count, row_width)
    lists = send_rows[0]
    col_count = lists.shape[0]
    picked = jnp.take(flat, lists.reshape(-1), axis=0).reshape(col_count, slot_count, row_width)
    alive = jnp.arange(slot_count, dtype=jnp.int32)[None, :] < send_counts[0][:, None]
    picked = jnp.where(alive[:, :, None], picked, jnp.zeros_like(picked))
    pieces = picked.reshape(col_count, slot_count, comps * parts, cores, SUBS,
                            part_bins // SUBS)
    pieces = jnp.transpose(pieces, (3, 0, 1, 4, 2, 5)).reshape(
        cores * col_count, slot_count, comps * parts * part_bins)
    pair_total = pair_rows.shape[1]
    meta = jnp.concatenate(
        [pair_rows, jnp.broadcast_to(pair_counts[:, None], (1, pair_total))], axis=0)
    panel, chip_meta = spread(pieces, meta, lax.axis_size("z"), cores * col_count, col_count)
    cos_rows, sin_rows = lag_tables(bin_count)
    chip_counts = jnp.concatenate([chip_meta[:, 2, 0], core.astype(jnp.int32)[None]])
    chip_first = chip_meta[:, 0, :].reshape(cores * pair_total, 1)
    chip_second = chip_meta[:, 1, :].reshape(cores * pair_total, 1)
    partial = pair_sums(chip_counts, chip_first, chip_second,
                        panel, cos_rows, sin_rows, cores, 0, None)
    total = exchange(partial, 1.0 / math.sqrt(bin_count))[:, :LAGS, :]
    live = jnp.arange(pair_total, dtype=jnp.int32) < pair_counts[0]
    total = jnp.where(live[None, None, :], total, 0.0).astype(jnp.bfloat16)
    return jnp.transpose(total, (1, 0, 2))


def solution(mesh):
    tile_size = mesh.shape["tile"]
    blk_size = mesh.shape["blk"]
    split = Mesh(mesh.devices.reshape(tile_size // 2, 2, blk_size), ("z", "core", "blk"))
    dev = ("z", "core", "blk")
    return jax.shard_map(
        shards,
        mesh=split,
        in_specs=(
            P(dev, None, None, None),
            P(dev, None, None),
            P(dev, None),
            P(None, dev),
            P(dev),
        ),
        out_specs=P(None, None, dev),
        check_vma=False,
    )
```

```python
import functools
import math

import jax
import ml_dtypes
import numpy as np
import jax.numpy as jnp
from jax import lax
from jax.experimental import pallas as pl
from jax.experimental.pallas import tpu as pltpu
from jax.sharding import Mesh
from jax.sharding import PartitionSpec as P

LAGS = 129
LAG_ROWS = 144
PAIR_BLOCK = 128
BIN_CHUNK = 256
GATHER_CHUNK = 512
SUBS = 2


def whiten(spectra):
    station_count = spectra.shape[0]
    bin_count = spectra.shape[-1]
    ramp_bins = bin_count // 32
    bin_index = jnp.arange(bin_count, dtype=jnp.int32)
    edge_dist = jnp.minimum(bin_index, bin_count - 1 - bin_index).astype(jnp.float32) + 0.5
    ramp_vals = 0.5 - 0.5 * jnp.cos(jnp.pi * edge_dist / ramp_bins)
    taper = jnp.where(edge_dist < ramp_bins, ramp_vals, jnp.ones_like(ramp_vals))
    blocked = spectra.reshape(station_count, 3, 2, bin_count // 64, 64)
    power = jnp.mean(blocked * blocked, axis=(1, 2, 4))
    inverse = 1.0 / jnp.sqrt(power + 1e-05)
    spread_scale = jnp.repeat(inverse, 64, axis=1)
    return (spectra * taper * spread_scale[:, None, None, :]).astype(jnp.bfloat16)


def lag_tables(bin_count):
    lag_index = np.arange(LAGS, dtype=np.int32) - LAGS // 2
    bin_index = np.arange(bin_count, dtype=np.int32)
    phase_steps = lag_index[:, None] * bin_index[None, :] % (2 * bin_count)
    angle = phase_steps.astype(np.float32) * np.float32(np.pi / bin_count)
    pad = ((0, LAG_ROWS - LAGS), (0, 0))
    cos_rows = np.pad(np.cos(angle).astype(np.float32).astype(ml_dtypes.bfloat16), pad)
    sin_rows = np.pad((-np.sin(angle)).astype(np.float32).astype(ml_dtypes.bfloat16), pad)
    return jnp.asarray(cos_rows), jnp.asarray(sin_rows)


def pair_kernel(counts_ref, core_ref, pairs_ref, panel_ref, cos_ref, sin_ref, *rest,
                blocks_per_owner, part_bins, accumulate):
    if accumulate:
        acc_ref, out_ref, f_scr, s_scr = rest
    else:
        out_ref, f_scr, s_scr = rest
    step = pl.program_id(0)
    owner = step // blocks_per_owner
    start = (step % blocks_per_owner) * PAIR_BLOCK
    live = start < counts_ref[owner, 0]
    if accumulate:
        out_ref[...] = acc_ref[...]
    else:
        out_ref[...] = jnp.zeros_like(out_ref)

    @pl.when(live)
    def _():
        rows = panel_ref.shape[0]
        width = panel_ref.shape[1]
        iota = lax.broadcasted_iota(jnp.int32, (rows, PAIR_BLOCK), 0)
        idx = pairs_ref[0]
        pick_first = jnp.where(idx[0:1, :] == iota, 1.0, 0.0).T.astype(jnp.bfloat16)
        pick_second = jnp.where(idx[1:2, :] == iota, 1.0, 0.0).T.astype(jnp.bfloat16)
        gather_chunk = min(GATHER_CHUNK, width)

        def gather(c, carry):
            off = pl.multiple_of(c * gather_chunk, gather_chunk)
            block = panel_ref[:, pl.ds(off, gather_chunk)]
            f_scr[:, pl.ds(off, gather_chunk)] = jnp.dot(
                pick_first, block, preferred_element_type=jnp.float32)
            s_scr[:, pl.ds(off, gather_chunk)] = jnp.dot(
                pick_second, block, preferred_element_type=jnp.float32)
            return carry

        lax.fori_loop(0, width // gather_chunk, gather, 0)
        nt = (((1,), (1,)), ((), ()))
        sub_bins = part_bins // SUBS
        bin_chunk = min(BIN_CHUNK, sub_bins)
        for sub in range(SUBS):
            col0 = sub * 6 * sub_bins

            def chunk(kc, carry):
                off = pl.multiple_of(kc * bin_chunk, bin_chunk)
                cos_blk = cos_ref[:, pl.ds(sub * sub_bins + off, bin_chunk)]
                sin_blk = sin_ref[:, pl.ds(sub * sub_bins + off, bin_chunk)]
                for a in range(3):
                    f_re = f_scr[:, pl.ds(col0 + 2 * a * sub_bins + off, bin_chunk)]
                    f_im = f_scr[:, pl.ds(col0 + (2 * a + 1) * sub_bins + off, bin_chunk)]
                    for b in range(3):
                        s_re = s_scr[:, pl.ds(col0 + 2 * b * sub_bins + off, bin_chunk)]
                        s_im = s_scr[:, pl.ds(col0 + (2 * b + 1) * sub_bins + off, bin_chunk)]
                        real_part = (f_re * s_re + f_im * s_im).astype(jnp.bfloat16)
                        imag_part = (f_im * s_re - f_re * s_im).astype(jnp.bfloat16)
                        acc = lax.dot_general(cos_blk, real_part, nt,
                                              preferred_element_type=jnp.float32)
                        acc = acc + lax.dot_general(sin_blk, imag_part, nt,
                                                    preferred_element_type=jnp.float32)
                        out_ref[0, 3 * a + b] += acc
                return carry

            lax.fori_loop(0, sub_bins // bin_chunk, chunk, 0)


def pair_sums(counts, core_arr, chip_pairs, panel, cos_rows, sin_rows, owners, chunk_id, acc):
    rows, width = panel.shape
    part_bins = width // 6
    pairs = chip_pairs.shape[0] * chip_pairs.shape[2]
    per_owner = pairs // owners
    blocks_per_owner = per_owner // PAIR_BLOCK
    grid = (pairs // PAIR_BLOCK,)
    accumulate = acc is not None
    kernel = functools.partial(pair_kernel, blocks_per_owner=blocks_per_owner,
                               part_bins=part_bins, accumulate=accumulate)
    flops = 2 * pairs * rows * width * 2 + 2 * LAG_ROWS * 2 * part_bins * 9 * pairs
    out_bytes = owners * 9 * LAG_ROWS * per_owner * 4
    cost = pl.CostEstimate(flops=flops, transcendentals=0,
                           bytes_accessed=rows * width * 2 + out_bytes * (2 if accumulate else 1))
    out_spec = pl.BlockSpec(
        (1, 9, LAG_ROWS, PAIR_BLOCK),
        lambda i, c, k: (i // blocks_per_owner, 0, 0, i % blocks_per_owner))
    in_specs = [
        pl.BlockSpec((1, 2, PAIR_BLOCK),
                     lambda i, c, k: (i // blocks_per_owner, 0, i % blocks_per_owner)),
        pl.BlockSpec((rows, width), lambda i, c, k: (0, 0)),
        pl.BlockSpec((LAG_ROWS, part_bins), lambda i, c, k: (0, k[0])),
        pl.BlockSpec((LAG_ROWS, part_bins), lambda i, c, k: (0, k[0])),
    ]
    args = [counts, core_arr, chip_pairs, panel, cos_rows, sin_rows]
    aliases = {}
    if accumulate:
        in_specs.append(out_spec)
        args.append(acc)
        aliases = {len(args) - 1: 0}
    return pl.pallas_call(
        kernel,
        out_shape=jax.ShapeDtypeStruct((owners, 9, LAG_ROWS, per_owner), jnp.float32),
        grid_spec=pltpu.PrefetchScalarGridSpec(
            num_scalar_prefetch=2,
            grid=grid,
            in_specs=in_specs,
            out_specs=out_spec,
            scratch_shapes=[
                pltpu.VMEM((PAIR_BLOCK, width), jnp.float32),
                pltpu.VMEM((PAIR_BLOCK, width), jnp.float32),
            ],
        ),
        input_output_aliases=aliases,
        compiler_params=pltpu.CompilerParams(
            dimension_semantics=("arbitrary",), vmem_limit_bytes=60 * 1024 * 1024),
        cost_estimate=cost,
    )(*args)


MESH_ID = pl.DeviceIdType.MESH


def spread_kernel(pieces_ref, rows_ref, count_ref, panel_ref, chip_rows_ref, chip_count_ref,
                  send_plane, recv_plane,
                  local_sem, send_right, send_left, recv_ring, meta_sems, *, ring_size,
                  plane_size, blk_size, slots, subs):
    me_z = lax.axis_index("z")
    me_c = lax.axis_index("core")
    me_b = lax.axis_index("blk")
    me_q = me_c * blk_size + me_b
    right = (me_z + 1) % ring_size
    left = (me_z + ring_size - 1) % ring_size

    def plane_dev(q):
        return (me_z, q // blk_size, q % blk_size)

    barrier = pltpu.get_barrier_semaphore()

    def greet(i, carry):
        q = (me_q + i) % plane_size
        pl.semaphore_signal(barrier, 1, device_id=plane_dev(q), device_id_type=MESH_ID)
        return carry

    lax.fori_loop(1, plane_size, greet, 0)
    pl.semaphore_signal(barrier, 1, device_id=(right, me_c, me_b), device_id_type=MESH_ID)
    pl.semaphore_signal(barrier, 1, device_id=(left, me_c, me_b), device_id_type=MESH_ID)
    pl.semaphore_wait(barrier, plane_size + 1)

    partner = (me_z, 1 - me_c, me_b)
    meta_copies = []
    for idx, (src, dst) in enumerate(((rows_ref, chip_rows_ref), (count_ref, chip_count_ref))):
        local = pltpu.make_async_copy(src, dst.at[me_c], meta_sems.at[3 * idx])
        local.start()
        remote = pltpu.make_async_remote_copy(
            src, dst.at[me_c], meta_sems.at[3 * idx + 1], meta_sems.at[3 * idx + 2],
            device_id=partner, device_id_type=MESH_ID)
        remote.start()
        arrival = pltpu.make_async_remote_copy(
            src, dst.at[1 - me_c], meta_sems.at[3 * idx + 1], meta_sems.at[3 * idx + 2],
            device_id=partner, device_id_type=MESH_ID)
        meta_copies.append((local, remote, arrival))

    sub_width = panel_ref.shape[1] // subs
    block_rows = plane_size * slots
    half_rows = block_rows // 2
    base = me_z * block_rows
    half = ring_size // 2

    def cols(sub):
        return pl.ds(sub * sub_width, sub_width)

    def rows_of(q, sub):
        return panel_ref.at[pl.ds(base + q * slots, slots), cols(sub)]

    def local_copy(sub):
        return pltpu.make_async_copy(
            pieces_ref.at[me_q, :, cols(sub)], rows_of(me_q, sub), local_sem.at[sub])

    def plane_copy(q, src_q, sub):
        return pltpu.make_async_remote_copy(
            pieces_ref.at[q, :, cols(sub)], rows_of(src_q, sub), send_plane.at[sub, q],
            recv_plane.at[sub, src_q], device_id=plane_dev(q), device_id_type=MESH_ID)

    def scatter(sub):
        local_copy(sub).start()

        def send(i, carry):
            q = (me_q + i) % plane_size
            plane_copy(q, me_q, sub).start()
            return carry

        lax.fori_loop(1, plane_size, send, 0)

    def gathered(sub):
        def arrive(i, carry):
            q = (me_q + plane_size - i) % plane_size
            plane_copy(q, q, sub).wait_recv()
            return carry

        lax.fori_loop(1, plane_size, arrive, 0)
        local_copy(sub).wait()

    def block_of(k, sub):
        return panel_ref.at[pl.ds(k * block_rows, block_rows), cols(sub)]

    def part_of(k, first, sub):
        start = k * block_rows + (0 if first else half_rows)
        return panel_ref.at[pl.ds(start, half_rows), cols(sub)]

    def ring_copy(k, sem, dev, sub):
        return pltpu.make_async_remote_copy(
            block_of(k, sub), block_of(k, sub), sem, recv_ring.at[sub, k],
            device_id=(dev, me_c, me_b), device_id_type=MESH_ID)

    def part_copy(k, first, sem, dev, sub):
        slot = k if first else ring_size
        return pltpu.make_async_remote_copy(
            part_of(k, first, sub), part_of(k, first, sub), sem, recv_ring.at[sub, slot],
            device_id=(dev, me_c, me_b), device_id_type=MESH_ID)

    sends = []

    def ring_step(s, sub):
        k = (me_z + ring_size - s) % ring_size
        if s > 0:
            ring_copy(k, send_right.at[sub, s], left, sub).wait_recv()
        c = ring_copy(k, send_right.at[sub, s], right, sub) if s < half - 1 else part_copy(
            k, True, send_right.at[sub, s], right, sub)
        c.start()
        sends.append(c)
        k = (me_z + s) % ring_size
        if s > 0:
            ring_copy(k, send_left.at[sub, s], right, sub).wait_recv()
        c = ring_copy(k, send_left.at[sub, s], left, sub) if s < half - 1 else part_copy(
            k, False, send_left.at[sub, s], left, sub)
        c.start()
        sends.append(c)

    for sub in range(subs):
        scatter(sub)
        gathered(sub)
        ring_step(0, sub)
    for s in range(1, half):
        for sub in range(subs):
            ring_step(s, sub)
    far = (me_z + half) % ring_size
    for sub in range(subs):
        part_copy(far, True, send_right.at[sub, 0], left, sub).wait_recv()
        part_copy(far, False, send_left.at[sub, 0], right, sub).wait_recv()
    for sub in range(subs):
        def sent(i, carry):
            q = (me_q + i) % plane_size
            plane_copy(q, me_q, sub).wait_send()
            return carry

        lax.fori_loop(1, plane_size, sent, 0)
    for c in sends:
        c.wait_send()
    for local, remote, arrival in meta_copies:
        local.wait()
        arrival.wait_recv()
        remote.wait_send()


def spread(pieces, pair_rows, pair_counts, ring_size, plane_size, blk_size):
    _, slots, width = pieces.shape
    rows = ring_size * plane_size * slots
    kernel = functools.partial(spread_kernel, ring_size=ring_size, plane_size=plane_size,
                               blk_size=blk_size, slots=slots, subs=SUBS)
    half = ring_size // 2
    return pl.pallas_call(
        kernel,
        out_shape=(jax.ShapeDtypeStruct((rows, width), pieces.dtype),
                   jax.ShapeDtypeStruct((2,) + pair_rows.shape, pair_rows.dtype),
                   jax.ShapeDtypeStruct((2,) + pair_counts.shape, pair_counts.dtype)),
        in_specs=[pl.BlockSpec(memory_space=pl.ANY)] * 3,
        out_specs=(pl.BlockSpec(memory_space=pl.ANY),) * 3,
        scratch_shapes=[
            pltpu.SemaphoreType.DMA((SUBS, plane_size)),
            pltpu.SemaphoreType.DMA((SUBS, plane_size)),
            pltpu.SemaphoreType.DMA((SUBS,)),
            pltpu.SemaphoreType.DMA((SUBS, half)),
            pltpu.SemaphoreType.DMA((SUBS, half)),
            pltpu.SemaphoreType.DMA((SUBS, ring_size + 1)),
            pltpu.SemaphoreType.DMA((6,)),
        ],
        compiler_params=pltpu.CompilerParams(collective_id=0, has_side_effects=True),
    )(pieces, pair_rows, pair_counts)


def exchange_kernel(part_ref, out_ref, recv_buf, sems, *, scale):
    me_z = lax.axis_index("z")
    me_c = lax.axis_index("core")
    me_b = lax.axis_index("blk")
    partner = (me_z, 1 - me_c, me_b)
    barrier = pltpu.get_barrier_semaphore()
    pl.semaphore_signal(barrier, 1, device_id=partner, device_id_type=MESH_ID)
    pl.semaphore_wait(barrier, 1)
    copy = pltpu.make_async_remote_copy(
        part_ref.at[1 - me_c], recv_buf, sems.at[0], sems.at[1],
        device_id=partner, device_id_type=MESH_ID)
    copy.start()
    copy.wait()
    out_ref[...] = (part_ref[me_c] + recv_buf[...]) * scale


def exchange(partial, scale):
    shape = partial.shape[1:]
    return pl.pallas_call(
        functools.partial(exchange_kernel, scale=scale),
        out_shape=jax.ShapeDtypeStruct(shape, partial.dtype),
        in_specs=[pl.BlockSpec(memory_space=pltpu.VMEM)],
        out_specs=pl.BlockSpec(memory_space=pltpu.VMEM),
        scratch_shapes=[
            pltpu.VMEM(shape, partial.dtype),
            pltpu.SemaphoreType.DMA((2,)),
        ],
        compiler_params=pltpu.CompilerParams(collective_id=1, has_side_effects=True),
    )(partial)


def shards(spectra, send_rows, send_counts, pair_rows, pair_counts):
    whitened = whiten(spectra)
    station_count, comps, parts, bin_count = whitened.shape
    row_width = comps * parts * bin_count
    slot_count = send_rows.shape[2]
    cores = lax.axis_size("core")
    part_bins = bin_count // cores
    core = lax.axis_index("core")

    flat = whitened.reshape(station_count, row_width)
    lists = send_rows[0]
    col_count = lists.shape[0]
    picked = jnp.take(flat, lists.reshape(-1), axis=0).reshape(col_count, slot_count, row_width)
    alive = jnp.arange(slot_count, dtype=jnp.int32)[None, :] < send_counts[0][:, None]
    picked = jnp.where(alive[:, :, None], picked, jnp.zeros_like(picked))
    pieces = picked.reshape(col_count, slot_count, comps * parts, cores, SUBS,
                            part_bins // SUBS)
    pieces = jnp.transpose(pieces, (3, 0, 1, 4, 2, 5)).reshape(
        cores * col_count, slot_count, comps * parts * part_bins)
    pair_total = pair_rows.shape[1]
    panel, chip_pairs, chip_counts = spread(pieces, pair_rows, pair_counts, lax.axis_size("z"),
                                            cores * col_count, col_count)
    cos_rows, sin_rows = lag_tables(bin_count)
    core_arr = core.astype(jnp.int32)[None]
    partial = pair_sums(chip_counts, core_arr, chip_pairs, panel, cos_rows, sin_rows, cores, 0,
                        None)
    total = exchange(partial, 1.0 / math.sqrt(bin_count))[:, :LAGS, :]
    live = jnp.arange(pair_total, dtype=jnp.int32) < pair_counts[0]
    total = jnp.where(live[None, None, :], total, 0.0).astype(jnp.bfloat16)
    return jnp.transpose(total, (1, 0, 2))


def solution(mesh):
    tile_size = mesh.shape["tile"]
    blk_size = mesh.shape["blk"]
    split = Mesh(mesh.devices.reshape(tile_size // 2, 2, blk_size), ("z", "core", "blk"))
    dev = ("z", "core", "blk")
    return jax.shard_map(
        shards,
        mesh=split,
        in_specs=(
            P(dev, None, None, None),
            P(dev, None, None),
            P(dev, None),
            P(None, dev),
            P(dev),
        ),
        out_specs=P(None, None, dev),
        check_vma=False,
    )
```

```python
import functools
import math

import jax
import ml_dtypes
import numpy as np
import jax.numpy as jnp
from jax import lax
from jax.experimental import pallas as pl
from jax.experimental.pallas import tpu as pltpu
from jax.sharding import Mesh
from jax.sharding import PartitionSpec as P

LAGS = 129
LAG_ROWS = 144
PAIR_BLOCK = 128
BIN_CHUNK = 256
GATHER_CHUNK = 512
SUBS = 2


def whiten(spectra):
    station_count = spectra.shape[0]
    bin_count = spectra.shape[-1]
    ramp_bins = bin_count // 32
    bin_index = jnp.arange(bin_count, dtype=jnp.int32)
    edge_dist = jnp.minimum(bin_index, bin_count - 1 - bin_index).astype(jnp.float32) + 0.5
    ramp_vals = 0.5 - 0.5 * jnp.cos(jnp.pi * edge_dist / ramp_bins)
    taper = jnp.where(edge_dist < ramp_bins, ramp_vals, jnp.ones_like(ramp_vals))
    blocked = spectra.reshape(station_count, 3, 2, bin_count // 64, 64)
    power = jnp.mean(blocked * blocked, axis=(1, 2, 4))
    inverse = 1.0 / jnp.sqrt(power + 1e-05)
    spread_scale = jnp.repeat(inverse, 64, axis=1)
    return (spectra * taper * spread_scale[:, None, None, :]).astype(jnp.bfloat16)


def lag_tables(bin_count):
    lag_index = np.arange(LAGS, dtype=np.int32) - LAGS // 2
    bin_index = np.arange(bin_count, dtype=np.int32)
    phase_steps = lag_index[:, None] * bin_index[None, :] % (2 * bin_count)
    angle = phase_steps.astype(np.float32) * np.float32(np.pi / bin_count)
    pad = ((0, LAG_ROWS - LAGS), (0, 0))
    cos_rows = np.pad(np.cos(angle).astype(np.float32).astype(ml_dtypes.bfloat16), pad)
    sin_rows = np.pad((-np.sin(angle)).astype(np.float32).astype(ml_dtypes.bfloat16), pad)
    return jnp.asarray(cos_rows), jnp.asarray(sin_rows)


def pair_kernel(counts_ref, core_ref, pairs_ref, panel_ref, cos_ref, sin_ref, *rest,
                blocks_per_owner, part_bins, accumulate):
    if accumulate:
        acc_ref, out_ref, f_scr, s_scr = rest
    else:
        out_ref, f_scr, s_scr = rest
    step = pl.program_id(0)
    owner = step // blocks_per_owner
    start = (step % blocks_per_owner) * PAIR_BLOCK
    live = start < counts_ref[owner, 0]
    if accumulate:
        out_ref[...] = acc_ref[...]
    else:
        out_ref[...] = jnp.zeros_like(out_ref)

    @pl.when(live)
    def _():
        rows = panel_ref.shape[0]
        width = panel_ref.shape[1]
        iota = lax.broadcasted_iota(jnp.int32, (rows, PAIR_BLOCK), 0)
        idx = pairs_ref[0]
        pick_first = jnp.where(idx[0:1, :] == iota, 1.0, 0.0).T.astype(jnp.bfloat16)
        pick_second = jnp.where(idx[1:2, :] == iota, 1.0, 0.0).T.astype(jnp.bfloat16)
        gather_chunk = min(GATHER_CHUNK, width)

        def gather(c, carry):
            off = pl.multiple_of(c * gather_chunk, gather_chunk)
            block = panel_ref[:, pl.ds(off, gather_chunk)]
            f_scr[:, pl.ds(off, gather_chunk)] = jnp.dot(
                pick_first, block, preferred_element_type=jnp.float32)
            s_scr[:, pl.ds(off, gather_chunk)] = jnp.dot(
                pick_second, block, preferred_element_type=jnp.float32)
            return carry

        lax.fori_loop(0, width // gather_chunk, gather, 0)
        nt = (((1,), (1,)), ((), ()))
        sub_bins = part_bins // SUBS
        bin_chunk = min(BIN_CHUNK, sub_bins)
        for sub in range(SUBS):
            col0 = sub * 6 * sub_bins

            def chunk(kc, carry):
                off = pl.multiple_of(kc * bin_chunk, bin_chunk)
                cos_blk = cos_ref[:, pl.ds(sub * sub_bins + off, bin_chunk)]
                sin_blk = sin_ref[:, pl.ds(sub * sub_bins + off, bin_chunk)]
                for a in range(3):
                    f_re = f_scr[:, pl.ds(col0 + 2 * a * sub_bins + off, bin_chunk)]
                    f_im = f_scr[:, pl.ds(col0 + (2 * a + 1) * sub_bins + off, bin_chunk)]
                    for b in range(3):
                        s_re = s_scr[:, pl.ds(col0 + 2 * b * sub_bins + off, bin_chunk)]
                        s_im = s_scr[:, pl.ds(col0 + (2 * b + 1) * sub_bins + off, bin_chunk)]
                        real_part = (f_re * s_re + f_im * s_im).astype(jnp.bfloat16)
                        imag_part = (f_im * s_re - f_re * s_im).astype(jnp.bfloat16)
                        acc = lax.dot_general(cos_blk, real_part, nt,
                                              preferred_element_type=jnp.float32)
                        acc = acc + lax.dot_general(sin_blk, imag_part, nt,
                                                    preferred_element_type=jnp.float32)
                        out_ref[0, 3 * a + b] += acc
                return carry

            lax.fori_loop(0, sub_bins // bin_chunk, chunk, 0)


def pair_sums(counts, core_arr, chip_pairs, panel, cos_rows, sin_rows, owners, chunk_id, acc):
    rows, width = panel.shape
    part_bins = width // 6
    pairs = chip_pairs.shape[0] * chip_pairs.shape[2]
    per_owner = pairs // owners
    blocks_per_owner = per_owner // PAIR_BLOCK
    grid = (pairs // PAIR_BLOCK,)
    accumulate = acc is not None
    kernel = functools.partial(pair_kernel, blocks_per_owner=blocks_per_owner,
                               part_bins=part_bins, accumulate=accumulate)
    flops = 2 * pairs * rows * width * 2 + 2 * LAG_ROWS * 2 * part_bins * 9 * pairs
    out_bytes = owners * 9 * LAG_ROWS * per_owner * 4
    cost = pl.CostEstimate(flops=flops, transcendentals=0,
                           bytes_accessed=rows * width * 2 + out_bytes * (2 if accumulate else 1))
    out_spec = pl.BlockSpec(
        (1, 9, LAG_ROWS, PAIR_BLOCK),
        lambda i, c, k: (i // blocks_per_owner, 0, 0, i % blocks_per_owner))
    in_specs = [
        pl.BlockSpec((1, 2, PAIR_BLOCK),
                     lambda i, c, k: (i // blocks_per_owner, 0, i % blocks_per_owner)),
        pl.BlockSpec((rows, width), lambda i, c, k: (0, 0)),
        pl.BlockSpec((LAG_ROWS, part_bins), lambda i, c, k: (0, k[0])),
        pl.BlockSpec((LAG_ROWS, part_bins), lambda i, c, k: (0, k[0])),
    ]
    args = [counts, core_arr, chip_pairs, panel, cos_rows, sin_rows]
    aliases = {}
    if accumulate:
        in_specs.append(out_spec)
        args.append(acc)
        aliases = {len(args) - 1: 0}
    return pl.pallas_call(
        kernel,
        out_shape=jax.ShapeDtypeStruct((owners, 9, LAG_ROWS, per_owner), jnp.float32),
        grid_spec=pltpu.PrefetchScalarGridSpec(
            num_scalar_prefetch=2,
            grid=grid,
            in_specs=in_specs,
            out_specs=out_spec,
            scratch_shapes=[
                pltpu.VMEM((PAIR_BLOCK, width), jnp.float32),
                pltpu.VMEM((PAIR_BLOCK, width), jnp.float32),
            ],
        ),
        input_output_aliases=aliases,
        compiler_params=pltpu.CompilerParams(
            dimension_semantics=("arbitrary",), vmem_limit_bytes=60 * 1024 * 1024),
        cost_estimate=cost,
    )(*args)


MESH_ID = pl.DeviceIdType.MESH


def spread_kernel(pieces_ref, rows_ref, count_ref, panel_ref, chip_rows_ref, chip_count_ref,
                  send_plane, recv_plane,
                  local_sem, send_right, send_left, recv_ring, meta_sems, *, ring_size,
                  plane_size, blk_size, slots, subs):
    me_z = lax.axis_index("z")
    me_c = lax.axis_index("core")
    me_b = lax.axis_index("blk")
    me_q = me_c * blk_size + me_b
    right = (me_z + 1) % ring_size
    left = (me_z + ring_size - 1) % ring_size

    def plane_dev(q):
        return (me_z, q // blk_size, q % blk_size)

    barrier = pltpu.get_barrier_semaphore()

    def greet(i, carry):
        q = (me_q + i) % plane_size
        pl.semaphore_signal(barrier, 1, device_id=plane_dev(q), device_id_type=MESH_ID)
        return carry

    lax.fori_loop(1, plane_size, greet, 0)
    pl.semaphore_signal(barrier, 1, device_id=(right, me_c, me_b), device_id_type=MESH_ID)
    pl.semaphore_signal(barrier, 1, device_id=(left, me_c, me_b), device_id_type=MESH_ID)
    pl.semaphore_wait(barrier, plane_size + 1)

    partner = (me_z, 1 - me_c, me_b)
    meta_copies = []
    for idx, (src, dst) in enumerate(((rows_ref, chip_rows_ref), (count_ref, chip_count_ref))):
        local = pltpu.make_async_copy(src, dst.at[me_c], meta_sems.at[3 * idx])
        local.start()
        remote = pltpu.make_async_remote_copy(
            src, dst.at[me_c], meta_sems.at[3 * idx + 1], meta_sems.at[3 * idx + 2],
            device_id=partner, device_id_type=MESH_ID)
        remote.start()
        arrival = pltpu.make_async_remote_copy(
            src, dst.at[1 - me_c], meta_sems.at[3 * idx + 1], meta_sems.at[3 * idx + 2],
            device_id=partner, device_id_type=MESH_ID)
        meta_copies.append((local, remote, arrival))

    sub_width = panel_ref.shape[1] // subs
    block_rows = plane_size * slots
    half_rows = block_rows // 2
    base = me_z * block_rows
    half = ring_size // 2

    def cols(sub):
        return pl.ds(sub * sub_width, sub_width)

    def rows_of(q, sub):
        return panel_ref.at[pl.ds(base + q * slots, slots), cols(sub)]

    def local_copy(sub):
        return pltpu.make_async_copy(
            pieces_ref.at[me_q, :, cols(sub)], rows_of(me_q, sub), local_sem.at[sub])

    def plane_copy(q, src_q, sub):
        return pltpu.make_async_remote_copy(
            pieces_ref.at[q, :, cols(sub)], rows_of(src_q, sub), send_plane.at[sub, q],
            recv_plane.at[sub, src_q], device_id=plane_dev(q), device_id_type=MESH_ID)

    def scatter(sub):
        local_copy(sub).start()

        def send(i, carry):
            q = (me_q + i) % plane_size
            plane_copy(q, me_q, sub).start()
            return carry

        lax.fori_loop(1, plane_size, send, 0)

    def gathered(sub):
        def arrive(i, carry):
            q = (me_q + plane_size - i) % plane_size
            plane_copy(q, q, sub).wait_recv()
            return carry

        lax.fori_loop(1, plane_size, arrive, 0)
        local_copy(sub).wait()

    def block_of(k, sub):
        return panel_ref.at[pl.ds(k * block_rows, block_rows), cols(sub)]

    def part_of(k, first, sub):
        start = k * block_rows + (0 if first else half_rows)
        return panel_ref.at[pl.ds(start, half_rows), cols(sub)]

    def ring_copy(k, sem, dev, sub):
        return pltpu.make_async_remote_copy(
            block_of(k, sub), block_of(k, sub), sem, recv_ring.at[sub, k],
            device_id=(dev, me_c, me_b), device_id_type=MESH_ID)

    def part_copy(k, first, sem, dev, sub):
        slot = k if first else ring_size
        return pltpu.make_async_remote_copy(
            part_of(k, first, sub), part_of(k, first, sub), sem, recv_ring.at[sub, slot],
            device_id=(dev, me_c, me_b), device_id_type=MESH_ID)

    sends = []

    def ring_step(s, sub):
        k = (me_z + ring_size - s) % ring_size
        if s > 0:
            ring_copy(k, send_right.at[sub, s], left, sub).wait_recv()
        c = ring_copy(k, send_right.at[sub, s], right, sub) if s < half - 1 else part_copy(
            k, True, send_right.at[sub, s], right, sub)
        c.start()
        sends.append(c)
        k = (me_z + s) % ring_size
        if s > 0:
            ring_copy(k, send_left.at[sub, s], right, sub).wait_recv()
        c = ring_copy(k, send_left.at[sub, s], left, sub) if s < half - 1 else part_copy(
            k, False, send_left.at[sub, s], left, sub)
        c.start()
        sends.append(c)

    for sub in range(subs):
        scatter(sub)
        gathered(sub)
        ring_step(0, sub)
    for s in range(1, half):
        for sub in range(subs):
            ring_step(s, sub)
    far = (me_z + half) % ring_size
    for sub in range(subs):
        part_copy(far, True, send_right.at[sub, 0], left, sub).wait_recv()
        part_copy(far, False, send_left.at[sub, 0], right, sub).wait_recv()
    for sub in range(subs):
        def sent(i, carry):
            q = (me_q + i) % plane_size
            plane_copy(q, me_q, sub).wait_send()
            return carry

        lax.fori_loop(1, plane_size, sent, 0)
    for c in sends:
        c.wait_send()
    for local, remote, arrival in meta_copies:
        local.wait()
        arrival.wait_recv()
        remote.wait_send()


def spread(pieces, pair_rows, pair_counts, ring_size, plane_size, blk_size):
    _, slots, width = pieces.shape
    rows = ring_size * plane_size * slots
    kernel = functools.partial(spread_kernel, ring_size=ring_size, plane_size=plane_size,
                               blk_size=blk_size, slots=slots, subs=SUBS)
    half = ring_size // 2
    return pl.pallas_call(
        kernel,
        out_shape=(jax.ShapeDtypeStruct((rows, width), pieces.dtype),
                   jax.ShapeDtypeStruct((2,) + pair_rows.shape, pair_rows.dtype),
                   jax.ShapeDtypeStruct((2,) + pair_counts.shape, pair_counts.dtype)),
        in_specs=[pl.BlockSpec(memory_space=pl.ANY)] * 3,
        out_specs=(pl.BlockSpec(memory_space=pl.ANY),) * 3,
        scratch_shapes=[
            pltpu.SemaphoreType.DMA((SUBS, plane_size)),
            pltpu.SemaphoreType.DMA((SUBS, plane_size)),
            pltpu.SemaphoreType.DMA((SUBS,)),
            pltpu.SemaphoreType.DMA((SUBS, half)),
            pltpu.SemaphoreType.DMA((SUBS, half)),
            pltpu.SemaphoreType.DMA((SUBS, ring_size + 1)),
            pltpu.SemaphoreType.DMA((6,)),
        ],
        compiler_params=pltpu.CompilerParams(collective_id=0, has_side_effects=True),
    )(pieces, pair_rows, pair_counts)


def exchange_kernel(part_ref, out_ref, recv_buf, sems, *, scale):
    me_z = lax.axis_index("z")
    me_c = lax.axis_index("core")
    me_b = lax.axis_index("blk")
    partner = (me_z, 1 - me_c, me_b)
    barrier = pltpu.get_barrier_semaphore()
    pl.semaphore_signal(barrier, 1, device_id=partner, device_id_type=MESH_ID)
    pl.semaphore_wait(barrier, 1)
    copy = pltpu.make_async_remote_copy(
        part_ref.at[1 - me_c], recv_buf, sems.at[0], sems.at[1],
        device_id=partner, device_id_type=MESH_ID)
    copy.start()
    copy.wait()
    out_ref[...] = (part_ref[me_c] + recv_buf[...]) * scale


def exchange(partial, scale):
    shape = partial.shape[1:]
    return pl.pallas_call(
        functools.partial(exchange_kernel, scale=scale),
        out_shape=jax.ShapeDtypeStruct(shape, partial.dtype),
        in_specs=[pl.BlockSpec(memory_space=pltpu.VMEM)],
        out_specs=pl.BlockSpec(memory_space=pltpu.VMEM),
        scratch_shapes=[
            pltpu.VMEM(shape, partial.dtype),
            pltpu.SemaphoreType.DMA((2,)),
        ],
        compiler_params=pltpu.CompilerParams(collective_id=1, has_side_effects=True),
    )(partial)


def shards(spectra, send_rows, send_counts, pair_rows, pair_counts):
    whitened = whiten(spectra)
    station_count, comps, parts, bin_count = whitened.shape
    slot_count = send_rows.shape[2]
    cores = lax.axis_size("core")
    part_bins = bin_count // cores
    core = lax.axis_index("core")

    sub_bins = part_bins // SUBS
    ordered = jnp.transpose(
        whitened.reshape(station_count, comps * parts, cores, SUBS, sub_bins), (0, 2, 3, 1, 4))
    flat = ordered.reshape(station_count * cores, comps * parts * part_bins)
    lists = send_rows[0]
    col_count = lists.shape[0]
    rows = lists[None, :, :] * cores + jnp.arange(cores, dtype=jnp.int32)[:, None, None]
    pieces = jnp.take(flat, rows.reshape(-1), axis=0).reshape(
        cores * col_count, slot_count, comps * parts * part_bins)
    alive = jnp.arange(slot_count, dtype=jnp.int32)[None, :] < send_counts[0][:, None]
    alive = jnp.tile(alive, (cores, 1))
    pieces = jnp.where(alive[:, :, None], pieces, jnp.zeros_like(pieces))
    pair_total = pair_rows.shape[1]
    panel, chip_pairs, chip_counts = spread(pieces, pair_rows, pair_counts, lax.axis_size("z"),
                                            cores * col_count, col_count)
    cos_rows, sin_rows = lag_tables(bin_count)
    core_arr = core.astype(jnp.int32)[None]
    partial = pair_sums(chip_counts, core_arr, chip_pairs, panel, cos_rows, sin_rows, cores, 0,
                        None)
    total = exchange(partial, 1.0 / math.sqrt(bin_count))[:, :LAGS, :]
    live = jnp.arange(pair_total, dtype=jnp.int32) < pair_counts[0]
    total = jnp.where(live[None, None, :], total, 0.0).astype(jnp.bfloat16)
    return jnp.transpose(total, (1, 0, 2))


def solution(mesh):
    tile_size = mesh.shape["tile"]
    blk_size = mesh.shape["blk"]
    split = Mesh(mesh.devices.reshape(tile_size // 2, 2, blk_size), ("z", "core", "blk"))
    dev = ("z", "core", "blk")
    return jax.shard_map(
        shards,
        mesh=split,
        in_specs=(
            P(dev, None, None, None),
            P(dev, None, None),
            P(dev, None),
            P(None, dev),
            P(dev),
        ),
        out_specs=P(None, None, dev),
        check_vma=False,
    )
```

```python
import functools
import math

import jax
import ml_dtypes
import numpy as np
import jax.numpy as jnp
from jax import lax
from jax.experimental import pallas as pl
from jax.experimental.pallas import tpu as pltpu
from jax.sharding import Mesh
from jax.sharding import PartitionSpec as P

LAGS = 129
LAG_ROWS = 144
PAIR_BLOCK = 128
BIN_CHUNK = 256
GATHER_CHUNK = 512
SUBS = 2


def whiten(spectra):
    station_count = spectra.shape[0]
    bin_count = spectra.shape[-1]
    ramp_bins = bin_count // 32
    bin_index = jnp.arange(bin_count, dtype=jnp.int32)
    edge_dist = jnp.minimum(bin_index, bin_count - 1 - bin_index).astype(jnp.float32) + 0.5
    ramp_vals = 0.5 - 0.5 * jnp.cos(jnp.pi * edge_dist / ramp_bins)
    taper = jnp.where(edge_dist < ramp_bins, ramp_vals, jnp.ones_like(ramp_vals))
    blocked = spectra.reshape(station_count, 3, 2, bin_count // 64, 64)
    power = jnp.mean(blocked * blocked, axis=(1, 2, 4))
    inverse = 1.0 / jnp.sqrt(power + 1e-05)
    spread_scale = jnp.repeat(inverse, 64, axis=1)
    return (spectra * taper * spread_scale[:, None, None, :]).astype(jnp.bfloat16)


def lag_tables(bin_count):
    lag_index = np.arange(LAGS, dtype=np.int32) - LAGS // 2
    bin_index = np.arange(bin_count, dtype=np.int32)
    phase_steps = lag_index[:, None] * bin_index[None, :] % (2 * bin_count)
    angle = phase_steps.astype(np.float32) * np.float32(np.pi / bin_count)
    pad = ((0, LAG_ROWS - LAGS), (0, 0))
    cos_rows = np.pad(np.cos(angle).astype(np.float32).astype(ml_dtypes.bfloat16), pad)
    sin_rows = np.pad((-np.sin(angle)).astype(np.float32).astype(ml_dtypes.bfloat16), pad)
    return jnp.asarray(cos_rows), jnp.asarray(sin_rows)


def pair_kernel(counts_ref, core_ref, pairs_ref, panel_ref, cos_ref, sin_ref, *rest,
                blocks_per_owner, part_bins, accumulate):
    if accumulate:
        acc_ref, out_ref, f_scr, s_scr = rest
    else:
        out_ref, f_scr, s_scr = rest
    step = pl.program_id(0)
    owner = step // blocks_per_owner
    start = (step % blocks_per_owner) * PAIR_BLOCK
    live = start < counts_ref[owner, 0]
    if accumulate:
        out_ref[...] = acc_ref[...]
    else:
        out_ref[...] = jnp.zeros_like(out_ref)

    @pl.when(live)
    def _():
        rows = panel_ref.shape[0]
        width = panel_ref.shape[1]
        iota = lax.broadcasted_iota(jnp.int32, (rows, PAIR_BLOCK), 0)
        idx = pairs_ref[0]
        pick_first = jnp.where(idx[0:1, :] == iota, 1.0, 0.0).T.astype(jnp.bfloat16)
        pick_second = jnp.where(idx[1:2, :] == iota, 1.0, 0.0).T.astype(jnp.bfloat16)
        gather_chunk = min(GATHER_CHUNK, width)

        def gather(c, carry):
            off = pl.multiple_of(c * gather_chunk, gather_chunk)
            block = panel_ref[:, pl.ds(off, gather_chunk)]
            f_scr[:, pl.ds(off, gather_chunk)] = jnp.dot(
                pick_first, block, preferred_element_type=jnp.float32).astype(jnp.bfloat16)
            s_scr[:, pl.ds(off, gather_chunk)] = jnp.dot(
                pick_second, block, preferred_element_type=jnp.float32).astype(jnp.bfloat16)
            return carry

        lax.fori_loop(0, width // gather_chunk, gather, 0)
        nt = (((1,), (1,)), ((), ()))
        sub_bins = part_bins // SUBS
        bin_chunk = min(BIN_CHUNK, sub_bins)
        for sub in range(SUBS):
            col0 = sub * 6 * sub_bins

            def chunk(kc, carry):
                off = pl.multiple_of(kc * bin_chunk, bin_chunk)
                cos_blk = cos_ref[:, pl.ds(sub * sub_bins + off, bin_chunk)]
                sin_blk = sin_ref[:, pl.ds(sub * sub_bins + off, bin_chunk)]
                for a in range(3):
                    f_re = f_scr[:, pl.ds(col0 + 2 * a * sub_bins + off, bin_chunk)]
                    f_im = f_scr[:, pl.ds(col0 + (2 * a + 1) * sub_bins + off, bin_chunk)]
                    for b in range(3):
                        s_re = s_scr[:, pl.ds(col0 + 2 * b * sub_bins + off, bin_chunk)]
                        s_im = s_scr[:, pl.ds(col0 + (2 * b + 1) * sub_bins + off, bin_chunk)]
                        real_part = f_re * s_re + f_im * s_im
                        imag_part = f_im * s_re - f_re * s_im
                        acc = lax.dot_general(cos_blk, real_part, nt,
                                              preferred_element_type=jnp.float32)
                        acc = acc + lax.dot_general(sin_blk, imag_part, nt,
                                                    preferred_element_type=jnp.float32)
                        out_ref[0, 3 * a + b] += acc
                return carry

            lax.fori_loop(0, sub_bins // bin_chunk, chunk, 0)


def pair_sums(counts, core_arr, chip_pairs, panel, cos_rows, sin_rows, owners, chunk_id, acc):
    rows, width = panel.shape
    part_bins = width // 6
    pairs = chip_pairs.shape[0] * chip_pairs.shape[2]
    per_owner = pairs // owners
    blocks_per_owner = per_owner // PAIR_BLOCK
    grid = (pairs // PAIR_BLOCK,)
    accumulate = acc is not None
    kernel = functools.partial(pair_kernel, blocks_per_owner=blocks_per_owner,
                               part_bins=part_bins, accumulate=accumulate)
    flops = 2 * pairs * rows * width * 2 + 2 * LAG_ROWS * 2 * part_bins * 9 * pairs
    out_bytes = owners * 9 * LAG_ROWS * per_owner * 4
    cost = pl.CostEstimate(flops=flops, transcendentals=0,
                           bytes_accessed=rows * width * 2 + out_bytes * (2 if accumulate else 1))
    out_spec = pl.BlockSpec(
        (1, 9, LAG_ROWS, PAIR_BLOCK),
        lambda i, c, k: (i // blocks_per_owner, 0, 0, i % blocks_per_owner))
    in_specs = [
        pl.BlockSpec((1, 2, PAIR_BLOCK),
                     lambda i, c, k: (i // blocks_per_owner, 0, i % blocks_per_owner)),
        pl.BlockSpec((rows, width), lambda i, c, k: (0, 0)),
        pl.BlockSpec((LAG_ROWS, part_bins), lambda i, c, k: (0, k[0])),
        pl.BlockSpec((LAG_ROWS, part_bins), lambda i, c, k: (0, k[0])),
    ]
    args = [counts, core_arr, chip_pairs, panel, cos_rows, sin_rows]
    aliases = {}
    if accumulate:
        in_specs.append(out_spec)
        args.append(acc)
        aliases = {len(args) - 1: 0}
    return pl.pallas_call(
        kernel,
        out_shape=jax.ShapeDtypeStruct((owners, 9, LAG_ROWS, per_owner), jnp.float32),
        grid_spec=pltpu.PrefetchScalarGridSpec(
            num_scalar_prefetch=2,
            grid=grid,
            in_specs=in_specs,
            out_specs=out_spec,
            scratch_shapes=[
                pltpu.VMEM((PAIR_BLOCK, width), jnp.bfloat16),
                pltpu.VMEM((PAIR_BLOCK, width), jnp.bfloat16),
            ],
        ),
        input_output_aliases=aliases,
        compiler_params=pltpu.CompilerParams(
            dimension_semantics=("arbitrary",), vmem_limit_bytes=60 * 1024 * 1024),
        cost_estimate=cost,
    )(*args)


MESH_ID = pl.DeviceIdType.MESH


def spread_kernel(pieces_ref, rows_ref, count_ref, panel_ref, chip_rows_ref, chip_count_ref,
                  send_plane, recv_plane,
                  local_sem, send_right, send_left, recv_ring, meta_sems, *, ring_size,
                  plane_size, blk_size, slots, subs):
    me_z = lax.axis_index("z")
    me_c = lax.axis_index("core")
    me_b = lax.axis_index("blk")
    me_q = me_c * blk_size + me_b
    right = (me_z + 1) % ring_size
    left = (me_z + ring_size - 1) % ring_size

    def plane_dev(q):
        return (me_z, q // blk_size, q % blk_size)

    barrier = pltpu.get_barrier_semaphore()

    def greet(i, carry):
        q = (me_q + i) % plane_size
        pl.semaphore_signal(barrier, 1, device_id=plane_dev(q), device_id_type=MESH_ID)
        return carry

    lax.fori_loop(1, plane_size, greet, 0)
    pl.semaphore_signal(barrier, 1, device_id=(right, me_c, me_b), device_id_type=MESH_ID)
    pl.semaphore_signal(barrier, 1, device_id=(left, me_c, me_b), device_id_type=MESH_ID)
    pl.semaphore_wait(barrier, plane_size + 1)

    partner = (me_z, 1 - me_c, me_b)
    meta_copies = []
    for idx, (src, dst) in enumerate(((rows_ref, chip_rows_ref), (count_ref, chip_count_ref))):
        local = pltpu.make_async_copy(src, dst.at[me_c], meta_sems.at[3 * idx])
        local.start()
        remote = pltpu.make_async_remote_copy(
            src, dst.at[me_c], meta_sems.at[3 * idx + 1], meta_sems.at[3 * idx + 2],
            device_id=partner, device_id_type=MESH_ID)
        remote.start()
        arrival = pltpu.make_async_remote_copy(
            src, dst.at[1 - me_c], meta_sems.at[3 * idx + 1], meta_sems.at[3 * idx + 2],
            device_id=partner, device_id_type=MESH_ID)
        meta_copies.append((local, remote, arrival))

    sub_width = panel_ref.shape[1] // subs
    block_rows = plane_size * slots
    half_rows = block_rows // 2
    base = me_z * block_rows
    half = ring_size // 2

    def cols(sub):
        return pl.ds(sub * sub_width, sub_width)

    def rows_of(q, sub):
        return panel_ref.at[pl.ds(base + q * slots, slots), cols(sub)]

    def local_copy(sub):
        return pltpu.make_async_copy(
            pieces_ref.at[me_q, :, cols(sub)], rows_of(me_q, sub), local_sem.at[sub])

    def plane_copy(q, src_q, sub):
        return pltpu.make_async_remote_copy(
            pieces_ref.at[q, :, cols(sub)], rows_of(src_q, sub), send_plane.at[sub, q],
            recv_plane.at[sub, src_q], device_id=plane_dev(q), device_id_type=MESH_ID)

    def scatter(sub):
        local_copy(sub).start()

        def send(i, carry):
            q = (me_q + i) % plane_size
            plane_copy(q, me_q, sub).start()
            return carry

        lax.fori_loop(1, plane_size, send, 0)

    def gathered(sub):
        def arrive(i, carry):
            q = (me_q + plane_size - i) % plane_size
            plane_copy(q, q, sub).wait_recv()
            return carry

        lax.fori_loop(1, plane_size, arrive, 0)
        local_copy(sub).wait()

    def block_of(k, sub):
        return panel_ref.at[pl.ds(k * block_rows, block_rows), cols(sub)]

    def part_of(k, first, sub):
        start = k * block_rows + (0 if first else half_rows)
        return panel_ref.at[pl.ds(start, half_rows), cols(sub)]

    def ring_copy(k, sem, dev, sub):
        return pltpu.make_async_remote_copy(
            block_of(k, sub), block_of(k, sub), sem, recv_ring.at[sub, k],
            device_id=(dev, me_c, me_b), device_id_type=MESH_ID)

    def part_copy(k, first, sem, dev, sub):
        slot = k if first else ring_size
        return pltpu.make_async_remote_copy(
            part_of(k, first, sub), part_of(k, first, sub), sem, recv_ring.at[sub, slot],
            device_id=(dev, me_c, me_b), device_id_type=MESH_ID)

    sends = []

    def ring_step(s, sub):
        k = (me_z + ring_size - s) % ring_size
        if s > 0:
            ring_copy(k, send_right.at[sub, s], left, sub).wait_recv()
        c = ring_copy(k, send_right.at[sub, s], right, sub) if s < half - 1 else part_copy(
            k, True, send_right.at[sub, s], right, sub)
        c.start()
        sends.append(c)
        k = (me_z + s) % ring_size
        if s > 0:
            ring_copy(k, send_left.at[sub, s], right, sub).wait_recv()
        c = ring_copy(k, send_left.at[sub, s], left, sub) if s < half - 1 else part_copy(
            k, False, send_left.at[sub, s], left, sub)
        c.start()
        sends.append(c)

    for sub in range(subs):
        scatter(sub)
        gathered(sub)
        ring_step(0, sub)
    for s in range(1, half):
        for sub in range(subs):
            ring_step(s, sub)
    far = (me_z + half) % ring_size
    for sub in range(subs):
        part_copy(far, True, send_right.at[sub, 0], left, sub).wait_recv()
        part_copy(far, False, send_left.at[sub, 0], right, sub).wait_recv()
    for sub in range(subs):
        def sent(i, carry):
            q = (me_q + i) % plane_size
            plane_copy(q, me_q, sub).wait_send()
            return carry

        lax.fori_loop(1, plane_size, sent, 0)
    for c in sends:
        c.wait_send()
    for local, remote, arrival in meta_copies:
        local.wait()
        arrival.wait_recv()
        remote.wait_send()


def spread(pieces, pair_rows, pair_counts, ring_size, plane_size, blk_size):
    _, slots, width = pieces.shape
    rows = ring_size * plane_size * slots
    kernel = functools.partial(spread_kernel, ring_size=ring_size, plane_size=plane_size,
                               blk_size=blk_size, slots=slots, subs=SUBS)
    half = ring_size // 2
    return pl.pallas_call(
        kernel,
        out_shape=(jax.ShapeDtypeStruct((rows, width), pieces.dtype),
                   jax.ShapeDtypeStruct((2,) + pair_rows.shape, pair_rows.dtype),
                   jax.ShapeDtypeStruct((2,) + pair_counts.shape, pair_counts.dtype)),
        in_specs=[pl.BlockSpec(memory_space=pl.ANY)] * 3,
        out_specs=(pl.BlockSpec(memory_space=pl.ANY),) * 3,
        scratch_shapes=[
            pltpu.SemaphoreType.DMA((SUBS, plane_size)),
            pltpu.SemaphoreType.DMA((SUBS, plane_size)),
            pltpu.SemaphoreType.DMA((SUBS,)),
            pltpu.SemaphoreType.DMA((SUBS, half)),
            pltpu.SemaphoreType.DMA((SUBS, half)),
            pltpu.SemaphoreType.DMA((SUBS, ring_size + 1)),
            pltpu.SemaphoreType.DMA((6,)),
        ],
        compiler_params=pltpu.CompilerParams(collective_id=0, has_side_effects=True),
    )(pieces, pair_rows, pair_counts)


def exchange_kernel(part_ref, out_ref, recv_buf, sems, *, scale):
    me_z = lax.axis_index("z")
    me_c = lax.axis_index("core")
    me_b = lax.axis_index("blk")
    partner = (me_z, 1 - me_c, me_b)
    barrier = pltpu.get_barrier_semaphore()
    pl.semaphore_signal(barrier, 1, device_id=partner, device_id_type=MESH_ID)
    pl.semaphore_wait(barrier, 1)
    copy = pltpu.make_async_remote_copy(
        part_ref.at[1 - me_c], recv_buf, sems.at[0], sems.at[1],
        device_id=partner, device_id_type=MESH_ID)
    copy.start()
    copy.wait()
    out_ref[...] = (part_ref[me_c] + recv_buf[...]) * scale


def exchange(partial, scale):
    shape = partial.shape[1:]
    return pl.pallas_call(
        functools.partial(exchange_kernel, scale=scale),
        out_shape=jax.ShapeDtypeStruct(shape, partial.dtype),
        in_specs=[pl.BlockSpec(memory_space=pltpu.VMEM)],
        out_specs=pl.BlockSpec(memory_space=pltpu.VMEM),
        scratch_shapes=[
            pltpu.VMEM(shape, partial.dtype),
            pltpu.SemaphoreType.DMA((2,)),
        ],
        compiler_params=pltpu.CompilerParams(collective_id=1, has_side_effects=True),
    )(partial)


def shards(spectra, send_rows, send_counts, pair_rows, pair_counts):
    whitened = whiten(spectra)
    station_count, comps, parts, bin_count = whitened.shape
    row_width = comps * parts * bin_count
    slot_count = send_rows.shape[2]
    cores = lax.axis_size("core")
    part_bins = bin_count // cores
    core = lax.axis_index("core")

    flat = whitened.reshape(station_count, row_width)
    lists = send_rows[0]
    col_count = lists.shape[0]
    picked = jnp.take(flat, lists.reshape(-1), axis=0).reshape(col_count, slot_count, row_width)
    alive = jnp.arange(slot_count, dtype=jnp.int32)[None, :] < send_counts[0][:, None]
    picked = jnp.where(alive[:, :, None], picked, jnp.zeros_like(picked))
    pieces = picked.reshape(col_count, slot_count, comps * parts, cores, SUBS,
                            part_bins // SUBS)
    pieces = jnp.transpose(pieces, (3, 0, 1, 4, 2, 5)).reshape(
        cores * col_count, slot_count, comps * parts * part_bins)
    pair_total = pair_rows.shape[1]
    panel, chip_pairs, chip_counts = spread(pieces, pair_rows, pair_counts, lax.axis_size("z"),
                                            cores * col_count, col_count)
    cos_rows, sin_rows = lag_tables(bin_count)
    core_arr = core.astype(jnp.int32)[None]
    partial = pair_sums(chip_counts, core_arr, chip_pairs, panel, cos_rows, sin_rows, cores, 0,
                        None)
    total = exchange(partial, 1.0 / math.sqrt(bin_count))[:, :LAGS, :]
    live = jnp.arange(pair_total, dtype=jnp.int32) < pair_counts[0]
    total = jnp.where(live[None, None, :], total, 0.0).astype(jnp.bfloat16)
    return jnp.transpose(total, (1, 0, 2))


def solution(mesh):
    tile_size = mesh.shape["tile"]
    blk_size = mesh.shape["blk"]
    split = Mesh(mesh.devices.reshape(tile_size // 2, 2, blk_size), ("z", "core", "blk"))
    dev = ("z", "core", "blk")
    return jax.shard_map(
        shards,
        mesh=split,
        in_specs=(
            P(dev, None, None, None),
            P(dev, None, None),
            P(dev, None),
            P(None, dev),
            P(dev),
        ),
        out_specs=P(None, None, dev),
        check_vma=False,
    )
```

```python
import functools
import math

import jax
import ml_dtypes
import numpy as np
import jax.numpy as jnp
from jax import lax
from jax.experimental import pallas as pl
from jax.experimental.pallas import tpu as pltpu
from jax.sharding import Mesh
from jax.sharding import PartitionSpec as P

LAGS = 129
LAG_ROWS = 144
PAIR_BLOCK = 128
BIN_CHUNK = 256
GATHER_CHUNK = 512
SUBS = 2


def whiten(spectra):
    station_count = spectra.shape[0]
    bin_count = spectra.shape[-1]
    ramp_bins = bin_count // 32
    bin_index = jnp.arange(bin_count, dtype=jnp.int32)
    edge_dist = jnp.minimum(bin_index, bin_count - 1 - bin_index).astype(jnp.float32) + 0.5
    ramp_vals = 0.5 - 0.5 * jnp.cos(jnp.pi * edge_dist / ramp_bins)
    taper = jnp.where(edge_dist < ramp_bins, ramp_vals, jnp.ones_like(ramp_vals))
    blocked = spectra.reshape(station_count, 3, 2, bin_count // 64, 64)
    power = jnp.mean(blocked * blocked, axis=(1, 2, 4))
    inverse = 1.0 / jnp.sqrt(power + 1e-05)
    spread_scale = jnp.repeat(inverse, 64, axis=1)
    return (spectra * taper * spread_scale[:, None, None, :]).astype(jnp.bfloat16)


def lag_tables(bin_count):
    lag_index = np.arange(LAGS, dtype=np.int32) - LAGS // 2
    bin_index = np.arange(bin_count, dtype=np.int32)
    phase_steps = lag_index[:, None] * bin_index[None, :] % (2 * bin_count)
    angle = phase_steps.astype(np.float32) * np.float32(np.pi / bin_count)
    pad = ((0, LAG_ROWS - LAGS), (0, 0))
    cos_rows = np.pad(np.cos(angle).astype(np.float32).astype(ml_dtypes.bfloat16), pad)
    sin_rows = np.pad((-np.sin(angle)).astype(np.float32).astype(ml_dtypes.bfloat16), pad)
    return jnp.asarray(cos_rows), jnp.asarray(sin_rows)


def pair_kernel(counts_ref, core_ref, pairs_ref, panel_ref, cos_ref, sin_ref, *rest,
                blocks_per_owner, part_bins, accumulate):
    if accumulate:
        acc_ref, out_ref, f_scr, s_scr = rest
    else:
        out_ref, f_scr, s_scr = rest
    step = pl.program_id(0)
    owner = step // blocks_per_owner
    start = (step % blocks_per_owner) * PAIR_BLOCK
    live = start < counts_ref[owner, 0]
    if accumulate:
        out_ref[...] = acc_ref[...]
    else:
        out_ref[...] = jnp.zeros_like(out_ref)

    @pl.when(live)
    def _():
        rows = panel_ref.shape[0]
        width = panel_ref.shape[1]
        iota = lax.broadcasted_iota(jnp.int32, (rows, PAIR_BLOCK), 0)
        idx = pairs_ref[0]
        pick_first = jnp.where(idx[0:1, :] == iota, 1.0, 0.0).T.astype(jnp.bfloat16)
        pick_second = jnp.where(idx[1:2, :] == iota, 1.0, 0.0).T.astype(jnp.bfloat16)
        gather_chunk = min(GATHER_CHUNK, width)

        def gather(c, carry):
            off = pl.multiple_of(c * gather_chunk, gather_chunk)
            block = panel_ref[:, pl.ds(off, gather_chunk)]
            f_scr[:, pl.ds(off, gather_chunk)] = jnp.dot(
                pick_first, block, preferred_element_type=jnp.float32)
            s_scr[:, pl.ds(off, gather_chunk)] = jnp.dot(
                pick_second, block, preferred_element_type=jnp.float32)
            return carry

        lax.fori_loop(0, width // gather_chunk, gather, 0)
        nt = (((1,), (1,)), ((), ()))
        sub_bins = part_bins // SUBS
        bin_chunk = min(BIN_CHUNK, sub_bins)
        for sub in range(SUBS):
            col0 = sub * 6 * sub_bins

            def chunk(kc, carry):
                off = pl.multiple_of(kc * bin_chunk, bin_chunk)
                cos_blk = cos_ref[:, pl.ds(sub * sub_bins + off, bin_chunk)]
                sin_blk = sin_ref[:, pl.ds(sub * sub_bins + off, bin_chunk)]
                for a in range(3):
                    f_re = f_scr[:, pl.ds(col0 + 2 * a * sub_bins + off, bin_chunk)]
                    f_im = f_scr[:, pl.ds(col0 + (2 * a + 1) * sub_bins + off, bin_chunk)]
                    for b in range(3):
                        s_re = s_scr[:, pl.ds(col0 + 2 * b * sub_bins + off, bin_chunk)]
                        s_im = s_scr[:, pl.ds(col0 + (2 * b + 1) * sub_bins + off, bin_chunk)]
                        real_part = (f_re * s_re + f_im * s_im).astype(jnp.bfloat16)
                        imag_part = (f_im * s_re - f_re * s_im).astype(jnp.bfloat16)
                        acc = lax.dot_general(cos_blk, real_part, nt,
                                              preferred_element_type=jnp.float32)
                        acc = acc + lax.dot_general(sin_blk, imag_part, nt,
                                                    preferred_element_type=jnp.float32)
                        out_ref[0, 3 * a + b] += acc
                return carry

            lax.fori_loop(0, sub_bins // bin_chunk, chunk, 0)
        column = start + lax.broadcasted_iota(jnp.int32, out_ref.shape, 3)
        out_ref[...] = jnp.where(column < counts_ref[owner, 0], out_ref[...], 0.0)


def pair_sums(counts, core_arr, chip_pairs, panel, cos_rows, sin_rows, owners, chunk_id, acc):
    rows, width = panel.shape
    part_bins = width // 6
    pairs = chip_pairs.shape[0] * chip_pairs.shape[2]
    per_owner = pairs // owners
    blocks_per_owner = per_owner // PAIR_BLOCK
    grid = (pairs // PAIR_BLOCK,)
    accumulate = acc is not None
    kernel = functools.partial(pair_kernel, blocks_per_owner=blocks_per_owner,
                               part_bins=part_bins, accumulate=accumulate)
    flops = 2 * pairs * rows * width * 2 + 2 * LAG_ROWS * 2 * part_bins * 9 * pairs
    out_bytes = owners * 9 * LAG_ROWS * per_owner * 4
    cost = pl.CostEstimate(flops=flops, transcendentals=0,
                           bytes_accessed=rows * width * 2 + out_bytes * (2 if accumulate else 1))
    out_spec = pl.BlockSpec(
        (1, 9, LAG_ROWS, PAIR_BLOCK),
        lambda i, c, k: (i // blocks_per_owner, 0, 0, i % blocks_per_owner))
    in_specs = [
        pl.BlockSpec((1, 2, PAIR_BLOCK),
                     lambda i, c, k: (i // blocks_per_owner, 0, i % blocks_per_owner)),
        pl.BlockSpec((rows, width), lambda i, c, k: (0, 0)),
        pl.BlockSpec((LAG_ROWS, part_bins), lambda i, c, k: (0, k[0])),
        pl.BlockSpec((LAG_ROWS, part_bins), lambda i, c, k: (0, k[0])),
    ]
    args = [counts, core_arr, chip_pairs, panel, cos_rows, sin_rows]
    aliases = {}
    if accumulate:
        in_specs.append(out_spec)
        args.append(acc)
        aliases = {len(args) - 1: 0}
    return pl.pallas_call(
        kernel,
        out_shape=jax.ShapeDtypeStruct((owners, 9, LAG_ROWS, per_owner), jnp.float32),
        grid_spec=pltpu.PrefetchScalarGridSpec(
            num_scalar_prefetch=2,
            grid=grid,
            in_specs=in_specs,
            out_specs=out_spec,
            scratch_shapes=[
                pltpu.VMEM((PAIR_BLOCK, width), jnp.float32),
                pltpu.VMEM((PAIR_BLOCK, width), jnp.float32),
            ],
        ),
        input_output_aliases=aliases,
        compiler_params=pltpu.CompilerParams(
            dimension_semantics=("arbitrary",), vmem_limit_bytes=60 * 1024 * 1024),
        cost_estimate=cost,
    )(*args)


MESH_ID = pl.DeviceIdType.MESH


def spread_kernel(pieces_ref, rows_ref, count_ref, panel_ref, chip_rows_ref, chip_count_ref,
                  send_plane, recv_plane,
                  local_sem, send_right, send_left, recv_ring, meta_sems, *, ring_size,
                  plane_size, blk_size, slots, subs):
    me_z = lax.axis_index("z")
    me_c = lax.axis_index("core")
    me_b = lax.axis_index("blk")
    me_q = me_c * blk_size + me_b
    right = (me_z + 1) % ring_size
    left = (me_z + ring_size - 1) % ring_size

    def plane_dev(q):
        return (me_z, q // blk_size, q % blk_size)

    barrier = pltpu.get_barrier_semaphore()

    def greet(i, carry):
        q = (me_q + i) % plane_size
        pl.semaphore_signal(barrier, 1, device_id=plane_dev(q), device_id_type=MESH_ID)
        return carry

    lax.fori_loop(1, plane_size, greet, 0)
    pl.semaphore_signal(barrier, 1, device_id=(right, me_c, me_b), device_id_type=MESH_ID)
    pl.semaphore_signal(barrier, 1, device_id=(left, me_c, me_b), device_id_type=MESH_ID)
    pl.semaphore_wait(barrier, plane_size + 1)

    partner = (me_z, 1 - me_c, me_b)
    meta_copies = []
    for idx, (src, dst) in enumerate(((rows_ref, chip_rows_ref), (count_ref, chip_count_ref))):
        local = pltpu.make_async_copy(src, dst.at[me_c], meta_sems.at[3 * idx])
        local.start()
        remote = pltpu.make_async_remote_copy(
            src, dst.at[me_c], meta_sems.at[3 * idx + 1], meta_sems.at[3 * idx + 2],
            device_id=partner, device_id_type=MESH_ID)
        remote.start()
        arrival = pltpu.make_async_remote_copy(
            src, dst.at[1 - me_c], meta_sems.at[3 * idx + 1], meta_sems.at[3 * idx + 2],
            device_id=partner, device_id_type=MESH_ID)
        meta_copies.append((local, remote, arrival))

    sub_width = panel_ref.shape[1] // subs
    block_rows = plane_size * slots
    half_rows = block_rows // 2
    base = me_z * block_rows
    half = ring_size // 2

    def cols(sub):
        return pl.ds(sub * sub_width, sub_width)

    def rows_of(q, sub):
        return panel_ref.at[pl.ds(base + q * slots, slots), cols(sub)]

    def local_copy(sub):
        return pltpu.make_async_copy(
            pieces_ref.at[me_q, :, cols(sub)], rows_of(me_q, sub), local_sem.at[sub])

    def plane_copy(q, src_q, sub):
        return pltpu.make_async_remote_copy(
            pieces_ref.at[q, :, cols(sub)], rows_of(src_q, sub), send_plane.at[sub, q],
            recv_plane.at[sub, src_q], device_id=plane_dev(q), device_id_type=MESH_ID)

    def scatter(sub):
        local_copy(sub).start()

        def send(i, carry):
            q = (me_q + i) % plane_size
            plane_copy(q, me_q, sub).start()
            return carry

        lax.fori_loop(1, plane_size, send, 0)

    def gathered(sub):
        def arrive(i, carry):
            q = (me_q + plane_size - i) % plane_size
            plane_copy(q, q, sub).wait_recv()
            return carry

        lax.fori_loop(1, plane_size, arrive, 0)
        local_copy(sub).wait()

    def block_of(k, sub):
        return panel_ref.at[pl.ds(k * block_rows, block_rows), cols(sub)]

    def part_of(k, first, sub):
        start = k * block_rows + (0 if first else half_rows)
        return panel_ref.at[pl.ds(start, half_rows), cols(sub)]

    def ring_copy(k, sem, dev, sub):
        return pltpu.make_async_remote_copy(
            block_of(k, sub), block_of(k, sub), sem, recv_ring.at[sub, k],
            device_id=(dev, me_c, me_b), device_id_type=MESH_ID)

    def part_copy(k, first, sem, dev, sub):
        slot = k if first else ring_size
        return pltpu.make_async_remote_copy(
            part_of(k, first, sub), part_of(k, first, sub), sem, recv_ring.at[sub, slot],
            device_id=(dev, me_c, me_b), device_id_type=MESH_ID)

    sends = []

    def ring_step(s, sub):
        k = (me_z + ring_size - s) % ring_size
        if s > 0:
            ring_copy(k, send_right.at[sub, s], left, sub).wait_recv()
        c = ring_copy(k, send_right.at[sub, s], right, sub) if s < half - 1 else part_copy(
            k, True, send_right.at[sub, s], right, sub)
        c.start()
        sends.append(c)
        k = (me_z + s) % ring_size
        if s > 0:
            ring_copy(k, send_left.at[sub, s], right, sub).wait_recv()
        c = ring_copy(k, send_left.at[sub, s], left, sub) if s < half - 1 else part_copy(
            k, False, send_left.at[sub, s], left, sub)
        c.start()
        sends.append(c)

    for sub in range(subs):
        scatter(sub)
        gathered(sub)
        ring_step(0, sub)
    for s in range(1, half):
        for sub in range(subs):
            ring_step(s, sub)
    far = (me_z + half) % ring_size
    for sub in range(subs):
        part_copy(far, True, send_right.at[sub, 0], left, sub).wait_recv()
        part_copy(far, False, send_left.at[sub, 0], right, sub).wait_recv()
    for sub in range(subs):
        def sent(i, carry):
            q = (me_q + i) % plane_size
            plane_copy(q, me_q, sub).wait_send()
            return carry

        lax.fori_loop(1, plane_size, sent, 0)
    for c in sends:
        c.wait_send()
    for local, remote, arrival in meta_copies:
        local.wait()
        arrival.wait_recv()
        remote.wait_send()


def spread(pieces, pair_rows, pair_counts, ring_size, plane_size, blk_size):
    _, slots, width = pieces.shape
    rows = ring_size * plane_size * slots
    kernel = functools.partial(spread_kernel, ring_size=ring_size, plane_size=plane_size,
                               blk_size=blk_size, slots=slots, subs=SUBS)
    half = ring_size // 2
    return pl.pallas_call(
        kernel,
        out_shape=(jax.ShapeDtypeStruct((rows, width), pieces.dtype),
                   jax.ShapeDtypeStruct((2,) + pair_rows.shape, pair_rows.dtype),
                   jax.ShapeDtypeStruct((2,) + pair_counts.shape, pair_counts.dtype)),
        in_specs=[pl.BlockSpec(memory_space=pl.ANY)] * 3,
        out_specs=(pl.BlockSpec(memory_space=pl.ANY),) * 3,
        scratch_shapes=[
            pltpu.SemaphoreType.DMA((SUBS, plane_size)),
            pltpu.SemaphoreType.DMA((SUBS, plane_size)),
            pltpu.SemaphoreType.DMA((SUBS,)),
            pltpu.SemaphoreType.DMA((SUBS, half)),
            pltpu.SemaphoreType.DMA((SUBS, half)),
            pltpu.SemaphoreType.DMA((SUBS, ring_size + 1)),
            pltpu.SemaphoreType.DMA((6,)),
        ],
        compiler_params=pltpu.CompilerParams(collective_id=0, has_side_effects=True),
    )(pieces, pair_rows, pair_counts)


def exchange_kernel(part_ref, out_ref, recv_buf, sems, *, scale):
    me_z = lax.axis_index("z")
    me_c = lax.axis_index("core")
    me_b = lax.axis_index("blk")
    partner = (me_z, 1 - me_c, me_b)
    barrier = pltpu.get_barrier_semaphore()
    pl.semaphore_signal(barrier, 1, device_id=partner, device_id_type=MESH_ID)
    pl.semaphore_wait(barrier, 1)
    copy = pltpu.make_async_remote_copy(
        part_ref.at[1 - me_c], recv_buf, sems.at[0], sems.at[1],
        device_id=partner, device_id_type=MESH_ID)
    copy.start()
    copy.wait()
    out_ref[...] = ((part_ref[me_c] + recv_buf[...]) * scale).astype(out_ref.dtype)


def exchange(partial, scale):
    shape = partial.shape[1:]
    return pl.pallas_call(
        functools.partial(exchange_kernel, scale=scale),
        out_shape=jax.ShapeDtypeStruct(shape, jnp.bfloat16),
        in_specs=[pl.BlockSpec(memory_space=pltpu.VMEM)],
        out_specs=pl.BlockSpec(memory_space=pltpu.VMEM),
        scratch_shapes=[
            pltpu.VMEM(shape, partial.dtype),
            pltpu.SemaphoreType.DMA((2,)),
        ],
        compiler_params=pltpu.CompilerParams(collective_id=1, has_side_effects=True),
    )(partial)


def shards(spectra, send_rows, send_counts, pair_rows, pair_counts):
    whitened = whiten(spectra)
    station_count, comps, parts, bin_count = whitened.shape
    row_width = comps * parts * bin_count
    slot_count = send_rows.shape[2]
    cores = lax.axis_size("core")
    part_bins = bin_count // cores
    core = lax.axis_index("core")

    flat = whitened.reshape(station_count, row_width)
    lists = send_rows[0]
    col_count = lists.shape[0]
    picked = jnp.take(flat, lists.reshape(-1), axis=0).reshape(col_count, slot_count, row_width)
    alive = jnp.arange(slot_count, dtype=jnp.int32)[None, :] < send_counts[0][:, None]
    picked = jnp.where(alive[:, :, None], picked, jnp.zeros_like(picked))
    pieces = picked.reshape(col_count, slot_count, comps * parts, cores, SUBS,
                            part_bins // SUBS)
    pieces = jnp.transpose(pieces, (3, 0, 1, 4, 2, 5)).reshape(
        cores * col_count, slot_count, comps * parts * part_bins)
    pair_total = pair_rows.shape[1]
    panel, chip_pairs, chip_counts = spread(pieces, pair_rows, pair_counts, lax.axis_size("z"),
                                            cores * col_count, col_count)
    cos_rows, sin_rows = lag_tables(bin_count)
    core_arr = core.astype(jnp.int32)[None]
    partial = pair_sums(chip_counts, core_arr, chip_pairs, panel, cos_rows, sin_rows, cores, 0,
                        None)
    total = exchange(partial, 1.0 / math.sqrt(bin_count))[:, :LAGS, :]
    return jnp.transpose(total, (1, 0, 2))


def solution(mesh):
    tile_size = mesh.shape["tile"]
    blk_size = mesh.shape["blk"]
    split = Mesh(mesh.devices.reshape(tile_size // 2, 2, blk_size), ("z", "core", "blk"))
    dev = ("z", "core", "blk")
    return jax.shard_map(
        shards,
        mesh=split,
        in_specs=(
            P(dev, None, None, None),
            P(dev, None, None),
            P(dev, None),
            P(None, dev),
            P(dev),
        ),
        out_specs=P(None, None, dev),
        check_vma=False,
    )
```

```python
import functools
import math

import jax
import ml_dtypes
import numpy as np
import jax.numpy as jnp
from jax import lax
from jax.experimental import pallas as pl
from jax.experimental.pallas import tpu as pltpu
from jax.sharding import Mesh
from jax.sharding import PartitionSpec as P

LAGS = 129
LAG_ROWS = 144
PAIR_BLOCK = 128
BIN_CHUNK = 256
GATHER_CHUNK = 512
SUBS = 2


def whiten(spectra):
    station_count = spectra.shape[0]
    bin_count = spectra.shape[-1]
    ramp_bins = bin_count // 32
    bin_index = jnp.arange(bin_count, dtype=jnp.int32)
    edge_dist = jnp.minimum(bin_index, bin_count - 1 - bin_index).astype(jnp.float32) + 0.5
    ramp_vals = 0.5 - 0.5 * jnp.cos(jnp.pi * edge_dist / ramp_bins)
    taper = jnp.where(edge_dist < ramp_bins, ramp_vals, jnp.ones_like(ramp_vals))
    blocked = spectra.reshape(station_count, 3, 2, bin_count // 64, 64)
    power = jnp.mean(blocked * blocked, axis=(1, 2, 4))
    inverse = 1.0 / jnp.sqrt(power + 1e-05)
    spread_scale = jnp.repeat(inverse, 64, axis=1)
    return (spectra * taper * spread_scale[:, None, None, :]).astype(jnp.bfloat16)


def lag_tables(bin_count):
    lag_index = np.arange(LAGS, dtype=np.int32) - LAGS // 2
    bin_index = np.arange(bin_count, dtype=np.int32)
    phase_steps = lag_index[:, None] * bin_index[None, :] % (2 * bin_count)
    angle = phase_steps.astype(np.float32) * np.float32(np.pi / bin_count)
    pad = ((0, LAG_ROWS - LAGS), (0, 0))
    cos_rows = np.pad(np.cos(angle).astype(np.float32).astype(ml_dtypes.bfloat16), pad)
    sin_rows = np.pad((-np.sin(angle)).astype(np.float32).astype(ml_dtypes.bfloat16), pad)
    chunks = bin_count // BIN_CHUNK
    both = np.stack([cos_rows.reshape(LAG_ROWS, chunks, BIN_CHUNK),
                     sin_rows.reshape(LAG_ROWS, chunks, BIN_CHUNK)], axis=2)
    return jnp.asarray(both.reshape(LAG_ROWS, 2 * bin_count))


def pair_kernel(counts_ref, core_ref, pairs_ref, panel_ref, lag_ref, *rest,
                blocks_per_owner, part_bins, accumulate):
    if accumulate:
        acc_ref, out_ref, f_scr, s_scr = rest
    else:
        out_ref, f_scr, s_scr = rest
    step = pl.program_id(0)
    owner = step // blocks_per_owner
    start = (step % blocks_per_owner) * PAIR_BLOCK
    live = start < counts_ref[owner, 0]
    if accumulate:
        out_ref[...] = acc_ref[...]
    else:
        out_ref[...] = jnp.zeros_like(out_ref)

    @pl.when(live)
    def _():
        rows = panel_ref.shape[0]
        width = panel_ref.shape[1]
        iota = lax.broadcasted_iota(jnp.int32, (rows, PAIR_BLOCK), 0)
        idx = pairs_ref[0]
        pick_first = jnp.where(idx[0:1, :] == iota, 1.0, 0.0).T.astype(jnp.bfloat16)
        pick_second = jnp.where(idx[1:2, :] == iota, 1.0, 0.0).T.astype(jnp.bfloat16)
        gather_chunk = min(GATHER_CHUNK, width)

        def gather(c, carry):
            off = pl.multiple_of(c * gather_chunk, gather_chunk)
            block = panel_ref[:, pl.ds(off, gather_chunk)]
            f_scr[:, pl.ds(off, gather_chunk)] = jnp.dot(
                pick_first, block, preferred_element_type=jnp.float32)
            s_scr[:, pl.ds(off, gather_chunk)] = jnp.dot(
                pick_second, block, preferred_element_type=jnp.float32)
            return carry

        lax.fori_loop(0, width // gather_chunk, gather, 0)
        nt = (((1,), (1,)), ((), ()))
        sub_bins = part_bins // SUBS
        bin_chunk = min(BIN_CHUNK, sub_bins)
        for sub in range(SUBS):
            col0 = sub * 6 * sub_bins

            def chunk(kc, carry):
                off = pl.multiple_of(kc * bin_chunk, bin_chunk)
                lag_blk = lag_ref[:, pl.ds(2 * (sub * sub_bins + off), 2 * bin_chunk)]
                for a in range(3):
                    f_re = f_scr[:, pl.ds(col0 + 2 * a * sub_bins + off, bin_chunk)]
                    f_im = f_scr[:, pl.ds(col0 + (2 * a + 1) * sub_bins + off, bin_chunk)]
                    for b in range(3):
                        s_re = s_scr[:, pl.ds(col0 + 2 * b * sub_bins + off, bin_chunk)]
                        s_im = s_scr[:, pl.ds(col0 + (2 * b + 1) * sub_bins + off, bin_chunk)]
                        real_part = (f_re * s_re + f_im * s_im).astype(jnp.bfloat16)
                        imag_part = (f_im * s_re - f_re * s_im).astype(jnp.bfloat16)
                        both = jnp.concatenate([real_part, imag_part], axis=1)
                        acc = lax.dot_general(lag_blk, both, nt,
                                              preferred_element_type=jnp.float32)
                        out_ref[0, 3 * a + b] += acc
                return carry

            lax.fori_loop(0, sub_bins // bin_chunk, chunk, 0)
        column = start + lax.broadcasted_iota(jnp.int32, out_ref.shape, 3)
        out_ref[...] = jnp.where(column < counts_ref[owner, 0], out_ref[...], 0.0)


def pair_sums(counts, core_arr, chip_pairs, panel, lag_rows, owners, chunk_id, acc):
    rows, width = panel.shape
    part_bins = width // 6
    pairs = chip_pairs.shape[0] * chip_pairs.shape[2]
    per_owner = pairs // owners
    blocks_per_owner = per_owner // PAIR_BLOCK
    grid = (pairs // PAIR_BLOCK,)
    accumulate = acc is not None
    kernel = functools.partial(pair_kernel, blocks_per_owner=blocks_per_owner,
                               part_bins=part_bins, accumulate=accumulate)
    flops = 2 * pairs * rows * width * 2 + 2 * LAG_ROWS * 2 * part_bins * 9 * pairs
    out_bytes = owners * 9 * LAG_ROWS * per_owner * 4
    cost = pl.CostEstimate(flops=flops, transcendentals=0,
                           bytes_accessed=rows * width * 2 + out_bytes * (2 if accumulate else 1))
    out_spec = pl.BlockSpec(
        (1, 9, LAG_ROWS, PAIR_BLOCK),
        lambda i, c, k: (i // blocks_per_owner, 0, 0, i % blocks_per_owner))
    in_specs = [
        pl.BlockSpec((1, 2, PAIR_BLOCK),
                     lambda i, c, k: (i // blocks_per_owner, 0, i % blocks_per_owner)),
        pl.BlockSpec((rows, width), lambda i, c, k: (0, 0)),
        pl.BlockSpec((LAG_ROWS, 2 * part_bins), lambda i, c, k: (0, k[0])),
    ]
    args = [counts, core_arr, chip_pairs, panel, lag_rows]
    aliases = {}
    if accumulate:
        in_specs.append(out_spec)
        args.append(acc)
        aliases = {len(args) - 1: 0}
    return pl.pallas_call(
        kernel,
        out_shape=jax.ShapeDtypeStruct((owners, 9, LAG_ROWS, per_owner), jnp.float32),
        grid_spec=pltpu.PrefetchScalarGridSpec(
            num_scalar_prefetch=2,
            grid=grid,
            in_specs=in_specs,
            out_specs=out_spec,
            scratch_shapes=[
                pltpu.VMEM((PAIR_BLOCK, width), jnp.float32),
                pltpu.VMEM((PAIR_BLOCK, width), jnp.float32),
            ],
        ),
        input_output_aliases=aliases,
        compiler_params=pltpu.CompilerParams(
            dimension_semantics=("arbitrary",), vmem_limit_bytes=60 * 1024 * 1024),
        cost_estimate=cost,
    )(*args)


MESH_ID = pl.DeviceIdType.MESH


def spread_kernel(pieces_ref, rows_ref, count_ref, panel_ref, chip_rows_ref, chip_count_ref,
                  send_plane, recv_plane,
                  local_sem, send_right, send_left, recv_ring, meta_sems, *, ring_size,
                  plane_size, blk_size, slots, subs):
    me_z = lax.axis_index("z")
    me_c = lax.axis_index("core")
    me_b = lax.axis_index("blk")
    me_q = me_c * blk_size + me_b
    right = (me_z + 1) % ring_size
    left = (me_z + ring_size - 1) % ring_size

    def plane_dev(q):
        return (me_z, q // blk_size, q % blk_size)

    barrier = pltpu.get_barrier_semaphore()

    def greet(i, carry):
        q = (me_q + i) % plane_size
        pl.semaphore_signal(barrier, 1, device_id=plane_dev(q), device_id_type=MESH_ID)
        return carry

    lax.fori_loop(1, plane_size, greet, 0)
    pl.semaphore_signal(barrier, 1, device_id=(right, me_c, me_b), device_id_type=MESH_ID)
    pl.semaphore_signal(barrier, 1, device_id=(left, me_c, me_b), device_id_type=MESH_ID)
    pl.semaphore_wait(barrier, plane_size + 1)

    partner = (me_z, 1 - me_c, me_b)
    meta_copies = []
    for idx, (src, dst) in enumerate(((rows_ref, chip_rows_ref), (count_ref, chip_count_ref))):
        local = pltpu.make_async_copy(src, dst.at[me_c], meta_sems.at[3 * idx])
        local.start()
        remote = pltpu.make_async_remote_copy(
            src, dst.at[me_c], meta_sems.at[3 * idx + 1], meta_sems.at[3 * idx + 2],
            device_id=partner, device_id_type=MESH_ID)
        remote.start()
        arrival = pltpu.make_async_remote_copy(
            src, dst.at[1 - me_c], meta_sems.at[3 * idx + 1], meta_sems.at[3 * idx + 2],
            device_id=partner, device_id_type=MESH_ID)
        meta_copies.append((local, remote, arrival))

    sub_width = panel_ref.shape[1] // subs
    block_rows = plane_size * slots
    half_rows = block_rows // 2
    base = me_z * block_rows
    half = ring_size // 2

    def cols(sub):
        return pl.ds(sub * sub_width, sub_width)

    def rows_of(q, sub):
        return panel_ref.at[pl.ds(base + q * slots, slots), cols(sub)]

    def local_copy(sub):
        return pltpu.make_async_copy(
            pieces_ref.at[me_q, :, cols(sub)], rows_of(me_q, sub), local_sem.at[sub])

    def plane_copy(q, src_q, sub):
        return pltpu.make_async_remote_copy(
            pieces_ref.at[q, :, cols(sub)], rows_of(src_q, sub), send_plane.at[sub, q],
            recv_plane.at[sub, src_q], device_id=plane_dev(q), device_id_type=MESH_ID)

    def scatter(sub):
        local_copy(sub).start()

        def send(i, carry):
            q = (me_q + i) % plane_size
            plane_copy(q, me_q, sub).start()
            return carry

        lax.fori_loop(1, plane_size, send, 0)

    def gathered(sub):
        def arrive(i, carry):
            q = (me_q + plane_size - i) % plane_size
            plane_copy(q, q, sub).wait_recv()
            return carry

        lax.fori_loop(1, plane_size, arrive, 0)
        local_copy(sub).wait()

    def block_of(k, sub):
        return panel_ref.at[pl.ds(k * block_rows, block_rows), cols(sub)]

    def part_of(k, first, sub):
        start = k * block_rows + (0 if first else half_rows)
        return panel_ref.at[pl.ds(start, half_rows), cols(sub)]

    def ring_copy(k, sem, dev, sub):
        return pltpu.make_async_remote_copy(
            block_of(k, sub), block_of(k, sub), sem, recv_ring.at[sub, k],
            device_id=(dev, me_c, me_b), device_id_type=MESH_ID)

    def part_copy(k, first, sem, dev, sub):
        slot = k if first else ring_size
        return pltpu.make_async_remote_copy(
            part_of(k, first, sub), part_of(k, first, sub), sem, recv_ring.at[sub, slot],
            device_id=(dev, me_c, me_b), device_id_type=MESH_ID)

    sends = []

    def ring_step(s, sub):
        k = (me_z + ring_size - s) % ring_size
        if s > 0:
            ring_copy(k, send_right.at[sub, s], left, sub).wait_recv()
        c = ring_copy(k, send_right.at[sub, s], right, sub) if s < half - 1 else part_copy(
            k, True, send_right.at[sub, s], right, sub)
        c.start()
        sends.append(c)
        k = (me_z + s) % ring_size
        if s > 0:
            ring_copy(k, send_left.at[sub, s], right, sub).wait_recv()
        c = ring_copy(k, send_left.at[sub, s], left, sub) if s < half - 1 else part_copy(
            k, False, send_left.at[sub, s], left, sub)
        c.start()
        sends.append(c)

    for sub in range(subs):
        scatter(sub)
        gathered(sub)
        ring_step(0, sub)
    for s in range(1, half):
        for sub in range(subs):
            ring_step(s, sub)
    far = (me_z + half) % ring_size
    for sub in range(subs):
        part_copy(far, True, send_right.at[sub, 0], left, sub).wait_recv()
        part_copy(far, False, send_left.at[sub, 0], right, sub).wait_recv()
    for sub in range(subs):
        def sent(i, carry):
            q = (me_q + i) % plane_size
            plane_copy(q, me_q, sub).wait_send()
            return carry

        lax.fori_loop(1, plane_size, sent, 0)
    for c in sends:
        c.wait_send()
    for local, remote, arrival in meta_copies:
        local.wait()
        arrival.wait_recv()
        remote.wait_send()


def spread(pieces, pair_rows, pair_counts, ring_size, plane_size, blk_size):
    _, slots, width = pieces.shape
    rows = ring_size * plane_size * slots
    kernel = functools.partial(spread_kernel, ring_size=ring_size, plane_size=plane_size,
                               blk_size=blk_size, slots=slots, subs=SUBS)
    half = ring_size // 2
    return pl.pallas_call(
        kernel,
        out_shape=(jax.ShapeDtypeStruct((rows, width), pieces.dtype),
                   jax.ShapeDtypeStruct((2,) + pair_rows.shape, pair_rows.dtype),
                   jax.ShapeDtypeStruct((2,) + pair_counts.shape, pair_counts.dtype)),
        in_specs=[pl.BlockSpec(memory_space=pl.ANY)] * 3,
        out_specs=(pl.BlockSpec(memory_space=pl.ANY),) * 3,
        scratch_shapes=[
            pltpu.SemaphoreType.DMA((SUBS, plane_size)),
            pltpu.SemaphoreType.DMA((SUBS, plane_size)),
            pltpu.SemaphoreType.DMA((SUBS,)),
            pltpu.SemaphoreType.DMA((SUBS, half)),
            pltpu.SemaphoreType.DMA((SUBS, half)),
            pltpu.SemaphoreType.DMA((SUBS, ring_size + 1)),
            pltpu.SemaphoreType.DMA((6,)),
        ],
        compiler_params=pltpu.CompilerParams(collective_id=0, has_side_effects=True),
    )(pieces, pair_rows, pair_counts)


def exchange_kernel(part_ref, out_ref, recv_buf, sems, *, scale):
    me_z = lax.axis_index("z")
    me_c = lax.axis_index("core")
    me_b = lax.axis_index("blk")
    partner = (me_z, 1 - me_c, me_b)
    barrier = pltpu.get_barrier_semaphore()
    pl.semaphore_signal(barrier, 1, device_id=partner, device_id_type=MESH_ID)
    pl.semaphore_wait(barrier, 1)
    copy = pltpu.make_async_remote_copy(
        part_ref.at[1 - me_c], recv_buf, sems.at[0], sems.at[1],
        device_id=partner, device_id_type=MESH_ID)
    copy.start()
    copy.wait()
    out_ref[...] = ((part_ref[me_c] + recv_buf[...]) * scale).astype(out_ref.dtype)


def exchange(partial, scale):
    shape = partial.shape[1:]
    return pl.pallas_call(
        functools.partial(exchange_kernel, scale=scale),
        out_shape=jax.ShapeDtypeStruct(shape, jnp.bfloat16),
        in_specs=[pl.BlockSpec(memory_space=pltpu.VMEM)],
        out_specs=pl.BlockSpec(memory_space=pltpu.VMEM),
        scratch_shapes=[
            pltpu.VMEM(shape, partial.dtype),
            pltpu.SemaphoreType.DMA((2,)),
        ],
        compiler_params=pltpu.CompilerParams(collective_id=1, has_side_effects=True),
    )(partial)


def shards(spectra, send_rows, send_counts, pair_rows, pair_counts):
    whitened = whiten(spectra)
    station_count, comps, parts, bin_count = whitened.shape
    row_width = comps * parts * bin_count
    slot_count = send_rows.shape[2]
    cores = lax.axis_size("core")
    part_bins = bin_count // cores
    core = lax.axis_index("core")

    flat = whitened.reshape(station_count, row_width)
    lists = send_rows[0]
    col_count = lists.shape[0]
    picked = jnp.take(flat, lists.reshape(-1), axis=0).reshape(col_count, slot_count, row_width)
    alive = jnp.arange(slot_count, dtype=jnp.int32)[None, :] < send_counts[0][:, None]
    picked = jnp.where(alive[:, :, None], picked, jnp.zeros_like(picked))
    pieces = picked.reshape(col_count, slot_count, comps * parts, cores, SUBS,
                            part_bins // SUBS)
    pieces = jnp.transpose(pieces, (3, 0, 1, 4, 2, 5)).reshape(
        cores * col_count, slot_count, comps * parts * part_bins)
    pair_total = pair_rows.shape[1]
    panel, chip_pairs, chip_counts = spread(pieces, pair_rows, pair_counts, lax.axis_size("z"),
                                            cores * col_count, col_count)
    lag_rows = lag_tables(bin_count)
    core_arr = core.astype(jnp.int32)[None]
    partial = pair_sums(chip_counts, core_arr, chip_pairs, panel, lag_rows, cores, 0, None)
    total = exchange(partial, 1.0 / math.sqrt(bin_count))[:, :LAGS, :]
    return jnp.transpose(total, (1, 0, 2))


def solution(mesh):
    tile_size = mesh.shape["tile"]
    blk_size = mesh.shape["blk"]
    split = Mesh(mesh.devices.reshape(tile_size // 2, 2, blk_size), ("z", "core", "blk"))
    dev = ("z", "core", "blk")
    return jax.shard_map(
        shards,
        mesh=split,
        in_specs=(
            P(dev, None, None, None),
            P(dev, None, None),
            P(dev, None),
            P(None, dev),
            P(dev),
        ),
        out_specs=P(None, None, dev),
        check_vma=False,
    )
```

```python
import functools
import math

import jax
import ml_dtypes
import numpy as np
import jax.numpy as jnp
from jax import lax
from jax.experimental import pallas as pl
from jax.experimental.pallas import tpu as pltpu
from jax.sharding import Mesh
from jax.sharding import PartitionSpec as P

LAGS = 129
LAG_ROWS = 144
PAIR_BLOCK = 128
BIN_CHUNK = 256
GATHER_CHUNK = 512
SUBS = 2


def whiten(spectra):
    station_count = spectra.shape[0]
    bin_count = spectra.shape[-1]
    ramp_bins = bin_count // 32
    bin_index = jnp.arange(bin_count, dtype=jnp.int32)
    edge_dist = jnp.minimum(bin_index, bin_count - 1 - bin_index).astype(jnp.float32) + 0.5
    ramp_vals = 0.5 - 0.5 * jnp.cos(jnp.pi * edge_dist / ramp_bins)
    taper = jnp.where(edge_dist < ramp_bins, ramp_vals, jnp.ones_like(ramp_vals))
    blocked = spectra.reshape(station_count, 3, 2, bin_count // 64, 64)
    power = jnp.mean(blocked * blocked, axis=(1, 2, 4))
    inverse = 1.0 / jnp.sqrt(power + 1e-05)
    spread_scale = jnp.repeat(inverse, 64, axis=1)
    return (spectra * taper * spread_scale[:, None, None, :]).astype(jnp.bfloat16)


def lag_tables(bin_count):
    lag_index = np.arange(LAGS, dtype=np.int32) - LAGS // 2
    bin_index = np.arange(bin_count, dtype=np.int32)
    phase_steps = lag_index[:, None] * bin_index[None, :] % (2 * bin_count)
    angle = phase_steps.astype(np.float32) * np.float32(np.pi / bin_count)
    pad = ((0, LAG_ROWS - LAGS), (0, 0))
    cos_rows = np.pad(np.cos(angle).astype(np.float32).astype(ml_dtypes.bfloat16), pad)
    sin_rows = np.pad((-np.sin(angle)).astype(np.float32).astype(ml_dtypes.bfloat16), pad)
    chunks = bin_count // BIN_CHUNK
    both = np.stack([cos_rows.reshape(LAG_ROWS, chunks, BIN_CHUNK),
                     sin_rows.reshape(LAG_ROWS, chunks, BIN_CHUNK)], axis=2)
    return jnp.asarray(both.reshape(LAG_ROWS, 2 * bin_count))


def pair_kernel(counts_ref, core_ref, pairs_ref, panel_ref, lag_ref, *rest,
                blocks_per_owner, part_bins, accumulate):
    if accumulate:
        acc_ref, out_ref, f_scr, s_scr = rest
    else:
        out_ref, f_scr, s_scr = rest
    step = pl.program_id(0)
    owner = step // blocks_per_owner
    start = (step % blocks_per_owner) * PAIR_BLOCK
    live = start < counts_ref[owner, 0]
    if accumulate:
        out_ref[...] = acc_ref[...]
    else:
        out_ref[...] = jnp.zeros_like(out_ref)

    @pl.when(live)
    def _():
        rows = panel_ref.shape[0]
        width = panel_ref.shape[1]
        iota = lax.broadcasted_iota(jnp.int32, (rows, PAIR_BLOCK), 0)
        idx = pairs_ref[0]
        pick_first = jnp.where(idx[0:1, :] == iota, 1.0, 0.0).T.astype(jnp.bfloat16)
        pick_second = jnp.where(idx[1:2, :] == iota, 1.0, 0.0).T.astype(jnp.bfloat16)
        pick = jnp.concatenate([pick_first, pick_second], axis=0)
        gather_chunk = min(GATHER_CHUNK, width)

        def gather(c, carry):
            off = pl.multiple_of(c * gather_chunk, gather_chunk)
            block = panel_ref[:, pl.ds(off, gather_chunk)]
            both = jnp.dot(pick, block, preferred_element_type=jnp.float32)
            f_scr[:, pl.ds(off, gather_chunk)] = both[:PAIR_BLOCK]
            s_scr[:, pl.ds(off, gather_chunk)] = both[PAIR_BLOCK:]
            return carry

        lax.fori_loop(0, width // gather_chunk, gather, 0)
        nt = (((1,), (1,)), ((), ()))
        sub_bins = part_bins // SUBS
        bin_chunk = min(BIN_CHUNK, sub_bins)
        for sub in range(SUBS):
            col0 = sub * 6 * sub_bins

            def chunk(kc, carry):
                off = pl.multiple_of(kc * bin_chunk, bin_chunk)
                lag_blk = lag_ref[:, pl.ds(2 * (sub * sub_bins + off), 2 * bin_chunk)]
                for a in range(3):
                    f_re = f_scr[:, pl.ds(col0 + 2 * a * sub_bins + off, bin_chunk)]
                    f_im = f_scr[:, pl.ds(col0 + (2 * a + 1) * sub_bins + off, bin_chunk)]
                    for b in range(3):
                        s_re = s_scr[:, pl.ds(col0 + 2 * b * sub_bins + off, bin_chunk)]
                        s_im = s_scr[:, pl.ds(col0 + (2 * b + 1) * sub_bins + off, bin_chunk)]
                        real_part = (f_re * s_re + f_im * s_im).astype(jnp.bfloat16)
                        imag_part = (f_im * s_re - f_re * s_im).astype(jnp.bfloat16)
                        both = jnp.concatenate([real_part, imag_part], axis=1)
                        acc = lax.dot_general(lag_blk, both, nt,
                                              preferred_element_type=jnp.float32)
                        out_ref[0, 3 * a + b] += acc
                return carry

            lax.fori_loop(0, sub_bins // bin_chunk, chunk, 0)
        column = start + lax.broadcasted_iota(jnp.int32, out_ref.shape, 3)
        out_ref[...] = jnp.where(column < counts_ref[owner, 0], out_ref[...], 0.0)


def pair_sums(counts, core_arr, chip_pairs, panel, lag_rows, owners, chunk_id, acc):
    rows, width = panel.shape
    part_bins = width // 6
    pairs = chip_pairs.shape[0] * chip_pairs.shape[2]
    per_owner = pairs // owners
    blocks_per_owner = per_owner // PAIR_BLOCK
    grid = (pairs // PAIR_BLOCK,)
    accumulate = acc is not None
    kernel = functools.partial(pair_kernel, blocks_per_owner=blocks_per_owner,
                               part_bins=part_bins, accumulate=accumulate)
    flops = 2 * pairs * rows * width * 2 + 2 * LAG_ROWS * 2 * part_bins * 9 * pairs
    out_bytes = owners * 9 * LAG_ROWS * per_owner * 4
    cost = pl.CostEstimate(flops=flops, transcendentals=0,
                           bytes_accessed=rows * width * 2 + out_bytes * (2 if accumulate else 1))
    out_spec = pl.BlockSpec(
        (1, 9, LAG_ROWS, PAIR_BLOCK),
        lambda i, c, k: (i // blocks_per_owner, 0, 0, i % blocks_per_owner))
    in_specs = [
        pl.BlockSpec((1, 2, PAIR_BLOCK),
                     lambda i, c, k: (i // blocks_per_owner, 0, i % blocks_per_owner)),
        pl.BlockSpec((rows, width), lambda i, c, k: (0, 0)),
        pl.BlockSpec((LAG_ROWS, 2 * part_bins), lambda i, c, k: (0, k[0])),
    ]
    args = [counts, core_arr, chip_pairs, panel, lag_rows]
    aliases = {}
    if accumulate:
        in_specs.append(out_spec)
        args.append(acc)
        aliases = {len(args) - 1: 0}
    return pl.pallas_call(
        kernel,
        out_shape=jax.ShapeDtypeStruct((owners, 9, LAG_ROWS, per_owner), jnp.float32),
        grid_spec=pltpu.PrefetchScalarGridSpec(
            num_scalar_prefetch=2,
            grid=grid,
            in_specs=in_specs,
            out_specs=out_spec,
            scratch_shapes=[
                pltpu.VMEM((PAIR_BLOCK, width), jnp.float32),
                pltpu.VMEM((PAIR_BLOCK, width), jnp.float32),
            ],
        ),
        input_output_aliases=aliases,
        compiler_params=pltpu.CompilerParams(
            dimension_semantics=("arbitrary",), vmem_limit_bytes=60 * 1024 * 1024),
        cost_estimate=cost,
    )(*args)


MESH_ID = pl.DeviceIdType.MESH


def spread_kernel(pieces_ref, rows_ref, count_ref, panel_ref, chip_rows_ref, chip_count_ref,
                  send_plane, recv_plane,
                  local_sem, send_right, send_left, recv_ring, meta_sems, *, ring_size,
                  plane_size, blk_size, slots, subs):
    me_z = lax.axis_index("z")
    me_c = lax.axis_index("core")
    me_b = lax.axis_index("blk")
    me_q = me_c * blk_size + me_b
    right = (me_z + 1) % ring_size
    left = (me_z + ring_size - 1) % ring_size

    def plane_dev(q):
        return (me_z, q // blk_size, q % blk_size)

    barrier = pltpu.get_barrier_semaphore()

    def greet(i, carry):
        q = (me_q + i) % plane_size
        pl.semaphore_signal(barrier, 1, device_id=plane_dev(q), device_id_type=MESH_ID)
        return carry

    lax.fori_loop(1, plane_size, greet, 0)
    pl.semaphore_signal(barrier, 1, device_id=(right, me_c, me_b), device_id_type=MESH_ID)
    pl.semaphore_signal(barrier, 1, device_id=(left, me_c, me_b), device_id_type=MESH_ID)
    pl.semaphore_wait(barrier, plane_size + 1)

    partner = (me_z, 1 - me_c, me_b)
    meta_copies = []
    for idx, (src, dst) in enumerate(((rows_ref, chip_rows_ref), (count_ref, chip_count_ref))):
        local = pltpu.make_async_copy(src, dst.at[me_c], meta_sems.at[3 * idx])
        local.start()
        remote = pltpu.make_async_remote_copy(
            src, dst.at[me_c], meta_sems.at[3 * idx + 1], meta_sems.at[3 * idx + 2],
            device_id=partner, device_id_type=MESH_ID)
        remote.start()
        arrival = pltpu.make_async_remote_copy(
            src, dst.at[1 - me_c], meta_sems.at[3 * idx + 1], meta_sems.at[3 * idx + 2],
            device_id=partner, device_id_type=MESH_ID)
        meta_copies.append((local, remote, arrival))

    sub_width = panel_ref.shape[1] // subs
    block_rows = plane_size * slots
    half_rows = block_rows // 2
    base = me_z * block_rows
    half = ring_size // 2

    def cols(sub):
        return pl.ds(sub * sub_width, sub_width)

    def rows_of(q, sub):
        return panel_ref.at[pl.ds(base + q * slots, slots), cols(sub)]

    def local_copy(sub):
        return pltpu.make_async_copy(
            pieces_ref.at[me_q, :, cols(sub)], rows_of(me_q, sub), local_sem.at[sub])

    def plane_copy(q, src_q, sub):
        return pltpu.make_async_remote_copy(
            pieces_ref.at[q, :, cols(sub)], rows_of(src_q, sub), send_plane.at[sub, q],
            recv_plane.at[sub, src_q], device_id=plane_dev(q), device_id_type=MESH_ID)

    def scatter(sub):
        local_copy(sub).start()

        def send(i, carry):
            q = (me_q + i) % plane_size
            plane_copy(q, me_q, sub).start()
            return carry

        lax.fori_loop(1, plane_size, send, 0)

    def gathered(sub):
        def arrive(i, carry):
            q = (me_q + plane_size - i) % plane_size
            plane_copy(q, q, sub).wait_recv()
            return carry

        lax.fori_loop(1, plane_size, arrive, 0)
        local_copy(sub).wait()

    def block_of(k, sub):
        return panel_ref.at[pl.ds(k * block_rows, block_rows), cols(sub)]

    def part_of(k, first, sub):
        start = k * block_rows + (0 if first else half_rows)
        return panel_ref.at[pl.ds(start, half_rows), cols(sub)]

    def ring_copy(k, sem, dev, sub):
        return pltpu.make_async_remote_copy(
            block_of(k, sub), block_of(k, sub), sem, recv_ring.at[sub, k],
            device_id=(dev, me_c, me_b), device_id_type=MESH_ID)

    def part_copy(k, first, sem, dev, sub):
        slot = k if first else ring_size
        return pltpu.make_async_remote_copy(
            part_of(k, first, sub), part_of(k, first, sub), sem, recv_ring.at[sub, slot],
            device_id=(dev, me_c, me_b), device_id_type=MESH_ID)

    sends = []

    def ring_step(s, sub):
        k = (me_z + ring_size - s) % ring_size
        if s > 0:
            ring_copy(k, send_right.at[sub, s], left, sub).wait_recv()
        c = ring_copy(k, send_right.at[sub, s], right, sub) if s < half - 1 else part_copy(
            k, True, send_right.at[sub, s], right, sub)
        c.start()
        sends.append(c)
        k = (me_z + s) % ring_size
        if s > 0:
            ring_copy(k, send_left.at[sub, s], right, sub).wait_recv()
        c = ring_copy(k, send_left.at[sub, s], left, sub) if s < half - 1 else part_copy(
            k, False, send_left.at[sub, s], left, sub)
        c.start()
        sends.append(c)

    for sub in range(subs):
        scatter(sub)
        gathered(sub)
        ring_step(0, sub)
    for s in range(1, half):
        for sub in range(subs):
            ring_step(s, sub)
    far = (me_z + half) % ring_size
    for sub in range(subs):
        part_copy(far, True, send_right.at[sub, 0], left, sub).wait_recv()
        part_copy(far, False, send_left.at[sub, 0], right, sub).wait_recv()
    for sub in range(subs):
        def sent(i, carry):
            q = (me_q + i) % plane_size
            plane_copy(q, me_q, sub).wait_send()
            return carry

        lax.fori_loop(1, plane_size, sent, 0)
    for c in sends:
        c.wait_send()
    for local, remote, arrival in meta_copies:
        local.wait()
        arrival.wait_recv()
        remote.wait_send()


def spread(pieces, pair_rows, pair_counts, ring_size, plane_size, blk_size):
    _, slots, width = pieces.shape
    rows = ring_size * plane_size * slots
    kernel = functools.partial(spread_kernel, ring_size=ring_size, plane_size=plane_size,
                               blk_size=blk_size, slots=slots, subs=SUBS)
    half = ring_size // 2
    return pl.pallas_call(
        kernel,
        out_shape=(jax.ShapeDtypeStruct((rows, width), pieces.dtype),
                   jax.ShapeDtypeStruct((2,) + pair_rows.shape, pair_rows.dtype),
                   jax.ShapeDtypeStruct((2,) + pair_counts.shape, pair_counts.dtype)),
        in_specs=[pl.BlockSpec(memory_space=pl.ANY)] * 3,
        out_specs=(pl.BlockSpec(memory_space=pl.ANY),) * 3,
        scratch_shapes=[
            pltpu.SemaphoreType.DMA((SUBS, plane_size)),
            pltpu.SemaphoreType.DMA((SUBS, plane_size)),
            pltpu.SemaphoreType.DMA((SUBS,)),
            pltpu.SemaphoreType.DMA((SUBS, half)),
            pltpu.SemaphoreType.DMA((SUBS, half)),
            pltpu.SemaphoreType.DMA((SUBS, ring_size + 1)),
            pltpu.SemaphoreType.DMA((6,)),
        ],
        compiler_params=pltpu.CompilerParams(collective_id=0, has_side_effects=True),
    )(pieces, pair_rows, pair_counts)


def exchange_kernel(part_ref, out_ref, recv_buf, sems, *, scale):
    me_z = lax.axis_index("z")
    me_c = lax.axis_index("core")
    me_b = lax.axis_index("blk")
    partner = (me_z, 1 - me_c, me_b)
    barrier = pltpu.get_barrier_semaphore()
    pl.semaphore_signal(barrier, 1, device_id=partner, device_id_type=MESH_ID)
    pl.semaphore_wait(barrier, 1)
    copy = pltpu.make_async_remote_copy(
        part_ref.at[1 - me_c], recv_buf, sems.at[0], sems.at[1],
        device_id=partner, device_id_type=MESH_ID)
    copy.start()
    copy.wait()
    out_ref[...] = ((part_ref[me_c] + recv_buf[...]) * scale).astype(out_ref.dtype)


def exchange(partial, scale):
    shape = partial.shape[1:]
    return pl.pallas_call(
        functools.partial(exchange_kernel, scale=scale),
        out_shape=jax.ShapeDtypeStruct(shape, jnp.bfloat16),
        in_specs=[pl.BlockSpec(memory_space=pltpu.VMEM)],
        out_specs=pl.BlockSpec(memory_space=pltpu.VMEM),
        scratch_shapes=[
            pltpu.VMEM(shape, partial.dtype),
            pltpu.SemaphoreType.DMA((2,)),
        ],
        compiler_params=pltpu.CompilerParams(collective_id=1, has_side_effects=True),
    )(partial)


def shards(spectra, send_rows, send_counts, pair_rows, pair_counts):
    whitened = whiten(spectra)
    station_count, comps, parts, bin_count = whitened.shape
    row_width = comps * parts * bin_count
    slot_count = send_rows.shape[2]
    cores = lax.axis_size("core")
    part_bins = bin_count // cores
    core = lax.axis_index("core")

    flat = whitened.reshape(station_count, row_width)
    lists = send_rows[0]
    col_count = lists.shape[0]
    picked = jnp.take(flat, lists.reshape(-1), axis=0).reshape(col_count, slot_count, row_width)
    alive = jnp.arange(slot_count, dtype=jnp.int32)[None, :] < send_counts[0][:, None]
    picked = jnp.where(alive[:, :, None], picked, jnp.zeros_like(picked))
    pieces = picked.reshape(col_count, slot_count, comps * parts, cores, SUBS,
                            part_bins // SUBS)
    pieces = jnp.transpose(pieces, (3, 0, 1, 4, 2, 5)).reshape(
        cores * col_count, slot_count, comps * parts * part_bins)
    pair_total = pair_rows.shape[1]
    panel, chip_pairs, chip_counts = spread(pieces, pair_rows, pair_counts, lax.axis_size("z"),
                                            cores * col_count, col_count)
    lag_rows = lag_tables(bin_count)
    core_arr = core.astype(jnp.int32)[None]
    partial = pair_sums(chip_counts, core_arr, chip_pairs, panel, lag_rows, cores, 0, None)
    total = exchange(partial, 1.0 / math.sqrt(bin_count))[:, :LAGS, :]
    return jnp.transpose(total, (1, 0, 2))


def solution(mesh):
    tile_size = mesh.shape["tile"]
    blk_size = mesh.shape["blk"]
    split = Mesh(mesh.devices.reshape(tile_size // 2, 2, blk_size), ("z", "core", "blk"))
    dev = ("z", "core", "blk")
    return jax.shard_map(
        shards,
        mesh=split,
        in_specs=(
            P(dev, None, None, None),
            P(dev, None, None),
            P(dev, None),
            P(None, dev),
            P(dev),
        ),
        out_specs=P(None, None, dev),
        check_vma=False,
    )
```

```python
import functools
import math

import jax
import ml_dtypes
import numpy as np
import jax.numpy as jnp
from jax import lax
from jax.experimental import pallas as pl
from jax.experimental.pallas import tpu as pltpu
from jax.sharding import Mesh
from jax.sharding import PartitionSpec as P

LAGS = 129
LAG_ROWS = 144
PAIR_BLOCK = 128
BIN_CHUNK = 256
GATHER_CHUNK = 512
SUBS = 2


def whiten(spectra):
    station_count = spectra.shape[0]
    bin_count = spectra.shape[-1]
    ramp_bins = bin_count // 32
    bin_index = jnp.arange(bin_count, dtype=jnp.int32)
    edge_dist = jnp.minimum(bin_index, bin_count - 1 - bin_index).astype(jnp.float32) + 0.5
    ramp_vals = 0.5 - 0.5 * jnp.cos(jnp.pi * edge_dist / ramp_bins)
    taper = jnp.where(edge_dist < ramp_bins, ramp_vals, jnp.ones_like(ramp_vals))
    blocked = spectra.reshape(station_count, 3, 2, bin_count // 64, 64)
    power = jnp.mean(blocked * blocked, axis=(1, 2, 4))
    inverse = 1.0 / jnp.sqrt(power + 1e-05)
    spread_scale = jnp.repeat(inverse, 64, axis=1)
    return (spectra * taper * spread_scale[:, None, None, :]).astype(jnp.bfloat16)


def lag_tables(bin_count):
    lag_index = np.arange(LAGS, dtype=np.int32) - LAGS // 2
    bin_index = np.arange(bin_count, dtype=np.int32)
    phase_steps = lag_index[:, None] * bin_index[None, :] % (2 * bin_count)
    angle = phase_steps.astype(np.float32) * np.float32(np.pi / bin_count)
    pad = ((0, LAG_ROWS - LAGS), (0, 0))
    cos_rows = np.pad(np.cos(angle).astype(np.float32).astype(ml_dtypes.bfloat16), pad)
    sin_rows = np.pad((-np.sin(angle)).astype(np.float32).astype(ml_dtypes.bfloat16), pad)
    chunks = bin_count // BIN_CHUNK
    both = np.stack([cos_rows.reshape(LAG_ROWS, chunks, BIN_CHUNK),
                     sin_rows.reshape(LAG_ROWS, chunks, BIN_CHUNK)], axis=2)
    return jnp.asarray(both.reshape(LAG_ROWS, 2 * bin_count))


def pair_kernel(counts_ref, core_ref, pairs_ref, panel_ref, lag_ref, *rest,
                blocks_per_owner, part_bins, accumulate):
    if accumulate:
        acc_ref, out_ref, f_scr, s_scr = rest
    else:
        out_ref, f_scr, s_scr = rest
    step = pl.program_id(0)
    owner = step // blocks_per_owner
    start = (step % blocks_per_owner) * PAIR_BLOCK
    live = start < counts_ref[owner, 0]
    if accumulate:
        out_ref[...] = acc_ref[...]
    else:
        out_ref[...] = jnp.zeros_like(out_ref)

    @pl.when(live)
    def _():
        rows = panel_ref.shape[0]
        width = panel_ref.shape[1]
        iota = lax.broadcasted_iota(jnp.int32, (rows, PAIR_BLOCK), 0)
        idx = pairs_ref[0]
        pick_first = jnp.where(idx[0:1, :] == iota, 1.0, 0.0).T.astype(jnp.bfloat16)
        pick_second = jnp.where(idx[1:2, :] == iota, 1.0, 0.0).T.astype(jnp.bfloat16)
        pick = jnp.concatenate([pick_first, pick_second], axis=0)
        gather_chunk = min(GATHER_CHUNK, width)

        def gather(c, carry):
            off = pl.multiple_of(c * gather_chunk, gather_chunk)
            block = panel_ref[:, pl.ds(off, gather_chunk)]
            both = jnp.dot(pick, block, preferred_element_type=jnp.float32)
            f_scr[:, pl.ds(off, gather_chunk)] = both[:PAIR_BLOCK]
            s_scr[:, pl.ds(off, gather_chunk)] = both[PAIR_BLOCK:]
            return carry

        lax.fori_loop(0, width // gather_chunk, gather, 0)
        nt = (((1,), (1,)), ((), ()))
        sub_bins = part_bins // SUBS
        bin_chunk = min(BIN_CHUNK, sub_bins)
        for sub in range(SUBS):
            col0 = sub * 6 * sub_bins

            def chunk(kc, carry):
                off = pl.multiple_of(kc * bin_chunk, bin_chunk)
                lag_blk = lag_ref[:, pl.ds(2 * (sub * sub_bins + off), 2 * bin_chunk)]
                crosses = []
                for a in range(3):
                    f_re = f_scr[:, pl.ds(col0 + 2 * a * sub_bins + off, bin_chunk)]
                    f_im = f_scr[:, pl.ds(col0 + (2 * a + 1) * sub_bins + off, bin_chunk)]
                    for b in range(3):
                        s_re = s_scr[:, pl.ds(col0 + 2 * b * sub_bins + off, bin_chunk)]
                        s_im = s_scr[:, pl.ds(col0 + (2 * b + 1) * sub_bins + off, bin_chunk)]
                        real_part = (f_re * s_re + f_im * s_im).astype(jnp.bfloat16)
                        imag_part = (f_im * s_re - f_re * s_im).astype(jnp.bfloat16)
                        crosses.append(jnp.concatenate([real_part, imag_part], axis=1))
                stacked = jnp.concatenate(crosses, axis=0)
                acc = lax.dot_general(stacked, lag_blk, nt, preferred_element_type=jnp.float32)
                out_ref[0] += acc.reshape(9, PAIR_BLOCK, LAG_ROWS)
                return carry

            lax.fori_loop(0, sub_bins // bin_chunk, chunk, 0)
        row = start + lax.broadcasted_iota(jnp.int32, out_ref.shape, 2)
        out_ref[...] = jnp.where(row < counts_ref[owner, 0], out_ref[...], 0.0)


def pair_sums(counts, core_arr, chip_pairs, panel, lag_rows, owners, chunk_id, acc):
    rows, width = panel.shape
    part_bins = width // 6
    pairs = chip_pairs.shape[0] * chip_pairs.shape[2]
    per_owner = pairs // owners
    blocks_per_owner = per_owner // PAIR_BLOCK
    grid = (pairs // PAIR_BLOCK,)
    accumulate = acc is not None
    kernel = functools.partial(pair_kernel, blocks_per_owner=blocks_per_owner,
                               part_bins=part_bins, accumulate=accumulate)
    flops = 2 * pairs * rows * width * 2 + 2 * LAG_ROWS * 2 * part_bins * 9 * pairs
    out_bytes = owners * 9 * LAG_ROWS * per_owner * 4
    cost = pl.CostEstimate(flops=flops, transcendentals=0,
                           bytes_accessed=rows * width * 2 + out_bytes * (2 if accumulate else 1))
    out_spec = pl.BlockSpec(
        (1, 9, PAIR_BLOCK, LAG_ROWS),
        lambda i, c, k: (i // blocks_per_owner, 0, i % blocks_per_owner, 0))
    in_specs = [
        pl.BlockSpec((1, 2, PAIR_BLOCK),
                     lambda i, c, k: (i // blocks_per_owner, 0, i % blocks_per_owner)),
        pl.BlockSpec((rows, width), lambda i, c, k: (0, 0)),
        pl.BlockSpec((LAG_ROWS, 2 * part_bins), lambda i, c, k: (0, k[0])),
    ]
    args = [counts, core_arr, chip_pairs, panel, lag_rows]
    aliases = {}
    if accumulate:
        in_specs.append(out_spec)
        args.append(acc)
        aliases = {len(args) - 1: 0}
    return pl.pallas_call(
        kernel,
        out_shape=jax.ShapeDtypeStruct((owners, 9, per_owner, LAG_ROWS), jnp.float32),
        grid_spec=pltpu.PrefetchScalarGridSpec(
            num_scalar_prefetch=2,
            grid=grid,
            in_specs=in_specs,
            out_specs=out_spec,
            scratch_shapes=[
                pltpu.VMEM((PAIR_BLOCK, width), jnp.float32),
                pltpu.VMEM((PAIR_BLOCK, width), jnp.float32),
            ],
        ),
        input_output_aliases=aliases,
        compiler_params=pltpu.CompilerParams(
            dimension_semantics=("arbitrary",), vmem_limit_bytes=60 * 1024 * 1024),
        cost_estimate=cost,
    )(*args)


MESH_ID = pl.DeviceIdType.MESH


def spread_kernel(pieces_ref, rows_ref, count_ref, panel_ref, chip_rows_ref, chip_count_ref,
                  send_plane, recv_plane,
                  local_sem, send_right, send_left, recv_ring, meta_sems, *, ring_size,
                  plane_size, blk_size, slots, subs):
    me_z = lax.axis_index("z")
    me_c = lax.axis_index("core")
    me_b = lax.axis_index("blk")
    me_q = me_c * blk_size + me_b
    right = (me_z + 1) % ring_size
    left = (me_z + ring_size - 1) % ring_size

    def plane_dev(q):
        return (me_z, q // blk_size, q % blk_size)

    barrier = pltpu.get_barrier_semaphore()

    def greet(i, carry):
        q = (me_q + i) % plane_size
        pl.semaphore_signal(barrier, 1, device_id=plane_dev(q), device_id_type=MESH_ID)
        return carry

    lax.fori_loop(1, plane_size, greet, 0)
    pl.semaphore_signal(barrier, 1, device_id=(right, me_c, me_b), device_id_type=MESH_ID)
    pl.semaphore_signal(barrier, 1, device_id=(left, me_c, me_b), device_id_type=MESH_ID)
    pl.semaphore_wait(barrier, plane_size + 1)

    partner = (me_z, 1 - me_c, me_b)
    meta_copies = []
    for idx, (src, dst) in enumerate(((rows_ref, chip_rows_ref), (count_ref, chip_count_ref))):
        local = pltpu.make_async_copy(src, dst.at[me_c], meta_sems.at[3 * idx])
        local.start()
        remote = pltpu.make_async_remote_copy(
            src, dst.at[me_c], meta_sems.at[3 * idx + 1], meta_sems.at[3 * idx + 2],
            device_id=partner, device_id_type=MESH_ID)
        remote.start()
        arrival = pltpu.make_async_remote_copy(
            src, dst.at[1 - me_c], meta_sems.at[3 * idx + 1], meta_sems.at[3 * idx + 2],
            device_id=partner, device_id_type=MESH_ID)
        meta_copies.append((local, remote, arrival))

    sub_width = panel_ref.shape[1] // subs
    block_rows = plane_size * slots
    half_rows = block_rows // 2
    base = me_z * block_rows
    half = ring_size // 2

    def cols(sub):
        return pl.ds(sub * sub_width, sub_width)

    def rows_of(q, sub):
        return panel_ref.at[pl.ds(base + q * slots, slots), cols(sub)]

    def local_copy(sub):
        return pltpu.make_async_copy(
            pieces_ref.at[me_q, :, cols(sub)], rows_of(me_q, sub), local_sem.at[sub])

    def plane_copy(q, src_q, sub):
        return pltpu.make_async_remote_copy(
            pieces_ref.at[q, :, cols(sub)], rows_of(src_q, sub), send_plane.at[sub, q],
            recv_plane.at[sub, src_q], device_id=plane_dev(q), device_id_type=MESH_ID)

    def scatter(sub):
        local_copy(sub).start()

        def send(i, carry):
            q = (me_q + i) % plane_size
            plane_copy(q, me_q, sub).start()
            return carry

        lax.fori_loop(1, plane_size, send, 0)

    def gathered(sub):
        def arrive(i, carry):
            q = (me_q + plane_size - i) % plane_size
            plane_copy(q, q, sub).wait_recv()
            return carry

        lax.fori_loop(1, plane_size, arrive, 0)
        local_copy(sub).wait()

    def block_of(k, sub):
        return panel_ref.at[pl.ds(k * block_rows, block_rows), cols(sub)]

    def part_of(k, first, sub):
        start = k * block_rows + (0 if first else half_rows)
        return panel_ref.at[pl.ds(start, half_rows), cols(sub)]

    def ring_copy(k, sem, dev, sub):
        return pltpu.make_async_remote_copy(
            block_of(k, sub), block_of(k, sub), sem, recv_ring.at[sub, k],
            device_id=(dev, me_c, me_b), device_id_type=MESH_ID)

    def part_copy(k, first, sem, dev, sub):
        slot = k if first else ring_size
        return pltpu.make_async_remote_copy(
            part_of(k, first, sub), part_of(k, first, sub), sem, recv_ring.at[sub, slot],
            device_id=(dev, me_c, me_b), device_id_type=MESH_ID)

    sends = []

    def ring_step(s, sub):
        k = (me_z + ring_size - s) % ring_size
        if s > 0:
            ring_copy(k, send_right.at[sub, s], left, sub).wait_recv()
        c = ring_copy(k, send_right.at[sub, s], right, sub) if s < half - 1 else part_copy(
            k, True, send_right.at[sub, s], right, sub)
        c.start()
        sends.append(c)
        k = (me_z + s) % ring_size
        if s > 0:
            ring_copy(k, send_left.at[sub, s], right, sub).wait_recv()
        c = ring_copy(k, send_left.at[sub, s], left, sub) if s < half - 1 else part_copy(
            k, False, send_left.at[sub, s], left, sub)
        c.start()
        sends.append(c)

    for sub in range(subs):
        scatter(sub)
        gathered(sub)
        ring_step(0, sub)
    for s in range(1, half):
        for sub in range(subs):
            ring_step(s, sub)
    far = (me_z + half) % ring_size
    for sub in range(subs):
        part_copy(far, True, send_right.at[sub, 0], left, sub).wait_recv()
        part_copy(far, False, send_left.at[sub, 0], right, sub).wait_recv()
    for sub in range(subs):
        def sent(i, carry):
            q = (me_q + i) % plane_size
            plane_copy(q, me_q, sub).wait_send()
            return carry

        lax.fori_loop(1, plane_size, sent, 0)
    for c in sends:
        c.wait_send()
    for local, remote, arrival in meta_copies:
        local.wait()
        arrival.wait_recv()
        remote.wait_send()


def spread(pieces, pair_rows, pair_counts, ring_size, plane_size, blk_size):
    _, slots, width = pieces.shape
    rows = ring_size * plane_size * slots
    kernel = functools.partial(spread_kernel, ring_size=ring_size, plane_size=plane_size,
                               blk_size=blk_size, slots=slots, subs=SUBS)
    half = ring_size // 2
    return pl.pallas_call(
        kernel,
        out_shape=(jax.ShapeDtypeStruct((rows, width), pieces.dtype),
                   jax.ShapeDtypeStruct((2,) + pair_rows.shape, pair_rows.dtype),
                   jax.ShapeDtypeStruct((2,) + pair_counts.shape, pair_counts.dtype)),
        in_specs=[pl.BlockSpec(memory_space=pl.ANY)] * 3,
        out_specs=(pl.BlockSpec(memory_space=pl.ANY),) * 3,
        scratch_shapes=[
            pltpu.SemaphoreType.DMA((SUBS, plane_size)),
            pltpu.SemaphoreType.DMA((SUBS, plane_size)),
            pltpu.SemaphoreType.DMA((SUBS,)),
            pltpu.SemaphoreType.DMA((SUBS, half)),
            pltpu.SemaphoreType.DMA((SUBS, half)),
            pltpu.SemaphoreType.DMA((SUBS, ring_size + 1)),
            pltpu.SemaphoreType.DMA((6,)),
        ],
        compiler_params=pltpu.CompilerParams(collective_id=0, has_side_effects=True),
    )(pieces, pair_rows, pair_counts)


def exchange_kernel(part_ref, out_ref, recv_buf, sems, *, scale):
    me_z = lax.axis_index("z")
    me_c = lax.axis_index("core")
    me_b = lax.axis_index("blk")
    partner = (me_z, 1 - me_c, me_b)
    barrier = pltpu.get_barrier_semaphore()
    pl.semaphore_signal(barrier, 1, device_id=partner, device_id_type=MESH_ID)
    pl.semaphore_wait(barrier, 1)
    copy = pltpu.make_async_remote_copy(
        part_ref.at[1 - me_c], recv_buf, sems.at[0], sems.at[1],
        device_id=partner, device_id_type=MESH_ID)
    copy.start()
    copy.wait()
    out_ref[...] = ((part_ref[me_c] + recv_buf[...]) * scale).astype(out_ref.dtype)


def exchange(partial, scale):
    shape = partial.shape[1:]
    return pl.pallas_call(
        functools.partial(exchange_kernel, scale=scale),
        out_shape=jax.ShapeDtypeStruct(shape, jnp.bfloat16),
        in_specs=[pl.BlockSpec(memory_space=pltpu.VMEM)],
        out_specs=pl.BlockSpec(memory_space=pltpu.VMEM),
        scratch_shapes=[
            pltpu.VMEM(shape, partial.dtype),
            pltpu.SemaphoreType.DMA((2,)),
        ],
        compiler_params=pltpu.CompilerParams(collective_id=1, has_side_effects=True),
    )(partial)


def shards(spectra, send_rows, send_counts, pair_rows, pair_counts):
    whitened = whiten(spectra)
    station_count, comps, parts, bin_count = whitened.shape
    row_width = comps * parts * bin_count
    slot_count = send_rows.shape[2]
    cores = lax.axis_size("core")
    part_bins = bin_count // cores
    core = lax.axis_index("core")

    flat = whitened.reshape(station_count, row_width)
    lists = send_rows[0]
    col_count = lists.shape[0]
    picked = jnp.take(flat, lists.reshape(-1), axis=0).reshape(col_count, slot_count, row_width)
    alive = jnp.arange(slot_count, dtype=jnp.int32)[None, :] < send_counts[0][:, None]
    picked = jnp.where(alive[:, :, None], picked, jnp.zeros_like(picked))
    pieces = picked.reshape(col_count, slot_count, comps * parts, cores, SUBS,
                            part_bins // SUBS)
    pieces = jnp.transpose(pieces, (3, 0, 1, 4, 2, 5)).reshape(
        cores * col_count, slot_count, comps * parts * part_bins)
    pair_total = pair_rows.shape[1]
    panel, chip_pairs, chip_counts = spread(pieces, pair_rows, pair_counts, lax.axis_size("z"),
                                            cores * col_count, col_count)
    lag_rows = lag_tables(bin_count)
    core_arr = core.astype(jnp.int32)[None]
    partial = pair_sums(chip_counts, core_arr, chip_pairs, panel, lag_rows, cores, 0, None)
    total = exchange(partial, 1.0 / math.sqrt(bin_count))[:, :, :LAGS]
    return jnp.transpose(total, (2, 0, 1))


def solution(mesh):
    tile_size = mesh.shape["tile"]
    blk_size = mesh.shape["blk"]
    split = Mesh(mesh.devices.reshape(tile_size // 2, 2, blk_size), ("z", "core", "blk"))
    dev = ("z", "core", "blk")
    return jax.shard_map(
        shards,
        mesh=split,
        in_specs=(
            P(dev, None, None, None),
            P(dev, None, None),
            P(dev, None),
            P(None, dev),
            P(dev),
        ),
        out_specs=P(None, None, dev),
        check_vma=False,
    )
```

```python
import functools
import math

import jax
import ml_dtypes
import numpy as np
import jax.numpy as jnp
from jax import lax
from jax.experimental import pallas as pl
from jax.experimental.pallas import tpu as pltpu
from jax.sharding import Mesh
from jax.sharding import PartitionSpec as P

LAGS = 129
LAG_ROWS = 144
PAIR_BLOCK = 128
BIN_CHUNK = 256
GATHER_CHUNK = 512
SUBS = 2


def whiten(spectra):
    station_count = spectra.shape[0]
    bin_count = spectra.shape[-1]
    ramp_bins = bin_count // 32
    bin_index = jnp.arange(bin_count, dtype=jnp.int32)
    edge_dist = jnp.minimum(bin_index, bin_count - 1 - bin_index).astype(jnp.float32) + 0.5
    ramp_vals = 0.5 - 0.5 * jnp.cos(jnp.pi * edge_dist / ramp_bins)
    taper = jnp.where(edge_dist < ramp_bins, ramp_vals, jnp.ones_like(ramp_vals))
    blocked = spectra.reshape(station_count, 3, 2, bin_count // 64, 64)
    power = jnp.mean(blocked * blocked, axis=(1, 2, 4))
    inverse = 1.0 / jnp.sqrt(power + 1e-05)
    spread_scale = jnp.repeat(inverse, 64, axis=1)
    return (spectra * taper * spread_scale[:, None, None, :]).astype(jnp.bfloat16)


def lag_tables(bin_count):
    lag_index = np.arange(LAGS, dtype=np.int32) - LAGS // 2
    bin_index = np.arange(bin_count, dtype=np.int32)
    phase_steps = lag_index[:, None] * bin_index[None, :] % (2 * bin_count)
    angle = phase_steps.astype(np.float32) * np.float32(np.pi / bin_count)
    pad = ((0, LAG_ROWS - LAGS), (0, 0))
    cos_rows = np.pad(np.cos(angle).astype(np.float32).astype(ml_dtypes.bfloat16), pad)
    sin_rows = np.pad((-np.sin(angle)).astype(np.float32).astype(ml_dtypes.bfloat16), pad)
    chunks = bin_count // BIN_CHUNK
    both = np.stack([cos_rows.reshape(LAG_ROWS, chunks, BIN_CHUNK),
                     sin_rows.reshape(LAG_ROWS, chunks, BIN_CHUNK)], axis=2)
    return jnp.asarray(both.reshape(LAG_ROWS, 2 * bin_count))


def pair_kernel(counts_ref, core_ref, pairs_ref, panel_ref, lag_ref, *rest,
                blocks_per_owner, part_bins, accumulate):
    if accumulate:
        acc_ref, out_ref, f_scr, s_scr = rest
    else:
        out_ref, f_scr, s_scr = rest
    step = pl.program_id(0)
    owner = step // blocks_per_owner
    start = (step % blocks_per_owner) * PAIR_BLOCK
    live = start < counts_ref[owner, 0]
    if accumulate:
        out_ref[...] = acc_ref[...]
    else:
        out_ref[...] = jnp.zeros_like(out_ref)

    @pl.when(live)
    def _():
        rows = panel_ref.shape[0]
        width = panel_ref.shape[1]
        iota = lax.broadcasted_iota(jnp.int32, (rows, PAIR_BLOCK), 0)
        idx = pairs_ref[0]
        pick_first = jnp.where(idx[0:1, :] == iota, 1.0, 0.0).T.astype(jnp.bfloat16)
        pick_second = jnp.where(idx[1:2, :] == iota, 1.0, 0.0).T.astype(jnp.bfloat16)
        pick = jnp.concatenate([pick_first, pick_second], axis=0)
        gather_chunk = min(GATHER_CHUNK, width)

        def gather(c, carry):
            off = pl.multiple_of(c * gather_chunk, gather_chunk)
            block = panel_ref[:, pl.ds(off, gather_chunk)]
            both = jnp.dot(pick, block, preferred_element_type=jnp.float32)
            f_scr[:, pl.ds(off, gather_chunk)] = both[:PAIR_BLOCK]
            s_scr[:, pl.ds(off, gather_chunk)] = both[PAIR_BLOCK:]
            return carry

        lax.fori_loop(0, width // gather_chunk, gather, 0)
        nt = (((1,), (1,)), ((), ()))
        sub_bins = part_bins // SUBS
        bin_chunk = min(BIN_CHUNK, sub_bins)
        for sub in range(SUBS):
            col0 = sub * 6 * sub_bins

            def chunk(kc, carry):
                off = pl.multiple_of(kc * bin_chunk, bin_chunk)
                lag_blk = lag_ref[:, pl.ds(2 * (sub * sub_bins + off), 2 * bin_chunk)]
                for a in range(3):
                    f_re = f_scr[:, pl.ds(col0 + 2 * a * sub_bins + off, bin_chunk)]
                    f_im = f_scr[:, pl.ds(col0 + (2 * a + 1) * sub_bins + off, bin_chunk)]
                    for b in range(3):
                        s_re = s_scr[:, pl.ds(col0 + 2 * b * sub_bins + off, bin_chunk)]
                        s_im = s_scr[:, pl.ds(col0 + (2 * b + 1) * sub_bins + off, bin_chunk)]
                        real_part = (f_re * s_re + f_im * s_im).astype(jnp.bfloat16)
                        imag_part = (f_im * s_re - f_re * s_im).astype(jnp.bfloat16)
                        both = jnp.concatenate([real_part, imag_part], axis=1)
                        acc = lax.dot_general(lag_blk, both, nt,
                                              preferred_element_type=jnp.float32)
                        out_ref[0, 3 * a + b] += acc
                return carry

            lax.fori_loop(0, sub_bins // bin_chunk, chunk, 0)
        column = start + lax.broadcasted_iota(jnp.int32, out_ref.shape, 3)
        out_ref[...] = jnp.where(column < counts_ref[owner, 0], out_ref[...], 0.0)


def pair_sums(counts, core_arr, chip_pairs, panel, lag_rows, owners, chunk_id, acc):
    rows, width = panel.shape
    part_bins = width // 6
    pairs = chip_pairs.shape[0] * chip_pairs.shape[2]
    per_owner = pairs // owners
    blocks_per_owner = per_owner // PAIR_BLOCK
    grid = (pairs // PAIR_BLOCK,)
    accumulate = acc is not None
    kernel = functools.partial(pair_kernel, blocks_per_owner=blocks_per_owner,
                               part_bins=part_bins, accumulate=accumulate)
    flops = 2 * pairs * rows * width * 2 + 2 * LAG_ROWS * 2 * part_bins * 9 * pairs
    out_bytes = owners * 9 * LAG_ROWS * per_owner * 4
    cost = pl.CostEstimate(flops=flops, transcendentals=0,
                           bytes_accessed=rows * width * 2 + out_bytes * (2 if accumulate else 1))
    out_spec = pl.BlockSpec(
        (1, 9, LAG_ROWS, PAIR_BLOCK),
        lambda i, c, k: (i // blocks_per_owner, 0, 0, i % blocks_per_owner))
    in_specs = [
        pl.BlockSpec((1, 2, PAIR_BLOCK),
                     lambda i, c, k: (i // blocks_per_owner, 0, i % blocks_per_owner)),
        pl.BlockSpec((rows, width), lambda i, c, k: (0, 0)),
        pl.BlockSpec((LAG_ROWS, 2 * part_bins), lambda i, c, k: (0, k[0])),
    ]
    args = [counts, core_arr, chip_pairs, panel, lag_rows]
    aliases = {}
    if accumulate:
        in_specs.append(out_spec)
        args.append(acc)
        aliases = {len(args) - 1: 0}
    return pl.pallas_call(
        kernel,
        out_shape=jax.ShapeDtypeStruct((owners, 9, LAG_ROWS, per_owner), jnp.float32),
        grid_spec=pltpu.PrefetchScalarGridSpec(
            num_scalar_prefetch=2,
            grid=grid,
            in_specs=in_specs,
            out_specs=out_spec,
            scratch_shapes=[
                pltpu.VMEM((PAIR_BLOCK, width), jnp.float32),
                pltpu.VMEM((PAIR_BLOCK, width), jnp.float32),
            ],
        ),
        input_output_aliases=aliases,
        compiler_params=pltpu.CompilerParams(
            dimension_semantics=("arbitrary",), vmem_limit_bytes=60 * 1024 * 1024),
        cost_estimate=cost,
    )(*args)


MESH_ID = pl.DeviceIdType.MESH


def spread_kernel(pieces_ref, rows_ref, count_ref, panel_ref, chip_rows_ref, chip_count_ref,
                  send_plane, recv_plane,
                  local_sem, send_right, send_left, recv_ring, meta_sems, *, ring_size,
                  plane_size, blk_size, slots, subs):
    me_z = lax.axis_index("z")
    me_c = lax.axis_index("core")
    me_b = lax.axis_index("blk")
    me_q = me_c * blk_size + me_b
    right = (me_z + 1) % ring_size
    left = (me_z + ring_size - 1) % ring_size

    def plane_dev(q):
        return (me_z, q // blk_size, q % blk_size)

    barrier = pltpu.get_barrier_semaphore()

    def greet(i, carry):
        q = (me_q + i) % plane_size
        pl.semaphore_signal(barrier, 1, device_id=plane_dev(q), device_id_type=MESH_ID)
        return carry

    lax.fori_loop(1, plane_size, greet, 0)
    pl.semaphore_signal(barrier, 1, device_id=(right, me_c, me_b), device_id_type=MESH_ID)
    pl.semaphore_signal(barrier, 1, device_id=(left, me_c, me_b), device_id_type=MESH_ID)
    pl.semaphore_wait(barrier, plane_size + 1)

    partner = (me_z, 1 - me_c, me_b)
    meta_copies = []
    for idx, (src, dst) in enumerate(((rows_ref, chip_rows_ref), (count_ref, chip_count_ref))):
        local = pltpu.make_async_copy(src, dst.at[me_c], meta_sems.at[3 * idx])
        local.start()
        remote = pltpu.make_async_remote_copy(
            src, dst.at[me_c], meta_sems.at[3 * idx + 1], meta_sems.at[3 * idx + 2],
            device_id=partner, device_id_type=MESH_ID)
        remote.start()
        arrival = pltpu.make_async_remote_copy(
            src, dst.at[1 - me_c], meta_sems.at[3 * idx + 1], meta_sems.at[3 * idx + 2],
            device_id=partner, device_id_type=MESH_ID)
        meta_copies.append((local, remote, arrival))

    sub_width = panel_ref.shape[1] // subs
    block_rows = plane_size * slots
    half_rows = block_rows // 2
    base = me_z * block_rows
    half = ring_size // 2

    def cols(sub):
        return pl.ds(sub * sub_width, sub_width)

    def rows_of(q, sub):
        return panel_ref.at[pl.ds(base + q * slots, slots), cols(sub)]

    def local_copy(sub):
        return pltpu.make_async_copy(
            pieces_ref.at[me_q, :, cols(sub)], rows_of(me_q, sub), local_sem.at[sub])

    def plane_copy(q, src_q, sub):
        return pltpu.make_async_remote_copy(
            pieces_ref.at[q, :, cols(sub)], rows_of(src_q, sub), send_plane.at[sub, q],
            recv_plane.at[sub, src_q], device_id=plane_dev(q), device_id_type=MESH_ID)

    def scatter(sub):
        local_copy(sub).start()

        def send(i, carry):
            q = (me_q + i) % plane_size
            plane_copy(q, me_q, sub).start()
            return carry

        lax.fori_loop(1, plane_size, send, 0)

    def gathered(sub):
        def arrive(i, carry):
            q = (me_q + plane_size - i) % plane_size
            plane_copy(q, q, sub).wait_recv()
            return carry

        lax.fori_loop(1, plane_size, arrive, 0)
        local_copy(sub).wait()

    def block_of(k, sub):
        return panel_ref.at[pl.ds(k * block_rows, block_rows), cols(sub)]

    def part_of(k, first, sub):
        start = k * block_rows + (0 if first else half_rows)
        return panel_ref.at[pl.ds(start, half_rows), cols(sub)]

    def ring_copy(k, sem, dev, sub):
        return pltpu.make_async_remote_copy(
            block_of(k, sub), block_of(k, sub), sem, recv_ring.at[sub, k],
            device_id=(dev, me_c, me_b), device_id_type=MESH_ID)

    def part_copy(k, first, sem, dev, sub):
        slot = k if first else ring_size
        return pltpu.make_async_remote_copy(
            part_of(k, first, sub), part_of(k, first, sub), sem, recv_ring.at[sub, slot],
            device_id=(dev, me_c, me_b), device_id_type=MESH_ID)

    sends = []

    def ring_step(s, sub):
        k = (me_z + ring_size - s) % ring_size
        if s > 0:
            ring_copy(k, send_right.at[sub, s], left, sub).wait_recv()
        c = ring_copy(k, send_right.at[sub, s], right, sub) if s < half - 1 else part_copy(
            k, True, send_right.at[sub, s], right, sub)
        c.start()
        sends.append(c)
        k = (me_z + s) % ring_size
        if s > 0:
            ring_copy(k, send_left.at[sub, s], right, sub).wait_recv()
        c = ring_copy(k, send_left.at[sub, s], left, sub) if s < half - 1 else part_copy(
            k, False, send_left.at[sub, s], left, sub)
        c.start()
        sends.append(c)

    for sub in range(subs):
        scatter(sub)
        gathered(sub)
        ring_step(0, sub)
    for s in range(1, half):
        for sub in range(subs):
            ring_step(s, sub)
    far = (me_z + half) % ring_size
    for sub in range(subs):
        part_copy(far, True, send_right.at[sub, 0], left, sub).wait_recv()
        part_copy(far, False, send_left.at[sub, 0], right, sub).wait_recv()
    for sub in range(subs):
        def sent(i, carry):
            q = (me_q + i) % plane_size
            plane_copy(q, me_q, sub).wait_send()
            return carry

        lax.fori_loop(1, plane_size, sent, 0)
    for c in sends:
        c.wait_send()
    for local, remote, arrival in meta_copies:
        local.wait()
        arrival.wait_recv()
        remote.wait_send()


def spread(pieces, pair_rows, pair_counts, ring_size, plane_size, blk_size):
    _, slots, width = pieces.shape
    rows = ring_size * plane_size * slots
    kernel = functools.partial(spread_kernel, ring_size=ring_size, plane_size=plane_size,
                               blk_size=blk_size, slots=slots, subs=SUBS)
    half = ring_size // 2
    return pl.pallas_call(
        kernel,
        out_shape=(jax.ShapeDtypeStruct((rows, width), pieces.dtype),
                   jax.ShapeDtypeStruct((2,) + pair_rows.shape, pair_rows.dtype),
                   jax.ShapeDtypeStruct((2,) + pair_counts.shape, pair_counts.dtype)),
        in_specs=[pl.BlockSpec(memory_space=pl.ANY)] * 3,
        out_specs=(pl.BlockSpec(memory_space=pl.ANY),) * 3,
        scratch_shapes=[
            pltpu.SemaphoreType.DMA((SUBS, plane_size)),
            pltpu.SemaphoreType.DMA((SUBS, plane_size)),
            pltpu.SemaphoreType.DMA((SUBS,)),
            pltpu.SemaphoreType.DMA((SUBS, half)),
            pltpu.SemaphoreType.DMA((SUBS, half)),
            pltpu.SemaphoreType.DMA((SUBS, ring_size + 1)),
            pltpu.SemaphoreType.DMA((6,)),
        ],
        compiler_params=pltpu.CompilerParams(collective_id=0, has_side_effects=True),
    )(pieces, pair_rows, pair_counts)


def exchange_kernel(part_ref, out_ref, mine_buf, recv_buf, sems, *, scale):
    me_z = lax.axis_index("z")
    me_c = lax.axis_index("core")
    me_b = lax.axis_index("blk")
    partner = (me_z, 1 - me_c, me_b)
    local = pltpu.make_async_copy(part_ref.at[me_c], mine_buf, sems.at[2])
    local.start()
    barrier = pltpu.get_barrier_semaphore()
    pl.semaphore_signal(barrier, 1, device_id=partner, device_id_type=MESH_ID)
    pl.semaphore_wait(barrier, 1)
    copy = pltpu.make_async_remote_copy(
        part_ref.at[1 - me_c], recv_buf, sems.at[0], sems.at[1],
        device_id=partner, device_id_type=MESH_ID)
    copy.start()
    local.wait()
    copy.wait()
    out_ref[...] = ((mine_buf[...] + recv_buf[...]) * scale).astype(out_ref.dtype)


def exchange(partial, scale):
    shape = partial.shape[1:]
    return pl.pallas_call(
        functools.partial(exchange_kernel, scale=scale),
        out_shape=jax.ShapeDtypeStruct(shape, jnp.bfloat16),
        in_specs=[pl.BlockSpec(memory_space=pl.ANY)],
        out_specs=pl.BlockSpec(memory_space=pltpu.VMEM),
        scratch_shapes=[
            pltpu.VMEM(shape, partial.dtype),
            pltpu.VMEM(shape, partial.dtype),
            pltpu.SemaphoreType.DMA((3,)),
        ],
        compiler_params=pltpu.CompilerParams(collective_id=1, has_side_effects=True),
    )(partial)


def shards(spectra, send_rows, send_counts, pair_rows, pair_counts):
    whitened = whiten(spectra)
    station_count, comps, parts, bin_count = whitened.shape
    row_width = comps * parts * bin_count
    slot_count = send_rows.shape[2]
    cores = lax.axis_size("core")
    part_bins = bin_count // cores
    core = lax.axis_index("core")

    flat = whitened.reshape(station_count, row_width)
    lists = send_rows[0]
    col_count = lists.shape[0]
    picked = jnp.take(flat, lists.reshape(-1), axis=0).reshape(col_count, slot_count, row_width)
    alive = jnp.arange(slot_count, dtype=jnp.int32)[None, :] < send_counts[0][:, None]
    picked = jnp.where(alive[:, :, None], picked, jnp.zeros_like(picked))
    pieces = picked.reshape(col_count, slot_count, comps * parts, cores, SUBS,
                            part_bins // SUBS)
    pieces = jnp.transpose(pieces, (3, 0, 1, 4, 2, 5)).reshape(
        cores * col_count, slot_count, comps * parts * part_bins)
    pair_total = pair_rows.shape[1]
    panel, chip_pairs, chip_counts = spread(pieces, pair_rows, pair_counts, lax.axis_size("z"),
                                            cores * col_count, col_count)
    lag_rows = lag_tables(bin_count)
    core_arr = core.astype(jnp.int32)[None]
    partial = pair_sums(chip_counts, core_arr, chip_pairs, panel, lag_rows, cores, 0, None)
    total = exchange(partial, 1.0 / math.sqrt(bin_count))[:, :LAGS, :]
    return jnp.transpose(total, (1, 0, 2))


def solution(mesh):
    tile_size = mesh.shape["tile"]
    blk_size = mesh.shape["blk"]
    split = Mesh(mesh.devices.reshape(tile_size // 2, 2, blk_size), ("z", "core", "blk"))
    dev = ("z", "core", "blk")
    return jax.shard_map(
        shards,
        mesh=split,
        in_specs=(
            P(dev, None, None, None),
            P(dev, None, None),
            P(dev, None),
            P(None, dev),
            P(dev),
        ),
        out_specs=P(None, None, dev),
        check_vma=False,
    )
```

```python
import functools
import math

import jax
import ml_dtypes
import numpy as np
import jax.numpy as jnp
from jax import lax
from jax.experimental import pallas as pl
from jax.experimental.pallas import tpu as pltpu
from jax.sharding import Mesh
from jax.sharding import PartitionSpec as P

LAGS = 129
LAG_ROWS = 144
PAIR_BLOCK = 128
BIN_CHUNK = 256
GATHER_CHUNK = 512
SUBS = 2


def whiten(spectra):
    station_count = spectra.shape[0]
    bin_count = spectra.shape[-1]
    ramp_bins = bin_count // 32
    bin_index = jnp.arange(bin_count, dtype=jnp.int32)
    edge_dist = jnp.minimum(bin_index, bin_count - 1 - bin_index).astype(jnp.float32) + 0.5
    ramp_vals = 0.5 - 0.5 * jnp.cos(jnp.pi * edge_dist / ramp_bins)
    taper = jnp.where(edge_dist < ramp_bins, ramp_vals, jnp.ones_like(ramp_vals))
    blocked = spectra.reshape(station_count, 3, 2, bin_count // 64, 64)
    power = jnp.mean(blocked * blocked, axis=(1, 2, 4))
    inverse = 1.0 / jnp.sqrt(power + 1e-05)
    spread_scale = jnp.repeat(inverse, 64, axis=1)
    return (spectra * taper * spread_scale[:, None, None, :]).astype(jnp.bfloat16)


def lag_tables(bin_count):
    lag_index = np.arange(LAGS, dtype=np.int32) - LAGS // 2
    bin_index = np.arange(bin_count, dtype=np.int32)
    phase_steps = lag_index[:, None] * bin_index[None, :] % (2 * bin_count)
    angle = phase_steps.astype(np.float32) * np.float32(np.pi / bin_count)
    pad = ((0, LAG_ROWS - LAGS), (0, 0))
    cos_rows = np.pad(np.cos(angle).astype(np.float32).astype(ml_dtypes.bfloat16), pad)
    sin_rows = np.pad((-np.sin(angle)).astype(np.float32).astype(ml_dtypes.bfloat16), pad)
    chunks = bin_count // BIN_CHUNK
    both = np.stack([cos_rows.reshape(LAG_ROWS, chunks, BIN_CHUNK),
                     sin_rows.reshape(LAG_ROWS, chunks, BIN_CHUNK)], axis=2)
    return jnp.asarray(both.reshape(LAG_ROWS, 2 * bin_count))


def pair_kernel(counts_ref, core_ref, pairs_ref, panel_hbm, lag_ref, *rest,
                blocks_per_owner, part_bins, accumulate):
    if accumulate:
        acc_ref, out_ref, f_scr, s_scr, panel_ref, panel_sems = rest
    else:
        out_ref, f_scr, s_scr, panel_ref, panel_sems = rest
    step = pl.program_id(0)
    owner = step // blocks_per_owner
    start = (step % blocks_per_owner) * PAIR_BLOCK
    live = start < counts_ref[owner, 0]
    load_chunk = min(GATHER_CHUNK, panel_ref.shape[1])
    load_count = panel_ref.shape[1] // load_chunk

    def panel_copy(c):
        cols = pl.ds(c * load_chunk, load_chunk)
        return pltpu.make_async_copy(panel_hbm.at[:, cols], panel_ref.at[:, cols],
                                     panel_sems.at[c])

    @pl.when(step == 0)
    def _():
        for c in range(load_count):
            panel_copy(c).start()

    if accumulate:
        out_ref[...] = acc_ref[...]
    else:
        out_ref[...] = jnp.zeros_like(out_ref)

    @pl.when(jnp.logical_and(step == 0, jnp.logical_not(live)))
    def _():
        for c in range(load_count):
            panel_copy(c).wait()

    @pl.when(live)
    def _():
        rows = panel_ref.shape[0]
        width = panel_ref.shape[1]
        iota = lax.broadcasted_iota(jnp.int32, (rows, PAIR_BLOCK), 0)
        idx = pairs_ref[0]
        pick_first = jnp.where(idx[0:1, :] == iota, 1.0, 0.0).T.astype(jnp.bfloat16)
        pick_second = jnp.where(idx[1:2, :] == iota, 1.0, 0.0).T.astype(jnp.bfloat16)
        pick = jnp.concatenate([pick_first, pick_second], axis=0)
        gather_chunk = min(GATHER_CHUNK, width)

        def gather(c, carry):
            @pl.when(step == 0)
            def _():
                panel_copy(c).wait()

            off = pl.multiple_of(c * gather_chunk, gather_chunk)
            block = panel_ref[:, pl.ds(off, gather_chunk)]
            both = jnp.dot(pick, block, preferred_element_type=jnp.float32)
            f_scr[:, pl.ds(off, gather_chunk)] = both[:PAIR_BLOCK]
            s_scr[:, pl.ds(off, gather_chunk)] = both[PAIR_BLOCK:]
            return carry

        lax.fori_loop(0, width // gather_chunk, gather, 0)
        nt = (((1,), (1,)), ((), ()))
        sub_bins = part_bins // SUBS
        bin_chunk = min(BIN_CHUNK, sub_bins)
        for sub in range(SUBS):
            col0 = sub * 6 * sub_bins

            def chunk(kc, carry):
                off = pl.multiple_of(kc * bin_chunk, bin_chunk)
                lag_blk = lag_ref[:, pl.ds(2 * (sub * sub_bins + off), 2 * bin_chunk)]
                for a in range(3):
                    f_re = f_scr[:, pl.ds(col0 + 2 * a * sub_bins + off, bin_chunk)]
                    f_im = f_scr[:, pl.ds(col0 + (2 * a + 1) * sub_bins + off, bin_chunk)]
                    for b in range(3):
                        s_re = s_scr[:, pl.ds(col0 + 2 * b * sub_bins + off, bin_chunk)]
                        s_im = s_scr[:, pl.ds(col0 + (2 * b + 1) * sub_bins + off, bin_chunk)]
                        real_part = (f_re * s_re + f_im * s_im).astype(jnp.bfloat16)
                        imag_part = (f_im * s_re - f_re * s_im).astype(jnp.bfloat16)
                        both = jnp.concatenate([real_part, imag_part], axis=1)
                        acc = lax.dot_general(lag_blk, both, nt,
                                              preferred_element_type=jnp.float32)
                        out_ref[0, 3 * a + b] += acc
                return carry

            lax.fori_loop(0, sub_bins // bin_chunk, chunk, 0)
        column = start + lax.broadcasted_iota(jnp.int32, out_ref.shape, 3)
        out_ref[...] = jnp.where(column < counts_ref[owner, 0], out_ref[...], 0.0)


def pair_sums(counts, core_arr, chip_pairs, panel, lag_rows, owners, chunk_id, acc):
    rows, width = panel.shape
    part_bins = width // 6
    pairs = chip_pairs.shape[0] * chip_pairs.shape[2]
    per_owner = pairs // owners
    blocks_per_owner = per_owner // PAIR_BLOCK
    grid = (pairs // PAIR_BLOCK,)
    accumulate = acc is not None
    kernel = functools.partial(pair_kernel, blocks_per_owner=blocks_per_owner,
                               part_bins=part_bins, accumulate=accumulate)
    flops = 2 * pairs * rows * width * 2 + 2 * LAG_ROWS * 2 * part_bins * 9 * pairs
    out_bytes = owners * 9 * LAG_ROWS * per_owner * 4
    cost = pl.CostEstimate(flops=flops, transcendentals=0,
                           bytes_accessed=rows * width * 2 + out_bytes * (2 if accumulate else 1))
    out_spec = pl.BlockSpec(
        (1, 9, LAG_ROWS, PAIR_BLOCK),
        lambda i, c, k: (i // blocks_per_owner, 0, 0, i % blocks_per_owner))
    in_specs = [
        pl.BlockSpec((1, 2, PAIR_BLOCK),
                     lambda i, c, k: (i // blocks_per_owner, 0, i % blocks_per_owner)),
        pl.BlockSpec(memory_space=pl.ANY),
        pl.BlockSpec((LAG_ROWS, 2 * part_bins), lambda i, c, k: (0, k[0])),
    ]
    args = [counts, core_arr, chip_pairs, panel, lag_rows]
    aliases = {}
    if accumulate:
        in_specs.append(out_spec)
        args.append(acc)
        aliases = {len(args) - 1: 0}
    return pl.pallas_call(
        kernel,
        out_shape=jax.ShapeDtypeStruct((owners, 9, LAG_ROWS, per_owner), jnp.float32),
        grid_spec=pltpu.PrefetchScalarGridSpec(
            num_scalar_prefetch=2,
            grid=grid,
            in_specs=in_specs,
            out_specs=out_spec,
            scratch_shapes=[
                pltpu.VMEM((PAIR_BLOCK, width), jnp.float32),
                pltpu.VMEM((PAIR_BLOCK, width), jnp.float32),
                pltpu.VMEM((rows, width), panel.dtype),
                pltpu.SemaphoreType.DMA((width // min(GATHER_CHUNK, width),)),
            ],
        ),
        input_output_aliases=aliases,
        compiler_params=pltpu.CompilerParams(
            dimension_semantics=("arbitrary",), vmem_limit_bytes=60 * 1024 * 1024),
        cost_estimate=cost,
    )(*args)


MESH_ID = pl.DeviceIdType.MESH


def spread_kernel(pieces_ref, rows_ref, count_ref, panel_ref, chip_rows_ref, chip_count_ref,
                  send_plane, recv_plane,
                  local_sem, send_right, send_left, recv_ring, meta_sems, *, ring_size,
                  plane_size, blk_size, slots, subs):
    me_z = lax.axis_index("z")
    me_c = lax.axis_index("core")
    me_b = lax.axis_index("blk")
    me_q = me_c * blk_size + me_b
    right = (me_z + 1) % ring_size
    left = (me_z + ring_size - 1) % ring_size

    def plane_dev(q):
        return (me_z, q // blk_size, q % blk_size)

    barrier = pltpu.get_barrier_semaphore()

    def greet(i, carry):
        q = (me_q + i) % plane_size
        pl.semaphore_signal(barrier, 1, device_id=plane_dev(q), device_id_type=MESH_ID)
        return carry

    lax.fori_loop(1, plane_size, greet, 0)
    pl.semaphore_signal(barrier, 1, device_id=(right, me_c, me_b), device_id_type=MESH_ID)
    pl.semaphore_signal(barrier, 1, device_id=(left, me_c, me_b), device_id_type=MESH_ID)
    pl.semaphore_wait(barrier, plane_size + 1)

    partner = (me_z, 1 - me_c, me_b)
    meta_copies = []
    for idx, (src, dst) in enumerate(((rows_ref, chip_rows_ref), (count_ref, chip_count_ref))):
        local = pltpu.make_async_copy(src, dst.at[me_c], meta_sems.at[3 * idx])
        local.start()
        remote = pltpu.make_async_remote_copy(
            src, dst.at[me_c], meta_sems.at[3 * idx + 1], meta_sems.at[3 * idx + 2],
            device_id=partner, device_id_type=MESH_ID)
        remote.start()
        arrival = pltpu.make_async_remote_copy(
            src, dst.at[1 - me_c], meta_sems.at[3 * idx + 1], meta_sems.at[3 * idx + 2],
            device_id=partner, device_id_type=MESH_ID)
        meta_copies.append((local, remote, arrival))

    sub_width = panel_ref.shape[1] // subs
    block_rows = plane_size * slots
    half_rows = block_rows // 2
    base = me_z * block_rows
    half = ring_size // 2

    def cols(sub):
        return pl.ds(sub * sub_width, sub_width)

    def rows_of(q, sub):
        return panel_ref.at[pl.ds(base + q * slots, slots), cols(sub)]

    def local_copy(sub):
        return pltpu.make_async_copy(
            pieces_ref.at[me_q, :, cols(sub)], rows_of(me_q, sub), local_sem.at[sub])

    def plane_copy(q, src_q, sub):
        return pltpu.make_async_remote_copy(
            pieces_ref.at[q, :, cols(sub)], rows_of(src_q, sub), send_plane.at[sub, q],
            recv_plane.at[sub, src_q], device_id=plane_dev(q), device_id_type=MESH_ID)

    def scatter(sub):
        local_copy(sub).start()

        def send(i, carry):
            q = (me_q + i) % plane_size
            plane_copy(q, me_q, sub).start()
            return carry

        lax.fori_loop(1, plane_size, send, 0)

    def gathered(sub):
        def arrive(i, carry):
            q = (me_q + plane_size - i) % plane_size
            plane_copy(q, q, sub).wait_recv()
            return carry

        lax.fori_loop(1, plane_size, arrive, 0)
        local_copy(sub).wait()

    def block_of(k, sub):
        return panel_ref.at[pl.ds(k * block_rows, block_rows), cols(sub)]

    def part_of(k, first, sub):
        start = k * block_rows + (0 if first else half_rows)
        return panel_ref.at[pl.ds(start, half_rows), cols(sub)]

    def ring_copy(k, sem, dev, sub):
        return pltpu.make_async_remote_copy(
            block_of(k, sub), block_of(k, sub), sem, recv_ring.at[sub, k],
            device_id=(dev, me_c, me_b), device_id_type=MESH_ID)

    def part_copy(k, first, sem, dev, sub):
        slot = k if first else ring_size
        return pltpu.make_async_remote_copy(
            part_of(k, first, sub), part_of(k, first, sub), sem, recv_ring.at[sub, slot],
            device_id=(dev, me_c, me_b), device_id_type=MESH_ID)

    sends = []

    def ring_step(s, sub):
        k = (me_z + ring_size - s) % ring_size
        if s > 0:
            ring_copy(k, send_right.at[sub, s], left, sub).wait_recv()
        c = ring_copy(k, send_right.at[sub, s], right, sub) if s < half - 1 else part_copy(
            k, True, send_right.at[sub, s], right, sub)
        c.start()
        sends.append(c)
        k = (me_z + s) % ring_size
        if s > 0:
            ring_copy(k, send_left.at[sub, s], right, sub).wait_recv()
        c = ring_copy(k, send_left.at[sub, s], left, sub) if s < half - 1 else part_copy(
            k, False, send_left.at[sub, s], left, sub)
        c.start()
        sends.append(c)

    for sub in range(subs):
        scatter(sub)
        gathered(sub)
        ring_step(0, sub)
    for s in range(1, half):
        for sub in range(subs):
            ring_step(s, sub)
    far = (me_z + half) % ring_size
    for sub in range(subs):
        part_copy(far, True, send_right.at[sub, 0], left, sub).wait_recv()
        part_copy(far, False, send_left.at[sub, 0], right, sub).wait_recv()
    for sub in range(subs):
        def sent(i, carry):
            q = (me_q + i) % plane_size
            plane_copy(q, me_q, sub).wait_send()
            return carry

        lax.fori_loop(1, plane_size, sent, 0)
    for c in sends:
        c.wait_send()
    for local, remote, arrival in meta_copies:
        local.wait()
        arrival.wait_recv()
        remote.wait_send()


def spread(pieces, pair_rows, pair_counts, ring_size, plane_size, blk_size):
    _, slots, width = pieces.shape
    rows = ring_size * plane_size * slots
    kernel = functools.partial(spread_kernel, ring_size=ring_size, plane_size=plane_size,
                               blk_size=blk_size, slots=slots, subs=SUBS)
    half = ring_size // 2
    return pl.pallas_call(
        kernel,
        out_shape=(jax.ShapeDtypeStruct((rows, width), pieces.dtype),
                   jax.ShapeDtypeStruct((2,) + pair_rows.shape, pair_rows.dtype),
                   jax.ShapeDtypeStruct((2,) + pair_counts.shape, pair_counts.dtype)),
        in_specs=[pl.BlockSpec(memory_space=pl.ANY)] * 3,
        out_specs=(pl.BlockSpec(memory_space=pl.ANY),) * 3,
        scratch_shapes=[
            pltpu.SemaphoreType.DMA((SUBS, plane_size)),
            pltpu.SemaphoreType.DMA((SUBS, plane_size)),
            pltpu.SemaphoreType.DMA((SUBS,)),
            pltpu.SemaphoreType.DMA((SUBS, half)),
            pltpu.SemaphoreType.DMA((SUBS, half)),
            pltpu.SemaphoreType.DMA((SUBS, ring_size + 1)),
            pltpu.SemaphoreType.DMA((6,)),
        ],
        compiler_params=pltpu.CompilerParams(collective_id=0, has_side_effects=True),
    )(pieces, pair_rows, pair_counts)


def exchange_kernel(part_ref, out_ref, mine_buf, recv_buf, sems, *, scale):
    me_z = lax.axis_index("z")
    me_c = lax.axis_index("core")
    me_b = lax.axis_index("blk")
    partner = (me_z, 1 - me_c, me_b)
    local = pltpu.make_async_copy(part_ref.at[me_c], mine_buf, sems.at[2])
    local.start()
    barrier = pltpu.get_barrier_semaphore()
    pl.semaphore_signal(barrier, 1, device_id=partner, device_id_type=MESH_ID)
    pl.semaphore_wait(barrier, 1)
    copy = pltpu.make_async_remote_copy(
        part_ref.at[1 - me_c], recv_buf, sems.at[0], sems.at[1],
        device_id=partner, device_id_type=MESH_ID)
    copy.start()
    local.wait()
    copy.wait()
    out_ref[...] = ((mine_buf[...] + recv_buf[...]) * scale).astype(out_ref.dtype)


def exchange(partial, scale):
    shape = partial.shape[1:]
    return pl.pallas_call(
        functools.partial(exchange_kernel, scale=scale),
        out_shape=jax.ShapeDtypeStruct(shape, jnp.bfloat16),
        in_specs=[pl.BlockSpec(memory_space=pl.ANY)],
        out_specs=pl.BlockSpec(memory_space=pltpu.VMEM),
        scratch_shapes=[
            pltpu.VMEM(shape, partial.dtype),
            pltpu.VMEM(shape, partial.dtype),
            pltpu.SemaphoreType.DMA((3,)),
        ],
        compiler_params=pltpu.CompilerParams(collective_id=1, has_side_effects=True),
    )(partial)


def shards(spectra, send_rows, send_counts, pair_rows, pair_counts):
    whitened = whiten(spectra)
    station_count, comps, parts, bin_count = whitened.shape
    row_width = comps * parts * bin_count
    slot_count = send_rows.shape[2]
    cores = lax.axis_size("core")
    part_bins = bin_count // cores
    core = lax.axis_index("core")

    flat = whitened.reshape(station_count, row_width)
    lists = send_rows[0]
    col_count = lists.shape[0]
    picked = jnp.take(flat, lists.reshape(-1), axis=0).reshape(col_count, slot_count, row_width)
    alive = jnp.arange(slot_count, dtype=jnp.int32)[None, :] < send_counts[0][:, None]
    picked = jnp.where(alive[:, :, None], picked, jnp.zeros_like(picked))
    pieces = picked.reshape(col_count, slot_count, comps * parts, cores, SUBS,
                            part_bins // SUBS)
    pieces = jnp.transpose(pieces, (3, 0, 1, 4, 2, 5)).reshape(
        cores * col_count, slot_count, comps * parts * part_bins)
    pair_total = pair_rows.shape[1]
    panel, chip_pairs, chip_counts = spread(pieces, pair_rows, pair_counts, lax.axis_size("z"),
                                            cores * col_count, col_count)
    lag_rows = lag_tables(bin_count)
    core_arr = core.astype(jnp.int32)[None]
    partial = pair_sums(chip_counts, core_arr, chip_pairs, panel, lag_rows, cores, 0, None)
    total = exchange(partial, 1.0 / math.sqrt(bin_count))[:, :LAGS, :]
    return jnp.transpose(total, (1, 0, 2))


def solution(mesh):
    tile_size = mesh.shape["tile"]
    blk_size = mesh.shape["blk"]
    split = Mesh(mesh.devices.reshape(tile_size // 2, 2, blk_size), ("z", "core", "blk"))
    dev = ("z", "core", "blk")
    return jax.shard_map(
        shards,
        mesh=split,
        in_specs=(
            P(dev, None, None, None),
            P(dev, None, None),
            P(dev, None),
            P(None, dev),
            P(dev),
        ),
        out_specs=P(None, None, dev),
        check_vma=False,
    )
```

```python
import functools
import math

import jax
import ml_dtypes
import numpy as np
import jax.numpy as jnp
from jax import lax
from jax.experimental import pallas as pl
from jax.experimental.pallas import tpu as pltpu
from jax.sharding import Mesh
from jax.sharding import PartitionSpec as P

LAGS = 129
LAG_ROWS = 136
PAIR_BLOCK = 128
BIN_CHUNK = 256
GATHER_CHUNK = 512
SUBS = 2


def whiten(spectra):
    station_count = spectra.shape[0]
    bin_count = spectra.shape[-1]
    ramp_bins = bin_count // 32
    bin_index = jnp.arange(bin_count, dtype=jnp.int32)
    edge_dist = jnp.minimum(bin_index, bin_count - 1 - bin_index).astype(jnp.float32) + 0.5
    ramp_vals = 0.5 - 0.5 * jnp.cos(jnp.pi * edge_dist / ramp_bins)
    taper = jnp.where(edge_dist < ramp_bins, ramp_vals, jnp.ones_like(ramp_vals))
    blocked = spectra.reshape(station_count, 3, 2, bin_count // 64, 64)
    power = jnp.mean(blocked * blocked, axis=(1, 2, 4))
    inverse = 1.0 / jnp.sqrt(power + 1e-05)
    spread_scale = jnp.repeat(inverse, 64, axis=1)
    return (spectra * taper * spread_scale[:, None, None, :]).astype(jnp.bfloat16)


def lag_tables(bin_count):
    lag_index = np.arange(LAGS, dtype=np.int32) - LAGS // 2
    bin_index = np.arange(bin_count, dtype=np.int32)
    phase_steps = lag_index[:, None] * bin_index[None, :] % (2 * bin_count)
    angle = phase_steps.astype(np.float32) * np.float32(np.pi / bin_count)
    pad = ((0, LAG_ROWS - LAGS), (0, 0))
    cos_rows = np.pad(np.cos(angle).astype(np.float32).astype(ml_dtypes.bfloat16), pad)
    sin_rows = np.pad((-np.sin(angle)).astype(np.float32).astype(ml_dtypes.bfloat16), pad)
    chunks = bin_count // BIN_CHUNK
    both = np.stack([cos_rows.reshape(LAG_ROWS, chunks, BIN_CHUNK),
                     sin_rows.reshape(LAG_ROWS, chunks, BIN_CHUNK)], axis=2)
    return jnp.asarray(both.reshape(LAG_ROWS, 2 * bin_count))


def pair_kernel(counts_ref, core_ref, pairs_ref, panel_ref, lag_ref, *rest,
                blocks_per_owner, part_bins, accumulate):
    if accumulate:
        acc_ref, out_ref, f_scr, s_scr = rest
    else:
        out_ref, f_scr, s_scr = rest
    step = pl.program_id(0)
    owner = step // blocks_per_owner
    start = (step % blocks_per_owner) * PAIR_BLOCK
    live = start < counts_ref[owner, 0]
    if accumulate:
        out_ref[...] = acc_ref[...]
    else:
        out_ref[...] = jnp.zeros_like(out_ref)

    @pl.when(live)
    def _():
        rows = panel_ref.shape[0]
        width = panel_ref.shape[1]
        iota = lax.broadcasted_iota(jnp.int32, (rows, PAIR_BLOCK), 0)
        idx = pairs_ref[0]
        pick_first = jnp.where(idx[0:1, :] == iota, 1.0, 0.0).T.astype(jnp.bfloat16)
        pick_second = jnp.where(idx[1:2, :] == iota, 1.0, 0.0).T.astype(jnp.bfloat16)
        pick = jnp.concatenate([pick_first, pick_second], axis=0)
        gather_chunk = min(GATHER_CHUNK, width)

        def gather(c, carry):
            off = pl.multiple_of(c * gather_chunk, gather_chunk)
            block = panel_ref[:, pl.ds(off, gather_chunk)]
            both = jnp.dot(pick, block, preferred_element_type=jnp.float32)
            f_scr[:, pl.ds(off, gather_chunk)] = both[:PAIR_BLOCK]
            s_scr[:, pl.ds(off, gather_chunk)] = both[PAIR_BLOCK:]
            return carry

        lax.fori_loop(0, width // gather_chunk, gather, 0)
        nt = (((1,), (1,)), ((), ()))
        sub_bins = part_bins // SUBS
        bin_chunk = min(BIN_CHUNK, sub_bins)
        for sub in range(SUBS):
            col0 = sub * 6 * sub_bins

            def chunk(kc, carry):
                off = pl.multiple_of(kc * bin_chunk, bin_chunk)
                lag_blk = lag_ref[:, pl.ds(2 * (sub * sub_bins + off), 2 * bin_chunk)]
                for a in range(3):
                    f_re = f_scr[:, pl.ds(col0 + 2 * a * sub_bins + off, bin_chunk)]
                    f_im = f_scr[:, pl.ds(col0 + (2 * a + 1) * sub_bins + off, bin_chunk)]
                    for b in range(3):
                        s_re = s_scr[:, pl.ds(col0 + 2 * b * sub_bins + off, bin_chunk)]
                        s_im = s_scr[:, pl.ds(col0 + (2 * b + 1) * sub_bins + off, bin_chunk)]
                        real_part = (f_re * s_re + f_im * s_im).astype(jnp.bfloat16)
                        imag_part = (f_im * s_re - f_re * s_im).astype(jnp.bfloat16)
                        both = jnp.concatenate([real_part, imag_part], axis=1)
                        acc = lax.dot_general(lag_blk, both, nt,
                                              preferred_element_type=jnp.float32)
                        out_ref[0, 3 * a + b] += acc
                return carry

            lax.fori_loop(0, sub_bins // bin_chunk, chunk, 0)
        column = start + lax.broadcasted_iota(jnp.int32, out_ref.shape, 3)
        out_ref[...] = jnp.where(column < counts_ref[owner, 0], out_ref[...], 0.0)


def pair_sums(counts, core_arr, chip_pairs, panel, lag_rows, owners, chunk_id, acc):
    rows, width = panel.shape
    part_bins = width // 6
    pairs = chip_pairs.shape[0] * chip_pairs.shape[2]
    per_owner = pairs // owners
    blocks_per_owner = per_owner // PAIR_BLOCK
    grid = (pairs // PAIR_BLOCK,)
    accumulate = acc is not None
    kernel = functools.partial(pair_kernel, blocks_per_owner=blocks_per_owner,
                               part_bins=part_bins, accumulate=accumulate)
    flops = 2 * pairs * rows * width * 2 + 2 * LAG_ROWS * 2 * part_bins * 9 * pairs
    out_bytes = owners * 9 * LAG_ROWS * per_owner * 4
    cost = pl.CostEstimate(flops=flops, transcendentals=0,
                           bytes_accessed=rows * width * 2 + out_bytes * (2 if accumulate else 1))
    out_spec = pl.BlockSpec(
        (1, 9, LAG_ROWS, PAIR_BLOCK),
        lambda i, c, k: (i // blocks_per_owner, 0, 0, i % blocks_per_owner))
    in_specs = [
        pl.BlockSpec((1, 2, PAIR_BLOCK),
                     lambda i, c, k: (i // blocks_per_owner, 0, i % blocks_per_owner)),
        pl.BlockSpec((rows, width), lambda i, c, k: (0, 0)),
        pl.BlockSpec((LAG_ROWS, 2 * part_bins), lambda i, c, k: (0, k[0])),
    ]
    args = [counts, core_arr, chip_pairs, panel, lag_rows]
    aliases = {}
    if accumulate:
        in_specs.append(out_spec)
        args.append(acc)
        aliases = {len(args) - 1: 0}
    return pl.pallas_call(
        kernel,
        out_shape=jax.ShapeDtypeStruct((owners, 9, LAG_ROWS, per_owner), jnp.float32),
        grid_spec=pltpu.PrefetchScalarGridSpec(
            num_scalar_prefetch=2,
            grid=grid,
            in_specs=in_specs,
            out_specs=out_spec,
            scratch_shapes=[
                pltpu.VMEM((PAIR_BLOCK, width), jnp.float32),
                pltpu.VMEM((PAIR_BLOCK, width), jnp.float32),
            ],
        ),
        input_output_aliases=aliases,
        compiler_params=pltpu.CompilerParams(
            dimension_semantics=("arbitrary",), vmem_limit_bytes=60 * 1024 * 1024),
        cost_estimate=cost,
    )(*args)


MESH_ID = pl.DeviceIdType.MESH


def spread_kernel(pieces_ref, rows_ref, count_ref, panel_ref, chip_rows_ref, chip_count_ref,
                  send_plane, recv_plane,
                  local_sem, send_right, send_left, recv_ring, meta_sems, *, ring_size,
                  plane_size, blk_size, slots, subs):
    me_z = lax.axis_index("z")
    me_c = lax.axis_index("core")
    me_b = lax.axis_index("blk")
    me_q = me_c * blk_size + me_b
    right = (me_z + 1) % ring_size
    left = (me_z + ring_size - 1) % ring_size

    def plane_dev(q):
        return (me_z, q // blk_size, q % blk_size)

    barrier = pltpu.get_barrier_semaphore()

    def greet(i, carry):
        q = (me_q + i) % plane_size
        pl.semaphore_signal(barrier, 1, device_id=plane_dev(q), device_id_type=MESH_ID)
        return carry

    lax.fori_loop(1, plane_size, greet, 0)
    pl.semaphore_signal(barrier, 1, device_id=(right, me_c, me_b), device_id_type=MESH_ID)
    pl.semaphore_signal(barrier, 1, device_id=(left, me_c, me_b), device_id_type=MESH_ID)
    pl.semaphore_wait(barrier, plane_size + 1)

    partner = (me_z, 1 - me_c, me_b)
    meta_copies = []
    for idx, (src, dst) in enumerate(((rows_ref, chip_rows_ref), (count_ref, chip_count_ref))):
        local = pltpu.make_async_copy(src, dst.at[me_c], meta_sems.at[3 * idx])
        local.start()
        remote = pltpu.make_async_remote_copy(
            src, dst.at[me_c], meta_sems.at[3 * idx + 1], meta_sems.at[3 * idx + 2],
            device_id=partner, device_id_type=MESH_ID)
        remote.start()
        arrival = pltpu.make_async_remote_copy(
            src, dst.at[1 - me_c], meta_sems.at[3 * idx + 1], meta_sems.at[3 * idx + 2],
            device_id=partner, device_id_type=MESH_ID)
        meta_copies.append((local, remote, arrival))

    sub_width = panel_ref.shape[1] // subs
    block_rows = plane_size * slots
    half_rows = block_rows // 2
    base = me_z * block_rows
    half = ring_size // 2

    def cols(sub):
        return pl.ds(sub * sub_width, sub_width)

    def rows_of(q, sub):
        return panel_ref.at[pl.ds(base + q * slots, slots), cols(sub)]

    def local_copy(sub):
        return pltpu.make_async_copy(
            pieces_ref.at[me_q, :, cols(sub)], rows_of(me_q, sub), local_sem.at[sub])

    def plane_copy(q, src_q, sub):
        return pltpu.make_async_remote_copy(
            pieces_ref.at[q, :, cols(sub)], rows_of(src_q, sub), send_plane.at[sub, q],
            recv_plane.at[sub, src_q], device_id=plane_dev(q), device_id_type=MESH_ID)

    def scatter(sub):
        local_copy(sub).start()

        def send(i, carry):
            q = (me_q + i) % plane_size
            plane_copy(q, me_q, sub).start()
            return carry

        lax.fori_loop(1, plane_size, send, 0)

    def gathered(sub):
        def arrive(i, carry):
            q = (me_q + plane_size - i) % plane_size
            plane_copy(q, q, sub).wait_recv()
            return carry

        lax.fori_loop(1, plane_size, arrive, 0)
        local_copy(sub).wait()

    def block_of(k, sub):
        return panel_ref.at[pl.ds(k * block_rows, block_rows), cols(sub)]

    def part_of(k, first, sub):
        start = k * block_rows + (0 if first else half_rows)
        return panel_ref.at[pl.ds(start, half_rows), cols(sub)]

    def ring_copy(k, sem, dev, sub):
        return pltpu.make_async_remote_copy(
            block_of(k, sub), block_of(k, sub), sem, recv_ring.at[sub, k],
            device_id=(dev, me_c, me_b), device_id_type=MESH_ID)

    def part_copy(k, first, sem, dev, sub):
        slot = k if first else ring_size
        return pltpu.make_async_remote_copy(
            part_of(k, first, sub), part_of(k, first, sub), sem, recv_ring.at[sub, slot],
            device_id=(dev, me_c, me_b), device_id_type=MESH_ID)

    sends = []

    def ring_step(s, sub):
        k = (me_z + ring_size - s) % ring_size
        if s > 0:
            ring_copy(k, send_right.at[sub, s], left, sub).wait_recv()
        c = ring_copy(k, send_right.at[sub, s], right, sub) if s < half - 1 else part_copy(
            k, True, send_right.at[sub, s], right, sub)
        c.start()
        sends.append(c)
        k = (me_z + s) % ring_size
        if s > 0:
            ring_copy(k, send_left.at[sub, s], right, sub).wait_recv()
        c = ring_copy(k, send_left.at[sub, s], left, sub) if s < half - 1 else part_copy(
            k, False, send_left.at[sub, s], left, sub)
        c.start()
        sends.append(c)

    for sub in range(subs):
        scatter(sub)
        gathered(sub)
        ring_step(0, sub)
    for s in range(1, half):
        for sub in range(subs):
            ring_step(s, sub)
    far = (me_z + half) % ring_size
    for sub in range(subs):
        part_copy(far, True, send_right.at[sub, 0], left, sub).wait_recv()
        part_copy(far, False, send_left.at[sub, 0], right, sub).wait_recv()
    for sub in range(subs):
        def sent(i, carry):
            q = (me_q + i) % plane_size
            plane_copy(q, me_q, sub).wait_send()
            return carry

        lax.fori_loop(1, plane_size, sent, 0)
    for c in sends:
        c.wait_send()
    for local, remote, arrival in meta_copies:
        local.wait()
        arrival.wait_recv()
        remote.wait_send()


def spread(pieces, pair_rows, pair_counts, ring_size, plane_size, blk_size):
    _, slots, width = pieces.shape
    rows = ring_size * plane_size * slots
    kernel = functools.partial(spread_kernel, ring_size=ring_size, plane_size=plane_size,
                               blk_size=blk_size, slots=slots, subs=SUBS)
    half = ring_size // 2
    return pl.pallas_call(
        kernel,
        out_shape=(jax.ShapeDtypeStruct((rows, width), pieces.dtype),
                   jax.ShapeDtypeStruct((2,) + pair_rows.shape, pair_rows.dtype),
                   jax.ShapeDtypeStruct((2,) + pair_counts.shape, pair_counts.dtype)),
        in_specs=[pl.BlockSpec(memory_space=pl.ANY)] * 3,
        out_specs=(pl.BlockSpec(memory_space=pl.ANY),) * 3,
        scratch_shapes=[
            pltpu.SemaphoreType.DMA((SUBS, plane_size)),
            pltpu.SemaphoreType.DMA((SUBS, plane_size)),
            pltpu.SemaphoreType.DMA((SUBS,)),
            pltpu.SemaphoreType.DMA((SUBS, half)),
            pltpu.SemaphoreType.DMA((SUBS, half)),
            pltpu.SemaphoreType.DMA((SUBS, ring_size + 1)),
            pltpu.SemaphoreType.DMA((6,)),
        ],
        compiler_params=pltpu.CompilerParams(collective_id=0, has_side_effects=True),
    )(pieces, pair_rows, pair_counts)


def exchange_kernel(part_ref, out_ref, mine_buf, recv_buf, sems, *, scale):
    me_z = lax.axis_index("z")
    me_c = lax.axis_index("core")
    me_b = lax.axis_index("blk")
    partner = (me_z, 1 - me_c, me_b)
    local = pltpu.make_async_copy(part_ref.at[me_c], mine_buf, sems.at[2])
    local.start()
    barrier = pltpu.get_barrier_semaphore()
    pl.semaphore_signal(barrier, 1, device_id=partner, device_id_type=MESH_ID)
    pl.semaphore_wait(barrier, 1)
    copy = pltpu.make_async_remote_copy(
        part_ref.at[1 - me_c], recv_buf, sems.at[0], sems.at[1],
        device_id=partner, device_id_type=MESH_ID)
    copy.start()
    local.wait()
    copy.wait()
    out_ref[...] = ((mine_buf[...] + recv_buf[...]) * scale).astype(out_ref.dtype)


def exchange(partial, scale):
    shape = partial.shape[1:]
    return pl.pallas_call(
        functools.partial(exchange_kernel, scale=scale),
        out_shape=jax.ShapeDtypeStruct(shape, jnp.bfloat16),
        in_specs=[pl.BlockSpec(memory_space=pl.ANY)],
        out_specs=pl.BlockSpec(memory_space=pltpu.VMEM),
        scratch_shapes=[
            pltpu.VMEM(shape, partial.dtype),
            pltpu.VMEM(shape, partial.dtype),
            pltpu.SemaphoreType.DMA((3,)),
        ],
        compiler_params=pltpu.CompilerParams(collective_id=1, has_side_effects=True),
    )(partial)


def shards(spectra, send_rows, send_counts, pair_rows, pair_counts):
    whitened = whiten(spectra)
    station_count, comps, parts, bin_count = whitened.shape
    row_width = comps * parts * bin_count
    slot_count = send_rows.shape[2]
    cores = lax.axis_size("core")
    part_bins = bin_count // cores
    core = lax.axis_index("core")

    flat = whitened.reshape(station_count, row_width)
    lists = send_rows[0]
    col_count = lists.shape[0]
    picked = jnp.take(flat, lists.reshape(-1), axis=0).reshape(col_count, slot_count, row_width)
    alive = jnp.arange(slot_count, dtype=jnp.int32)[None, :] < send_counts[0][:, None]
    picked = jnp.where(alive[:, :, None], picked, jnp.zeros_like(picked))
    pieces = picked.reshape(col_count, slot_count, comps * parts, cores, SUBS,
                            part_bins // SUBS)
    pieces = jnp.transpose(pieces, (3, 0, 1, 4, 2, 5)).reshape(
        cores * col_count, slot_count, comps * parts * part_bins)
    pair_total = pair_rows.shape[1]
    panel, chip_pairs, chip_counts = spread(pieces, pair_rows, pair_counts, lax.axis_size("z"),
                                            cores * col_count, col_count)
    lag_rows = lag_tables(bin_count)
    core_arr = core.astype(jnp.int32)[None]
    partial = pair_sums(chip_counts, core_arr, chip_pairs, panel, lag_rows, cores, 0, None)
    total = exchange(partial, 1.0 / math.sqrt(bin_count))[:, :LAGS, :]
    return jnp.transpose(total, (1, 0, 2))


def solution(mesh):
    tile_size = mesh.shape["tile"]
    blk_size = mesh.shape["blk"]
    split = Mesh(mesh.devices.reshape(tile_size // 2, 2, blk_size), ("z", "core", "blk"))
    dev = ("z", "core", "blk")
    return jax.shard_map(
        shards,
        mesh=split,
        in_specs=(
            P(dev, None, None, None),
            P(dev, None, None),
            P(dev, None),
            P(None, dev),
            P(dev),
        ),
        out_specs=P(None, None, dev),
        check_vma=False,
    )
```

```python
import functools
import math

import jax
import ml_dtypes
import numpy as np
import jax.numpy as jnp
from jax import lax
from jax.experimental import pallas as pl
from jax.experimental.pallas import tpu as pltpu
from jax.sharding import Mesh
from jax.sharding import PartitionSpec as P

LAGS = 129
LAG_ROWS = 144
PAIR_BLOCK = 128
BIN_CHUNK = 256
GATHER_CHUNK = 512
SUBS = 2


def whiten(spectra):
    station_count = spectra.shape[0]
    bin_count = spectra.shape[-1]
    ramp_bins = bin_count // 32
    bin_index = jnp.arange(bin_count, dtype=jnp.int32)
    edge_dist = jnp.minimum(bin_index, bin_count - 1 - bin_index).astype(jnp.float32) + 0.5
    ramp_vals = 0.5 - 0.5 * jnp.cos(jnp.pi * edge_dist / ramp_bins)
    taper = jnp.where(edge_dist < ramp_bins, ramp_vals, jnp.ones_like(ramp_vals))
    blocked = spectra.reshape(station_count, 3, 2, bin_count // 64, 64)
    power = jnp.mean(blocked * blocked, axis=(1, 2, 4))
    inverse = 1.0 / jnp.sqrt(power + 1e-05)
    spread_scale = jnp.repeat(inverse, 64, axis=1)
    return (spectra * taper * spread_scale[:, None, None, :]).astype(jnp.bfloat16)


def lag_tables(bin_count):
    lag_index = np.arange(LAGS, dtype=np.int32) - LAGS // 2
    bin_index = np.arange(bin_count, dtype=np.int32)
    phase_steps = lag_index[:, None] * bin_index[None, :] % (2 * bin_count)
    angle = phase_steps.astype(np.float32) * np.float32(np.pi / bin_count)
    pad = ((0, LAG_ROWS - LAGS), (0, 0))
    cos_rows = np.pad(np.cos(angle).astype(np.float32).astype(ml_dtypes.bfloat16), pad)
    sin_rows = np.pad((-np.sin(angle)).astype(np.float32).astype(ml_dtypes.bfloat16), pad)
    chunks = bin_count // BIN_CHUNK
    both = np.stack([cos_rows.reshape(LAG_ROWS, chunks, BIN_CHUNK),
                     sin_rows.reshape(LAG_ROWS, chunks, BIN_CHUNK)], axis=2)
    return jnp.asarray(both.reshape(LAG_ROWS, 2 * bin_count))


def pair_kernel(counts_ref, core_ref, pairs_ref, panel_ref, lag_ref, *rest,
                blocks_per_owner, part_bins, accumulate):
    if accumulate:
        acc_ref, out_ref, f_scr, s_scr = rest
    else:
        out_ref, f_scr, s_scr = rest
    step = pl.program_id(0)
    owner = step // blocks_per_owner
    start = (step % blocks_per_owner) * PAIR_BLOCK
    live = start < counts_ref[owner, 0]
    if accumulate:
        out_ref[...] = acc_ref[...]
    else:
        out_ref[...] = jnp.zeros_like(out_ref)

    @pl.when(live)
    def _():
        rows = panel_ref.shape[0]
        width = panel_ref.shape[1]
        iota = lax.broadcasted_iota(jnp.int32, (rows, PAIR_BLOCK), 0)
        idx = pairs_ref[0]
        pick_first = jnp.where(idx[0:1, :] == iota, 1.0, 0.0).T.astype(jnp.bfloat16)
        pick_second = jnp.where(idx[1:2, :] == iota, 1.0, 0.0).T.astype(jnp.bfloat16)
        pick = jnp.concatenate([pick_first, pick_second], axis=0)
        gather_chunk = min(GATHER_CHUNK, width)

        def gather(c, carry):
            off = pl.multiple_of(c * gather_chunk, gather_chunk)
            block = panel_ref[:, pl.ds(off, gather_chunk)]
            both = jnp.dot(pick, block, preferred_element_type=jnp.float32)
            f_scr[:, pl.ds(off, gather_chunk)] = both[:PAIR_BLOCK]
            s_scr[:, pl.ds(off, gather_chunk)] = both[PAIR_BLOCK:]
            return carry

        lax.fori_loop(0, width // gather_chunk, gather, 0)
        nt = (((1,), (1,)), ((), ()))
        sub_bins = part_bins // SUBS
        bin_chunk = min(BIN_CHUNK, sub_bins)
        for sub in range(SUBS):
            col0 = sub * 6 * sub_bins

            def chunk(kc, carry):
                off = pl.multiple_of(kc * bin_chunk, bin_chunk)
                lag_blk = lag_ref[:, pl.ds(2 * (sub * sub_bins + off), 2 * bin_chunk)]
                for a in range(3):
                    f_re = f_scr[:, pl.ds(col0 + 2 * a * sub_bins + off, bin_chunk)]
                    f_im = f_scr[:, pl.ds(col0 + (2 * a + 1) * sub_bins + off, bin_chunk)]
                    for b in range(3):
                        s_re = s_scr[:, pl.ds(col0 + 2 * b * sub_bins + off, bin_chunk)]
                        s_im = s_scr[:, pl.ds(col0 + (2 * b + 1) * sub_bins + off, bin_chunk)]
                        real_part = (f_re * s_re + f_im * s_im).astype(jnp.bfloat16)
                        imag_part = (f_im * s_re - f_re * s_im).astype(jnp.bfloat16)
                        both = jnp.concatenate([real_part, imag_part], axis=1)
                        acc = lax.dot_general(lag_blk, both, nt,
                                              preferred_element_type=jnp.float32)
                        out_ref[0, 3 * a + b] += acc
                return carry

            lax.fori_loop(0, sub_bins // bin_chunk, chunk, 0)
        column = start + lax.broadcasted_iota(jnp.int32, out_ref.shape, 3)
        out_ref[...] = jnp.where(column < counts_ref[owner, 0], out_ref[...], 0.0)


def pair_sums(counts, core_arr, chip_pairs, panel, lag_rows, owners, chunk_id, acc):
    rows, width = panel.shape
    part_bins = width // 6
    pairs = chip_pairs.shape[0] * chip_pairs.shape[2]
    per_owner = pairs // owners
    blocks_per_owner = per_owner // PAIR_BLOCK
    grid = (pairs // PAIR_BLOCK,)
    accumulate = acc is not None
    kernel = functools.partial(pair_kernel, blocks_per_owner=blocks_per_owner,
                               part_bins=part_bins, accumulate=accumulate)
    flops = 2 * pairs * rows * width * 2 + 2 * LAG_ROWS * 2 * part_bins * 9 * pairs
    out_bytes = owners * 9 * LAG_ROWS * per_owner * 4
    cost = pl.CostEstimate(flops=flops, transcendentals=0,
                           bytes_accessed=rows * width * 2 + out_bytes * (2 if accumulate else 1))
    out_spec = pl.BlockSpec(
        (1, 9, LAG_ROWS, PAIR_BLOCK),
        lambda i, c, k: (i // blocks_per_owner, 0, 0, i % blocks_per_owner))
    in_specs = [
        pl.BlockSpec((1, 2, PAIR_BLOCK),
                     lambda i, c, k: (i // blocks_per_owner, 0, i % blocks_per_owner)),
        pl.BlockSpec((rows, width), lambda i, c, k: (0, 0)),
        pl.BlockSpec((LAG_ROWS, 2 * part_bins), lambda i, c, k: (0, k[0])),
    ]
    args = [counts, core_arr, chip_pairs, panel, lag_rows]
    aliases = {}
    if accumulate:
        in_specs.append(out_spec)
        args.append(acc)
        aliases = {len(args) - 1: 0}
    return pl.pallas_call(
        kernel,
        out_shape=jax.ShapeDtypeStruct((owners, 9, LAG_ROWS, per_owner), jnp.float32),
        grid_spec=pltpu.PrefetchScalarGridSpec(
            num_scalar_prefetch=2,
            grid=grid,
            in_specs=in_specs,
            out_specs=out_spec,
            scratch_shapes=[
                pltpu.VMEM((PAIR_BLOCK, width), jnp.float32),
                pltpu.VMEM((PAIR_BLOCK, width), jnp.float32),
            ],
        ),
        input_output_aliases=aliases,
        compiler_params=pltpu.CompilerParams(
            dimension_semantics=("arbitrary",), vmem_limit_bytes=60 * 1024 * 1024),
        cost_estimate=cost,
    )(*args)


MESH_ID = pl.DeviceIdType.MESH


def spread_kernel(pieces_ref, rows_ref, count_ref, panel_ref, chip_rows_ref, chip_count_ref,
                  send_plane, recv_plane,
                  local_sem, send_right, send_left, recv_ring, meta_sems, *, ring_size,
                  plane_size, blk_size, slots, subs):
    me_z = lax.axis_index("z")
    me_c = lax.axis_index("core")
    me_b = lax.axis_index("blk")
    me_q = me_c * blk_size + me_b
    right = (me_z + 1) % ring_size
    left = (me_z + ring_size - 1) % ring_size

    def plane_dev(q):
        return (me_z, q // blk_size, q % blk_size)

    barrier = pltpu.get_barrier_semaphore()

    def greet(i, carry):
        q = (me_q + i) % plane_size
        pl.semaphore_signal(barrier, 1, device_id=plane_dev(q), device_id_type=MESH_ID)
        return carry

    lax.fori_loop(1, plane_size, greet, 0)
    pl.semaphore_signal(barrier, 1, device_id=(right, me_c, me_b), device_id_type=MESH_ID)
    pl.semaphore_signal(barrier, 1, device_id=(left, me_c, me_b), device_id_type=MESH_ID)
    pl.semaphore_wait(barrier, plane_size + 1)

    partner = (me_z, 1 - me_c, me_b)
    meta_copies = []
    for idx, (src, dst) in enumerate(((rows_ref, chip_rows_ref), (count_ref, chip_count_ref))):
        local = pltpu.make_async_copy(src, dst.at[me_c], meta_sems.at[3 * idx])
        local.start()
        remote = pltpu.make_async_remote_copy(
            src, dst.at[me_c], meta_sems.at[3 * idx + 1], meta_sems.at[3 * idx + 2],
            device_id=partner, device_id_type=MESH_ID)
        remote.start()
        arrival = pltpu.make_async_remote_copy(
            src, dst.at[1 - me_c], meta_sems.at[3 * idx + 1], meta_sems.at[3 * idx + 2],
            device_id=partner, device_id_type=MESH_ID)
        meta_copies.append((local, remote, arrival))

    sub_width = panel_ref.shape[1] // subs
    block_rows = plane_size * slots
    half_rows = block_rows // 2
    base = me_z * block_rows
    half = ring_size // 2

    def cols(sub):
        return pl.ds(sub * sub_width, sub_width)

    def rows_of(q, sub):
        return panel_ref.at[pl.ds(base + q * slots, slots), cols(sub)]

    def local_copy(sub):
        return pltpu.make_async_copy(
            pieces_ref.at[me_q, :, cols(sub)], rows_of(me_q, sub), local_sem.at[sub])

    def plane_copy(q, src_q, sub):
        return pltpu.make_async_remote_copy(
            pieces_ref.at[q, :, cols(sub)], rows_of(src_q, sub), send_plane.at[sub, q],
            recv_plane.at[sub, src_q], device_id=plane_dev(q), device_id_type=MESH_ID)

    def scatter(sub):
        local_copy(sub).start()

        def send(i, carry):
            q = (me_q + i) % plane_size
            plane_copy(q, me_q, sub).start()
            return carry

        lax.fori_loop(1, plane_size, send, 0)

    def gathered(sub):
        def arrive(i, carry):
            q = (me_q + plane_size - i) % plane_size
            plane_copy(q, q, sub).wait_recv()
            return carry

        lax.fori_loop(1, plane_size, arrive, 0)
        local_copy(sub).wait()

    def block_of(k, sub):
        return panel_ref.at[pl.ds(k * block_rows, block_rows), cols(sub)]

    def part_of(k, first, sub):
        start = k * block_rows + (0 if first else half_rows)
        return panel_ref.at[pl.ds(start, half_rows), cols(sub)]

    def ring_copy(k, sem, dev, sub):
        return pltpu.make_async_remote_copy(
            block_of(k, sub), block_of(k, sub), sem, recv_ring.at[sub, k],
            device_id=(dev, me_c, me_b), device_id_type=MESH_ID)

    def part_copy(k, first, sem, dev, sub):
        slot = k if first else ring_size
        return pltpu.make_async_remote_copy(
            part_of(k, first, sub), part_of(k, first, sub), sem, recv_ring.at[sub, slot],
            device_id=(dev, me_c, me_b), device_id_type=MESH_ID)

    sends = []

    def ring_step(s, sub):
        k = (me_z + ring_size - s) % ring_size
        if s > 0:
            ring_copy(k, send_right.at[sub, s], left, sub).wait_recv()
        c = ring_copy(k, send_right.at[sub, s], right, sub) if s < half - 1 else part_copy(
            k, True, send_right.at[sub, s], right, sub)
        c.start()
        sends.append(c)
        k = (me_z + s) % ring_size
        if s > 0:
            ring_copy(k, send_left.at[sub, s], right, sub).wait_recv()
        c = ring_copy(k, send_left.at[sub, s], left, sub) if s < half - 1 else part_copy(
            k, False, send_left.at[sub, s], left, sub)
        c.start()
        sends.append(c)

    for sub in range(subs):
        scatter(sub)
    for sub in range(subs):
        gathered(sub)
        ring_step(0, sub)
    for s in range(1, half):
        for sub in range(subs):
            ring_step(s, sub)
    far = (me_z + half) % ring_size
    for sub in range(subs):
        part_copy(far, True, send_right.at[sub, 0], left, sub).wait_recv()
        part_copy(far, False, send_left.at[sub, 0], right, sub).wait_recv()
    for sub in range(subs):
        def sent(i, carry):
            q = (me_q + i) % plane_size
            plane_copy(q, me_q, sub).wait_send()
            return carry

        lax.fori_loop(1, plane_size, sent, 0)
    for c in sends:
        c.wait_send()
    for local, remote, arrival in meta_copies:
        local.wait()
        arrival.wait_recv()
        remote.wait_send()


def spread(pieces, pair_rows, pair_counts, ring_size, plane_size, blk_size):
    _, slots, width = pieces.shape
    rows = ring_size * plane_size * slots
    kernel = functools.partial(spread_kernel, ring_size=ring_size, plane_size=plane_size,
                               blk_size=blk_size, slots=slots, subs=SUBS)
    half = ring_size // 2
    return pl.pallas_call(
        kernel,
        out_shape=(jax.ShapeDtypeStruct((rows, width), pieces.dtype),
                   jax.ShapeDtypeStruct((2,) + pair_rows.shape, pair_rows.dtype),
                   jax.ShapeDtypeStruct((2,) + pair_counts.shape, pair_counts.dtype)),
        in_specs=[pl.BlockSpec(memory_space=pl.ANY)] * 3,
        out_specs=(pl.BlockSpec(memory_space=pl.ANY),) * 3,
        scratch_shapes=[
            pltpu.SemaphoreType.DMA((SUBS, plane_size)),
            pltpu.SemaphoreType.DMA((SUBS, plane_size)),
            pltpu.SemaphoreType.DMA((SUBS,)),
            pltpu.SemaphoreType.DMA((SUBS, half)),
            pltpu.SemaphoreType.DMA((SUBS, half)),
            pltpu.SemaphoreType.DMA((SUBS, ring_size + 1)),
            pltpu.SemaphoreType.DMA((6,)),
        ],
        compiler_params=pltpu.CompilerParams(collective_id=0, has_side_effects=True),
    )(pieces, pair_rows, pair_counts)


def exchange_kernel(part_ref, out_ref, mine_buf, recv_buf, sems, *, scale):
    me_z = lax.axis_index("z")
    me_c = lax.axis_index("core")
    me_b = lax.axis_index("blk")
    partner = (me_z, 1 - me_c, me_b)
    local = pltpu.make_async_copy(part_ref.at[me_c], mine_buf, sems.at[2])
    local.start()
    barrier = pltpu.get_barrier_semaphore()
    pl.semaphore_signal(barrier, 1, device_id=partner, device_id_type=MESH_ID)
    pl.semaphore_wait(barrier, 1)
    copy = pltpu.make_async_remote_copy(
        part_ref.at[1 - me_c], recv_buf, sems.at[0], sems.at[1],
        device_id=partner, device_id_type=MESH_ID)
    copy.start()
    local.wait()
    copy.wait()
    out_ref[...] = ((mine_buf[...] + recv_buf[...]) * scale).astype(out_ref.dtype)


def exchange(partial, scale):
    shape = partial.shape[1:]
    return pl.pallas_call(
        functools.partial(exchange_kernel, scale=scale),
        out_shape=jax.ShapeDtypeStruct(shape, jnp.bfloat16),
        in_specs=[pl.BlockSpec(memory_space=pl.ANY)],
        out_specs=pl.BlockSpec(memory_space=pltpu.VMEM),
        scratch_shapes=[
            pltpu.VMEM(shape, partial.dtype),
            pltpu.VMEM(shape, partial.dtype),
            pltpu.SemaphoreType.DMA((3,)),
        ],
        compiler_params=pltpu.CompilerParams(collective_id=1, has_side_effects=True),
    )(partial)


def shards(spectra, send_rows, send_counts, pair_rows, pair_counts):
    whitened = whiten(spectra)
    station_count, comps, parts, bin_count = whitened.shape
    row_width = comps * parts * bin_count
    slot_count = send_rows.shape[2]
    cores = lax.axis_size("core")
    part_bins = bin_count // cores
    core = lax.axis_index("core")

    flat = whitened.reshape(station_count, row_width)
    lists = send_rows[0]
    col_count = lists.shape[0]
    picked = jnp.take(flat, lists.reshape(-1), axis=0).reshape(col_count, slot_count, row_width)
    alive = jnp.arange(slot_count, dtype=jnp.int32)[None, :] < send_counts[0][:, None]
    picked = jnp.where(alive[:, :, None], picked, jnp.zeros_like(picked))
    pieces = picked.reshape(col_count, slot_count, comps * parts, cores, SUBS,
                            part_bins // SUBS)
    pieces = jnp.transpose(pieces, (3, 0, 1, 4, 2, 5)).reshape(
        cores * col_count, slot_count, comps * parts * part_bins)
    pair_total = pair_rows.shape[1]
    panel, chip_pairs, chip_counts = spread(pieces, pair_rows, pair_counts, lax.axis_size("z"),
                                            cores * col_count, col_count)
    lag_rows = lag_tables(bin_count)
    core_arr = core.astype(jnp.int32)[None]
    partial = pair_sums(chip_counts, core_arr, chip_pairs, panel, lag_rows, cores, 0, None)
    total = exchange(partial, 1.0 / math.sqrt(bin_count))[:, :LAGS, :]
    return jnp.transpose(total, (1, 0, 2))


def solution(mesh):
    tile_size = mesh.shape["tile"]
    blk_size = mesh.shape["blk"]
    split = Mesh(mesh.devices.reshape(tile_size // 2, 2, blk_size), ("z", "core", "blk"))
    dev = ("z", "core", "blk")
    return jax.shard_map(
        shards,
        mesh=split,
        in_specs=(
            P(dev, None, None, None),
            P(dev, None, None),
            P(dev, None),
            P(None, dev),
            P(dev),
        ),
        out_specs=P(None, None, dev),
        check_vma=False,
    )
```

```python
import functools
import math

import jax
import ml_dtypes
import numpy as np
import jax.numpy as jnp
from jax import lax
from jax.experimental import pallas as pl
from jax.experimental.pallas import tpu as pltpu
from jax.sharding import Mesh
from jax.sharding import PartitionSpec as P

LAGS = 129
LAG_ROWS = 144
PAIR_BLOCK = 128
BIN_CHUNK = 256
GATHER_CHUNK = 1024
SUBS = 2


def whiten(spectra):
    station_count = spectra.shape[0]
    bin_count = spectra.shape[-1]
    ramp_bins = bin_count // 32
    bin_index = jnp.arange(bin_count, dtype=jnp.int32)
    edge_dist = jnp.minimum(bin_index, bin_count - 1 - bin_index).astype(jnp.float32) + 0.5
    ramp_vals = 0.5 - 0.5 * jnp.cos(jnp.pi * edge_dist / ramp_bins)
    taper = jnp.where(edge_dist < ramp_bins, ramp_vals, jnp.ones_like(ramp_vals))
    blocked = spectra.reshape(station_count, 3, 2, bin_count // 64, 64)
    power = jnp.mean(blocked * blocked, axis=(1, 2, 4))
    inverse = 1.0 / jnp.sqrt(power + 1e-05)
    spread_scale = jnp.repeat(inverse, 64, axis=1)
    return (spectra * taper * spread_scale[:, None, None, :]).astype(jnp.bfloat16)


def lag_tables(bin_count):
    lag_index = np.arange(LAGS, dtype=np.int32) - LAGS // 2
    bin_index = np.arange(bin_count, dtype=np.int32)
    phase_steps = lag_index[:, None] * bin_index[None, :] % (2 * bin_count)
    angle = phase_steps.astype(np.float32) * np.float32(np.pi / bin_count)
    pad = ((0, LAG_ROWS - LAGS), (0, 0))
    cos_rows = np.pad(np.cos(angle).astype(np.float32).astype(ml_dtypes.bfloat16), pad)
    sin_rows = np.pad((-np.sin(angle)).astype(np.float32).astype(ml_dtypes.bfloat16), pad)
    chunks = bin_count // BIN_CHUNK
    both = np.stack([cos_rows.reshape(LAG_ROWS, chunks, BIN_CHUNK),
                     sin_rows.reshape(LAG_ROWS, chunks, BIN_CHUNK)], axis=2)
    return jnp.asarray(both.reshape(LAG_ROWS, 2 * bin_count))


def pair_kernel(counts_ref, core_ref, pairs_ref, panel_ref, lag_ref, *rest,
                blocks_per_owner, part_bins, accumulate):
    if accumulate:
        acc_ref, out_ref, f_scr, s_scr = rest
    else:
        out_ref, f_scr, s_scr = rest
    step = pl.program_id(0)
    owner = step // blocks_per_owner
    start = (step % blocks_per_owner) * PAIR_BLOCK
    live = start < counts_ref[owner, 0]
    if accumulate:
        out_ref[...] = acc_ref[...]
    else:
        out_ref[...] = jnp.zeros_like(out_ref)

    @pl.when(live)
    def _():
        rows = panel_ref.shape[0]
        width = panel_ref.shape[1]
        iota = lax.broadcasted_iota(jnp.int32, (rows, PAIR_BLOCK), 0)
        idx = pairs_ref[0]
        pick_first = jnp.where(idx[0:1, :] == iota, 1.0, 0.0).T.astype(jnp.bfloat16)
        pick_second = jnp.where(idx[1:2, :] == iota, 1.0, 0.0).T.astype(jnp.bfloat16)
        pick = jnp.concatenate([pick_first, pick_second], axis=0)
        gather_chunk = min(GATHER_CHUNK, width)

        def gather(c, carry):
            off = pl.multiple_of(c * gather_chunk, gather_chunk)
            block = panel_ref[:, pl.ds(off, gather_chunk)]
            both = jnp.dot(pick, block, preferred_element_type=jnp.float32)
            f_scr[:, pl.ds(off, gather_chunk)] = both[:PAIR_BLOCK]
            s_scr[:, pl.ds(off, gather_chunk)] = both[PAIR_BLOCK:]
            return carry

        lax.fori_loop(0, width // gather_chunk, gather, 0)
        nt = (((1,), (1,)), ((), ()))
        sub_bins = part_bins // SUBS
        bin_chunk = min(BIN_CHUNK, sub_bins)
        for sub in range(SUBS):
            col0 = sub * 6 * sub_bins

            def chunk(kc, carry):
                off = pl.multiple_of(kc * bin_chunk, bin_chunk)
                lag_blk = lag_ref[:, pl.ds(2 * (sub * sub_bins + off), 2 * bin_chunk)]
                for a in range(3):
                    f_re = f_scr[:, pl.ds(col0 + 2 * a * sub_bins + off, bin_chunk)]
                    f_im = f_scr[:, pl.ds(col0 + (2 * a + 1) * sub_bins + off, bin_chunk)]
                    for b in range(3):
                        s_re = s_scr[:, pl.ds(col0 + 2 * b * sub_bins + off, bin_chunk)]
                        s_im = s_scr[:, pl.ds(col0 + (2 * b + 1) * sub_bins + off, bin_chunk)]
                        real_part = (f_re * s_re + f_im * s_im).astype(jnp.bfloat16)
                        imag_part = (f_im * s_re - f_re * s_im).astype(jnp.bfloat16)
                        both = jnp.concatenate([real_part, imag_part], axis=1)
                        acc = lax.dot_general(lag_blk, both, nt,
                                              preferred_element_type=jnp.float32)
                        out_ref[0, 3 * a + b] += acc
                return carry

            lax.fori_loop(0, sub_bins // bin_chunk, chunk, 0)
        column = start + lax.broadcasted_iota(jnp.int32, out_ref.shape, 3)
        out_ref[...] = jnp.where(column < counts_ref[owner, 0], out_ref[...], 0.0)


def pair_sums(counts, core_arr, chip_pairs, panel, lag_rows, owners, chunk_id, acc):
    rows, width = panel.shape
    part_bins = width // 6
    pairs = chip_pairs.shape[0] * chip_pairs.shape[2]
    per_owner = pairs // owners
    blocks_per_owner = per_owner // PAIR_BLOCK
    grid = (pairs // PAIR_BLOCK,)
    accumulate = acc is not None
    kernel = functools.partial(pair_kernel, blocks_per_owner=blocks_per_owner,
                               part_bins=part_bins, accumulate=accumulate)
    flops = 2 * pairs * rows * width * 2 + 2 * LAG_ROWS * 2 * part_bins * 9 * pairs
    out_bytes = owners * 9 * LAG_ROWS * per_owner * 4
    cost = pl.CostEstimate(flops=flops, transcendentals=0,
                           bytes_accessed=rows * width * 2 + out_bytes * (2 if accumulate else 1))
    out_spec = pl.BlockSpec(
        (1, 9, LAG_ROWS, PAIR_BLOCK),
        lambda i, c, k: (i // blocks_per_owner, 0, 0, i % blocks_per_owner))
    in_specs = [
        pl.BlockSpec((1, 2, PAIR_BLOCK),
                     lambda i, c, k: (i // blocks_per_owner, 0, i % blocks_per_owner)),
        pl.BlockSpec((rows, width), lambda i, c, k: (0, 0)),
        pl.BlockSpec((LAG_ROWS, 2 * part_bins), lambda i, c, k: (0, k[0])),
    ]
    args = [counts, core_arr, chip_pairs, panel, lag_rows]
    aliases = {}
    if accumulate:
        in_specs.append(out_spec)
        args.append(acc)
        aliases = {len(args) - 1: 0}
    return pl.pallas_call(
        kernel,
        out_shape=jax.ShapeDtypeStruct((owners, 9, LAG_ROWS, per_owner), jnp.float32),
        grid_spec=pltpu.PrefetchScalarGridSpec(
            num_scalar_prefetch=2,
            grid=grid,
            in_specs=in_specs,
            out_specs=out_spec,
            scratch_shapes=[
                pltpu.VMEM((PAIR_BLOCK, width), jnp.float32),
                pltpu.VMEM((PAIR_BLOCK, width), jnp.float32),
            ],
        ),
        input_output_aliases=aliases,
        compiler_params=pltpu.CompilerParams(
            dimension_semantics=("arbitrary",), vmem_limit_bytes=60 * 1024 * 1024),
        cost_estimate=cost,
    )(*args)


MESH_ID = pl.DeviceIdType.MESH


def spread_kernel(pieces_ref, rows_ref, count_ref, panel_ref, chip_rows_ref, chip_count_ref,
                  send_plane, recv_plane,
                  local_sem, send_right, send_left, recv_ring, meta_sems, *, ring_size,
                  plane_size, blk_size, slots, subs):
    me_z = lax.axis_index("z")
    me_c = lax.axis_index("core")
    me_b = lax.axis_index("blk")
    me_q = me_c * blk_size + me_b
    right = (me_z + 1) % ring_size
    left = (me_z + ring_size - 1) % ring_size

    def plane_dev(q):
        return (me_z, q // blk_size, q % blk_size)

    barrier = pltpu.get_barrier_semaphore()

    def greet(i, carry):
        q = (me_q + i) % plane_size
        pl.semaphore_signal(barrier, 1, device_id=plane_dev(q), device_id_type=MESH_ID)
        return carry

    lax.fori_loop(1, plane_size, greet, 0)
    pl.semaphore_signal(barrier, 1, device_id=(right, me_c, me_b), device_id_type=MESH_ID)
    pl.semaphore_signal(barrier, 1, device_id=(left, me_c, me_b), device_id_type=MESH_ID)
    pl.semaphore_wait(barrier, plane_size + 1)

    partner = (me_z, 1 - me_c, me_b)
    meta_copies = []
    for idx, (src, dst) in enumerate(((rows_ref, chip_rows_ref), (count_ref, chip_count_ref))):
        local = pltpu.make_async_copy(src, dst.at[me_c], meta_sems.at[3 * idx])
        local.start()
        remote = pltpu.make_async_remote_copy(
            src, dst.at[me_c], meta_sems.at[3 * idx + 1], meta_sems.at[3 * idx + 2],
            device_id=partner, device_id_type=MESH_ID)
        remote.start()
        arrival = pltpu.make_async_remote_copy(
            src, dst.at[1 - me_c], meta_sems.at[3 * idx + 1], meta_sems.at[3 * idx + 2],
            device_id=partner, device_id_type=MESH_ID)
        meta_copies.append((local, remote, arrival))

    sub_width = panel_ref.shape[1] // subs
    block_rows = plane_size * slots
    half_rows = block_rows // 2
    base = me_z * block_rows
    half = ring_size // 2

    def cols(sub):
        return pl.ds(sub * sub_width, sub_width)

    def rows_of(q, sub):
        return panel_ref.at[pl.ds(base + q * slots, slots), cols(sub)]

    def local_copy(sub):
        return pltpu.make_async_copy(
            pieces_ref.at[me_q, :, cols(sub)], rows_of(me_q, sub), local_sem.at[sub])

    def plane_copy(q, src_q, sub):
        return pltpu.make_async_remote_copy(
            pieces_ref.at[q, :, cols(sub)], rows_of(src_q, sub), send_plane.at[sub, q],
            recv_plane.at[sub, src_q], device_id=plane_dev(q), device_id_type=MESH_ID)

    def scatter(sub):
        local_copy(sub).start()

        def send(i, carry):
            q = (me_q + i) % plane_size
            plane_copy(q, me_q, sub).start()
            return carry

        lax.fori_loop(1, plane_size, send, 0)

    def gathered(sub):
        def arrive(i, carry):
            q = (me_q + plane_size - i) % plane_size
            plane_copy(q, q, sub).wait_recv()
            return carry

        lax.fori_loop(1, plane_size, arrive, 0)
        local_copy(sub).wait()

    def block_of(k, sub):
        return panel_ref.at[pl.ds(k * block_rows, block_rows), cols(sub)]

    def part_of(k, first, sub):
        start = k * block_rows + (0 if first else half_rows)
        return panel_ref.at[pl.ds(start, half_rows), cols(sub)]

    def ring_copy(k, sem, dev, sub):
        return pltpu.make_async_remote_copy(
            block_of(k, sub), block_of(k, sub), sem, recv_ring.at[sub, k],
            device_id=(dev, me_c, me_b), device_id_type=MESH_ID)

    def part_copy(k, first, sem, dev, sub):
        slot = k if first else ring_size
        return pltpu.make_async_remote_copy(
            part_of(k, first, sub), part_of(k, first, sub), sem, recv_ring.at[sub, slot],
            device_id=(dev, me_c, me_b), device_id_type=MESH_ID)

    sends = []

    def ring_step(s, sub):
        k = (me_z + ring_size - s) % ring_size
        if s > 0:
            ring_copy(k, send_right.at[sub, s], left, sub).wait_recv()
        c = ring_copy(k, send_right.at[sub, s], right, sub) if s < half - 1 else part_copy(
            k, True, send_right.at[sub, s], right, sub)
        c.start()
        sends.append(c)
        k = (me_z + s) % ring_size
        if s > 0:
            ring_copy(k, send_left.at[sub, s], right, sub).wait_recv()
        c = ring_copy(k, send_left.at[sub, s], left, sub) if s < half - 1 else part_copy(
            k, False, send_left.at[sub, s], left, sub)
        c.start()
        sends.append(c)

    for sub in range(subs):
        scatter(sub)
        gathered(sub)
        ring_step(0, sub)
    for s in range(1, half):
        for sub in range(subs):
            ring_step(s, sub)
    far = (me_z + half) % ring_size
    for sub in range(subs):
        part_copy(far, True, send_right.at[sub, 0], left, sub).wait_recv()
        part_copy(far, False, send_left.at[sub, 0], right, sub).wait_recv()
    for sub in range(subs):
        def sent(i, carry):
            q = (me_q + i) % plane_size
            plane_copy(q, me_q, sub).wait_send()
            return carry

        lax.fori_loop(1, plane_size, sent, 0)
    for c in sends:
        c.wait_send()
    for local, remote, arrival in meta_copies:
        local.wait()
        arrival.wait_recv()
        remote.wait_send()


def spread(pieces, pair_rows, pair_counts, ring_size, plane_size, blk_size):
    _, slots, width = pieces.shape
    rows = ring_size * plane_size * slots
    kernel = functools.partial(spread_kernel, ring_size=ring_size, plane_size=plane_size,
                               blk_size=blk_size, slots=slots, subs=SUBS)
    half = ring_size // 2
    return pl.pallas_call(
        kernel,
        out_shape=(jax.ShapeDtypeStruct((rows, width), pieces.dtype),
                   jax.ShapeDtypeStruct((2,) + pair_rows.shape, pair_rows.dtype),
                   jax.ShapeDtypeStruct((2,) + pair_counts.shape, pair_counts.dtype)),
        in_specs=[pl.BlockSpec(memory_space=pl.ANY)] * 3,
        out_specs=(pl.BlockSpec(memory_space=pl.ANY),) * 3,
        scratch_shapes=[
            pltpu.SemaphoreType.DMA((SUBS, plane_size)),
            pltpu.SemaphoreType.DMA((SUBS, plane_size)),
            pltpu.SemaphoreType.DMA((SUBS,)),
            pltpu.SemaphoreType.DMA((SUBS, half)),
            pltpu.SemaphoreType.DMA((SUBS, half)),
            pltpu.SemaphoreType.DMA((SUBS, ring_size + 1)),
            pltpu.SemaphoreType.DMA((6,)),
        ],
        compiler_params=pltpu.CompilerParams(collective_id=0, has_side_effects=True),
    )(pieces, pair_rows, pair_counts)


def exchange_kernel(part_ref, out_ref, mine_buf, recv_buf, sems, *, scale):
    me_z = lax.axis_index("z")
    me_c = lax.axis_index("core")
    me_b = lax.axis_index("blk")
    partner = (me_z, 1 - me_c, me_b)
    local = pltpu.make_async_copy(part_ref.at[me_c], mine_buf, sems.at[2])
    local.start()
    barrier = pltpu.get_barrier_semaphore()
    pl.semaphore_signal(barrier, 1, device_id=partner, device_id_type=MESH_ID)
    pl.semaphore_wait(barrier, 1)
    copy = pltpu.make_async_remote_copy(
        part_ref.at[1 - me_c], recv_buf, sems.at[0], sems.at[1],
        device_id=partner, device_id_type=MESH_ID)
    copy.start()
    local.wait()
    copy.wait()
    out_ref[...] = ((mine_buf[...] + recv_buf[...]) * scale).astype(out_ref.dtype)


def exchange(partial, scale):
    shape = partial.shape[1:]
    return pl.pallas_call(
        functools.partial(exchange_kernel, scale=scale),
        out_shape=jax.ShapeDtypeStruct(shape, jnp.bfloat16),
        in_specs=[pl.BlockSpec(memory_space=pl.ANY)],
        out_specs=pl.BlockSpec(memory_space=pltpu.VMEM),
        scratch_shapes=[
            pltpu.VMEM(shape, partial.dtype),
            pltpu.VMEM(shape, partial.dtype),
            pltpu.SemaphoreType.DMA((3,)),
        ],
        compiler_params=pltpu.CompilerParams(collective_id=1, has_side_effects=True),
    )(partial)


def shards(spectra, send_rows, send_counts, pair_rows, pair_counts):
    whitened = whiten(spectra)
    station_count, comps, parts, bin_count = whitened.shape
    row_width = comps * parts * bin_count
    slot_count = send_rows.shape[2]
    cores = lax.axis_size("core")
    part_bins = bin_count // cores
    core = lax.axis_index("core")

    flat = whitened.reshape(station_count, row_width)
    lists = send_rows[0]
    col_count = lists.shape[0]
    picked = jnp.take(flat, lists.reshape(-1), axis=0).reshape(col_count, slot_count, row_width)
    alive = jnp.arange(slot_count, dtype=jnp.int32)[None, :] < send_counts[0][:, None]
    picked = jnp.where(alive[:, :, None], picked, jnp.zeros_like(picked))
    pieces = picked.reshape(col_count, slot_count, comps * parts, cores, SUBS,
                            part_bins // SUBS)
    pieces = jnp.transpose(pieces, (3, 0, 1, 4, 2, 5)).reshape(
        cores * col_count, slot_count, comps * parts * part_bins)
    pair_total = pair_rows.shape[1]
    panel, chip_pairs, chip_counts = spread(pieces, pair_rows, pair_counts, lax.axis_size("z"),
                                            cores * col_count, col_count)
    lag_rows = lag_tables(bin_count)
    core_arr = core.astype(jnp.int32)[None]
    partial = pair_sums(chip_counts, core_arr, chip_pairs, panel, lag_rows, cores, 0, None)
    total = exchange(partial, 1.0 / math.sqrt(bin_count))[:, :LAGS, :]
    return jnp.transpose(total, (1, 0, 2))


def solution(mesh):
    tile_size = mesh.shape["tile"]
    blk_size = mesh.shape["blk"]
    split = Mesh(mesh.devices.reshape(tile_size // 2, 2, blk_size), ("z", "core", "blk"))
    dev = ("z", "core", "blk")
    return jax.shard_map(
        shards,
        mesh=split,
        in_specs=(
            P(dev, None, None, None),
            P(dev, None, None),
            P(dev, None),
            P(None, dev),
            P(dev),
        ),
        out_specs=P(None, None, dev),
        check_vma=False,
    )
```

```python
import functools
import math

import jax
import ml_dtypes
import numpy as np
import jax.numpy as jnp
from jax import lax
from jax.experimental import pallas as pl
from jax.experimental.pallas import tpu as pltpu
from jax.sharding import Mesh
from jax.sharding import PartitionSpec as P

LAGS = 129
LAG_ROWS = 144
PAIR_BLOCK = 128
BIN_CHUNK = 256
GATHER_CHUNK = 2048
SUBS = 2


def whiten(spectra):
    station_count = spectra.shape[0]
    bin_count = spectra.shape[-1]
    ramp_bins = bin_count // 32
    bin_index = jnp.arange(bin_count, dtype=jnp.int32)
    edge_dist = jnp.minimum(bin_index, bin_count - 1 - bin_index).astype(jnp.float32) + 0.5
    ramp_vals = 0.5 - 0.5 * jnp.cos(jnp.pi * edge_dist / ramp_bins)
    taper = jnp.where(edge_dist < ramp_bins, ramp_vals, jnp.ones_like(ramp_vals))
    blocked = spectra.reshape(station_count, 3, 2, bin_count // 64, 64)
    power = jnp.mean(blocked * blocked, axis=(1, 2, 4))
    inverse = 1.0 / jnp.sqrt(power + 1e-05)
    spread_scale = jnp.repeat(inverse, 64, axis=1)
    return (spectra * taper * spread_scale[:, None, None, :]).astype(jnp.bfloat16)


def lag_tables(bin_count):
    lag_index = np.arange(LAGS, dtype=np.int32) - LAGS // 2
    bin_index = np.arange(bin_count, dtype=np.int32)
    phase_steps = lag_index[:, None] * bin_index[None, :] % (2 * bin_count)
    angle = phase_steps.astype(np.float32) * np.float32(np.pi / bin_count)
    pad = ((0, LAG_ROWS - LAGS), (0, 0))
    cos_rows = np.pad(np.cos(angle).astype(np.float32).astype(ml_dtypes.bfloat16), pad)
    sin_rows = np.pad((-np.sin(angle)).astype(np.float32).astype(ml_dtypes.bfloat16), pad)
    chunks = bin_count // BIN_CHUNK
    both = np.stack([cos_rows.reshape(LAG_ROWS, chunks, BIN_CHUNK),
                     sin_rows.reshape(LAG_ROWS, chunks, BIN_CHUNK)], axis=2)
    return jnp.asarray(both.reshape(LAG_ROWS, 2 * bin_count))


def pair_kernel(counts_ref, core_ref, pairs_ref, panel_ref, lag_ref, *rest,
                blocks_per_owner, part_bins, accumulate):
    if accumulate:
        acc_ref, out_ref, f_scr, s_scr = rest
    else:
        out_ref, f_scr, s_scr = rest
    step = pl.program_id(0)
    owner = step // blocks_per_owner
    start = (step % blocks_per_owner) * PAIR_BLOCK
    live = start < counts_ref[owner, 0]
    if accumulate:
        out_ref[...] = acc_ref[...]
    else:
        out_ref[...] = jnp.zeros_like(out_ref)

    @pl.when(live)
    def _():
        rows = panel_ref.shape[0]
        width = panel_ref.shape[1]
        iota = lax.broadcasted_iota(jnp.int32, (rows, PAIR_BLOCK), 0)
        idx = pairs_ref[0]
        pick_first = jnp.where(idx[0:1, :] == iota, 1.0, 0.0).T.astype(jnp.bfloat16)
        pick_second = jnp.where(idx[1:2, :] == iota, 1.0, 0.0).T.astype(jnp.bfloat16)
        pick = jnp.concatenate([pick_first, pick_second], axis=0)
        gather_chunk = min(GATHER_CHUNK, width)

        def gather(c, carry):
            off = pl.multiple_of(c * gather_chunk, gather_chunk)
            block = panel_ref[:, pl.ds(off, gather_chunk)]
            both = jnp.dot(pick, block, preferred_element_type=jnp.float32)
            f_scr[:, pl.ds(off, gather_chunk)] = both[:PAIR_BLOCK]
            s_scr[:, pl.ds(off, gather_chunk)] = both[PAIR_BLOCK:]
            return carry

        lax.fori_loop(0, width // gather_chunk, gather, 0)
        nt = (((1,), (1,)), ((), ()))
        sub_bins = part_bins // SUBS
        bin_chunk = min(BIN_CHUNK, sub_bins)
        for sub in range(SUBS):
            col0 = sub * 6 * sub_bins

            def chunk(kc, carry):
                off = pl.multiple_of(kc * bin_chunk, bin_chunk)
                lag_blk = lag_ref[:, pl.ds(2 * (sub * sub_bins + off), 2 * bin_chunk)]
                for a in range(3):
                    f_re = f_scr[:, pl.ds(col0 + 2 * a * sub_bins + off, bin_chunk)]
                    f_im = f_scr[:, pl.ds(col0 + (2 * a + 1) * sub_bins + off, bin_chunk)]
                    for b in range(3):
                        s_re = s_scr[:, pl.ds(col0 + 2 * b * sub_bins + off, bin_chunk)]
                        s_im = s_scr[:, pl.ds(col0 + (2 * b + 1) * sub_bins + off, bin_chunk)]
                        real_part = (f_re * s_re + f_im * s_im).astype(jnp.bfloat16)
                        imag_part = (f_im * s_re - f_re * s_im).astype(jnp.bfloat16)
                        both = jnp.concatenate([real_part, imag_part], axis=1)
                        acc = lax.dot_general(lag_blk, both, nt,
                                              preferred_element_type=jnp.float32)
                        out_ref[0, 3 * a + b] += acc
                return carry

            lax.fori_loop(0, sub_bins // bin_chunk, chunk, 0)
        column = start + lax.broadcasted_iota(jnp.int32, out_ref.shape, 3)
        out_ref[...] = jnp.where(column < counts_ref[owner, 0], out_ref[...], 0.0)


def pair_sums(counts, core_arr, chip_pairs, panel, lag_rows, owners, chunk_id, acc):
    rows, width = panel.shape
    part_bins = width // 6
    pairs = chip_pairs.shape[0] * chip_pairs.shape[2]
    per_owner = pairs // owners
    blocks_per_owner = per_owner // PAIR_BLOCK
    grid = (pairs // PAIR_BLOCK,)
    accumulate = acc is not None
    kernel = functools.partial(pair_kernel, blocks_per_owner=blocks_per_owner,
                               part_bins=part_bins, accumulate=accumulate)
    flops = 2 * pairs * rows * width * 2 + 2 * LAG_ROWS * 2 * part_bins * 9 * pairs
    out_bytes = owners * 9 * LAG_ROWS * per_owner * 4
    cost = pl.CostEstimate(flops=flops, transcendentals=0,
                           bytes_accessed=rows * width * 2 + out_bytes * (2 if accumulate else 1))
    out_spec = pl.BlockSpec(
        (1, 9, LAG_ROWS, PAIR_BLOCK),
        lambda i, c, k: (i // blocks_per_owner, 0, 0, i % blocks_per_owner))
    in_specs = [
        pl.BlockSpec((1, 2, PAIR_BLOCK),
                     lambda i, c, k: (i // blocks_per_owner, 0, i % blocks_per_owner)),
        pl.BlockSpec((rows, width), lambda i, c, k: (0, 0)),
        pl.BlockSpec((LAG_ROWS, 2 * part_bins), lambda i, c, k: (0, k[0])),
    ]
    args = [counts, core_arr, chip_pairs, panel, lag_rows]
    aliases = {}
    if accumulate:
        in_specs.append(out_spec)
        args.append(acc)
        aliases = {len(args) - 1: 0}
    return pl.pallas_call(
        kernel,
        out_shape=jax.ShapeDtypeStruct((owners, 9, LAG_ROWS, per_owner), jnp.float32),
        grid_spec=pltpu.PrefetchScalarGridSpec(
            num_scalar_prefetch=2,
            grid=grid,
            in_specs=in_specs,
            out_specs=out_spec,
            scratch_shapes=[
                pltpu.VMEM((PAIR_BLOCK, width), jnp.float32),
                pltpu.VMEM((PAIR_BLOCK, width), jnp.float32),
            ],
        ),
        input_output_aliases=aliases,
        compiler_params=pltpu.CompilerParams(
            dimension_semantics=("arbitrary",), vmem_limit_bytes=60 * 1024 * 1024),
        cost_estimate=cost,
    )(*args)


MESH_ID = pl.DeviceIdType.MESH


def spread_kernel(pieces_ref, rows_ref, count_ref, panel_ref, chip_rows_ref, chip_count_ref,
                  send_plane, recv_plane,
                  local_sem, send_right, send_left, recv_ring, meta_sems, *, ring_size,
                  plane_size, blk_size, slots, subs):
    me_z = lax.axis_index("z")
    me_c = lax.axis_index("core")
    me_b = lax.axis_index("blk")
    me_q = me_c * blk_size + me_b
    right = (me_z + 1) % ring_size
    left = (me_z + ring_size - 1) % ring_size

    def plane_dev(q):
        return (me_z, q // blk_size, q % blk_size)

    barrier = pltpu.get_barrier_semaphore()

    def greet(i, carry):
        q = (me_q + i) % plane_size
        pl.semaphore_signal(barrier, 1, device_id=plane_dev(q), device_id_type=MESH_ID)
        return carry

    lax.fori_loop(1, plane_size, greet, 0)
    pl.semaphore_signal(barrier, 1, device_id=(right, me_c, me_b), device_id_type=MESH_ID)
    pl.semaphore_signal(barrier, 1, device_id=(left, me_c, me_b), device_id_type=MESH_ID)
    pl.semaphore_wait(barrier, plane_size + 1)

    partner = (me_z, 1 - me_c, me_b)
    meta_copies = []
    for idx, (src, dst) in enumerate(((rows_ref, chip_rows_ref), (count_ref, chip_count_ref))):
        local = pltpu.make_async_copy(src, dst.at[me_c], meta_sems.at[3 * idx])
        local.start()
        remote = pltpu.make_async_remote_copy(
            src, dst.at[me_c], meta_sems.at[3 * idx + 1], meta_sems.at[3 * idx + 2],
            device_id=partner, device_id_type=MESH_ID)
        remote.start()
        arrival = pltpu.make_async_remote_copy(
            src, dst.at[1 - me_c], meta_sems.at[3 * idx + 1], meta_sems.at[3 * idx + 2],
            device_id=partner, device_id_type=MESH_ID)
        meta_copies.append((local, remote, arrival))

    sub_width = panel_ref.shape[1] // subs
    block_rows = plane_size * slots
    half_rows = block_rows // 2
    base = me_z * block_rows
    half = ring_size // 2

    def cols(sub):
        return pl.ds(sub * sub_width, sub_width)

    def rows_of(q, sub):
        return panel_ref.at[pl.ds(base + q * slots, slots), cols(sub)]

    def local_copy(sub):
        return pltpu.make_async_copy(
            pieces_ref.at[me_q, :, cols(sub)], rows_of(me_q, sub), local_sem.at[sub])

    def plane_copy(q, src_q, sub):
        return pltpu.make_async_remote_copy(
            pieces_ref.at[q, :, cols(sub)], rows_of(src_q, sub), send_plane.at[sub, q],
            recv_plane.at[sub, src_q], device_id=plane_dev(q), device_id_type=MESH_ID)

    def scatter(sub):
        local_copy(sub).start()

        def send(i, carry):
            q = (me_q + i) % plane_size
            plane_copy(q, me_q, sub).start()
            return carry

        lax.fori_loop(1, plane_size, send, 0)

    def gathered(sub):
        def arrive(i, carry):
            q = (me_q + plane_size - i) % plane_size
            plane_copy(q, q, sub).wait_recv()
            return carry

        lax.fori_loop(1, plane_size, arrive, 0)
        local_copy(sub).wait()

    def block_of(k, sub):
        return panel_ref.at[pl.ds(k * block_rows, block_rows), cols(sub)]

    def part_of(k, first, sub):
        start = k * block_rows + (0 if first else half_rows)
        return panel_ref.at[pl.ds(start, half_rows), cols(sub)]

    def ring_copy(k, sem, dev, sub):
        return pltpu.make_async_remote_copy(
            block_of(k, sub), block_of(k, sub), sem, recv_ring.at[sub, k],
            device_id=(dev, me_c, me_b), device_id_type=MESH_ID)

    def part_copy(k, first, sem, dev, sub):
        slot = k if first else ring_size
        return pltpu.make_async_remote_copy(
            part_of(k, first, sub), part_of(k, first, sub), sem, recv_ring.at[sub, slot],
            device_id=(dev, me_c, me_b), device_id_type=MESH_ID)

    sends = []

    def ring_step(s, sub):
        k = (me_z + ring_size - s) % ring_size
        if s > 0:
            ring_copy(k, send_right.at[sub, s], left, sub).wait_recv()
        c = ring_copy(k, send_right.at[sub, s], right, sub) if s < half - 1 else part_copy(
            k, True, send_right.at[sub, s], right, sub)
        c.start()
        sends.append(c)
        k = (me_z + s) % ring_size
        if s > 0:
            ring_copy(k, send_left.at[sub, s], right, sub).wait_recv()
        c = ring_copy(k, send_left.at[sub, s], left, sub) if s < half - 1 else part_copy(
            k, False, send_left.at[sub, s], left, sub)
        c.start()
        sends.append(c)

    for sub in range(subs):
        scatter(sub)
        gathered(sub)
        ring_step(0, sub)
    for s in range(1, half):
        for sub in range(subs):
            ring_step(s, sub)
    far = (me_z + half) % ring_size
    for sub in range(subs):
        part_copy(far, True, send_right.at[sub, 0], left, sub).wait_recv()
        part_copy(far, False, send_left.at[sub, 0], right, sub).wait_recv()
    for sub in range(subs):
        def sent(i, carry):
            q = (me_q + i) % plane_size
            plane_copy(q, me_q, sub).wait_send()
            return carry

        lax.fori_loop(1, plane_size, sent, 0)
    for c in sends:
        c.wait_send()
    for local, remote, arrival in meta_copies:
        local.wait()
        arrival.wait_recv()
        remote.wait_send()


def spread(pieces, pair_rows, pair_counts, ring_size, plane_size, blk_size):
    _, slots, width = pieces.shape
    rows = ring_size * plane_size * slots
    kernel = functools.partial(spread_kernel, ring_size=ring_size, plane_size=plane_size,
                               blk_size=blk_size, slots=slots, subs=SUBS)
    half = ring_size // 2
    return pl.pallas_call(
        kernel,
        out_shape=(jax.ShapeDtypeStruct((rows, width), pieces.dtype),
                   jax.ShapeDtypeStruct((2,) + pair_rows.shape, pair_rows.dtype),
                   jax.ShapeDtypeStruct((2,) + pair_counts.shape, pair_counts.dtype)),
        in_specs=[pl.BlockSpec(memory_space=pl.ANY)] * 3,
        out_specs=(pl.BlockSpec(memory_space=pl.ANY),) * 3,
        scratch_shapes=[
            pltpu.SemaphoreType.DMA((SUBS, plane_size)),
            pltpu.SemaphoreType.DMA((SUBS, plane_size)),
            pltpu.SemaphoreType.DMA((SUBS,)),
            pltpu.SemaphoreType.DMA((SUBS, half)),
            pltpu.SemaphoreType.DMA((SUBS, half)),
            pltpu.SemaphoreType.DMA((SUBS, ring_size + 1)),
            pltpu.SemaphoreType.DMA((6,)),
        ],
        compiler_params=pltpu.CompilerParams(collective_id=0, has_side_effects=True),
    )(pieces, pair_rows, pair_counts)


def exchange_kernel(part_ref, out_ref, mine_buf, recv_buf, sems, *, scale):
    me_z = lax.axis_index("z")
    me_c = lax.axis_index("core")
    me_b = lax.axis_index("blk")
    partner = (me_z, 1 - me_c, me_b)
    local = pltpu.make_async_copy(part_ref.at[me_c], mine_buf, sems.at[2])
    local.start()
    barrier = pltpu.get_barrier_semaphore()
    pl.semaphore_signal(barrier, 1, device_id=partner, device_id_type=MESH_ID)
    pl.semaphore_wait(barrier, 1)
    copy = pltpu.make_async_remote_copy(
        part_ref.at[1 - me_c], recv_buf, sems.at[0], sems.at[1],
        device_id=partner, device_id_type=MESH_ID)
    copy.start()
    local.wait()
    copy.wait()
    out_ref[...] = ((mine_buf[...] + recv_buf[...]) * scale).astype(out_ref.dtype)


def exchange(partial, scale):
    shape = partial.shape[1:]
    return pl.pallas_call(
        functools.partial(exchange_kernel, scale=scale),
        out_shape=jax.ShapeDtypeStruct(shape, jnp.bfloat16),
        in_specs=[pl.BlockSpec(memory_space=pl.ANY)],
        out_specs=pl.BlockSpec(memory_space=pltpu.VMEM),
        scratch_shapes=[
            pltpu.VMEM(shape, partial.dtype),
            pltpu.VMEM(shape, partial.dtype),
            pltpu.SemaphoreType.DMA((3,)),
        ],
        compiler_params=pltpu.CompilerParams(collective_id=1, has_side_effects=True),
    )(partial)


def shards(spectra, send_rows, send_counts, pair_rows, pair_counts):
    whitened = whiten(spectra)
    station_count, comps, parts, bin_count = whitened.shape
    row_width = comps * parts * bin_count
    slot_count = send_rows.shape[2]
    cores = lax.axis_size("core")
    part_bins = bin_count // cores
    core = lax.axis_index("core")

    flat = whitened.reshape(station_count, row_width)
    lists = send_rows[0]
    col_count = lists.shape[0]
    picked = jnp.take(flat, lists.reshape(-1), axis=0).reshape(col_count, slot_count, row_width)
    alive = jnp.arange(slot_count, dtype=jnp.int32)[None, :] < send_counts[0][:, None]
    picked = jnp.where(alive[:, :, None], picked, jnp.zeros_like(picked))
    pieces = picked.reshape(col_count, slot_count, comps * parts, cores, SUBS,
                            part_bins // SUBS)
    pieces = jnp.transpose(pieces, (3, 0, 1, 4, 2, 5)).reshape(
        cores * col_count, slot_count, comps * parts * part_bins)
    pair_total = pair_rows.shape[1]
    panel, chip_pairs, chip_counts = spread(pieces, pair_rows, pair_counts, lax.axis_size("z"),
                                            cores * col_count, col_count)
    lag_rows = lag_tables(bin_count)
    core_arr = core.astype(jnp.int32)[None]
    partial = pair_sums(chip_counts, core_arr, chip_pairs, panel, lag_rows, cores, 0, None)
    total = exchange(partial, 1.0 / math.sqrt(bin_count))[:, :LAGS, :]
    return jnp.transpose(total, (1, 0, 2))


def solution(mesh):
    tile_size = mesh.shape["tile"]
    blk_size = mesh.shape["blk"]
    split = Mesh(mesh.devices.reshape(tile_size // 2, 2, blk_size), ("z", "core", "blk"))
    dev = ("z", "core", "blk")
    return jax.shard_map(
        shards,
        mesh=split,
        in_specs=(
            P(dev, None, None, None),
            P(dev, None, None),
            P(dev, None),
            P(None, dev),
            P(dev),
        ),
        out_specs=P(None, None, dev),
        check_vma=False,
    )
```
